32 devices in a mesh: dp: 8 (over z, core), tensor: 4 (over y, x).
Axes of the slice: x: 2, y: 2, z: 4, core: 2. Of those that a mesh axis runs over, the one named last changes fastest.
Arguments:
- inputs: bfloat16 [2048, 2048], P('dp'), may hold values from -6 to 6
- segment_ids: int32 [2048], P('dp'), may hold values from 0 to 16, as said below
- first_gain: bfloat16 [2048], replicated, may hold values from 0.25 to 1.75
- first_shift: bfloat16 [2048], replicated, may hold values from -3 to 3
- project_in: bfloat16 [3, 2048, 2048], P(None, 'dp', 'tensor'), may hold values from -0.1875 to 0.1875
- query_bias: bfloat16 [2048], P('tensor'), may hold values from -3 to 3
- value_bias: bfloat16 [2048], P('tensor'), may hold values from -3 to 3
- project_out: bfloat16 [2048, 2048], P('tensor', 'dp'), may hold values from -0.75 to 0.75
- out_bias: bfloat16 [2048], replicated, may hold values from -3 to 3
- second_gain: bfloat16 [2048], replicated, may hold values from 0.25 to 1.75
- second_shift: bfloat16 [2048], replicated, may hold values from -3 to 3
- up_weight: bfloat16 [2048, 8192], P('dp', 'tensor'), may hold values from -0.125 to 0.125
- up_bias: bfloat16 [8192], P('tensor'), may hold values from -3 to 3
- down_weight: bfloat16 [8192, 2048], P('tensor', 'dp'), may hold values from -0.0625 to 0.0625
- down_bias: bfloat16 [2048], replicated, may hold values from -3 to 3
- cotangent: bfloat16 [2048, 2048], P('dp'), may hold values from -6 to 6
Outputs:
- outputs: bfloat16 [2048, 2048], P('dp')
- input_gradient: bfloat16 [2048, 2048], P('dp')
- gradient_first_gain: float32 [2048], replicated
- gradient_first_shift: float32 [2048], replicated
- gradient_project_in: float32 [3, 2048, 2048], P(None, 'dp', 'tensor')
- gradient_query_bias: float32 [2048], P('tensor')
- gradient_value_bias: float32 [2048], P('tensor')
- gradient_project_out: float32 [2048, 2048], P('tensor', 'dp')
- gradient_out_bias: float32 [2048], replicated
- gradient_second_gain: float32 [2048], replicated
- gradient_second_shift: float32 [2048], replicated
- gradient_up_weight: float32 [2048, 8192], P('dp', 'tensor')
- gradient_up_bias: float32 [8192], P('tensor')
- gradient_down_weight: float32 [8192, 2048], P('tensor', 'dp')
- gradient_down_bias: float32 [2048], replicated
The draws below stay inside these ranges and needn't reach their ends.
Inputs may be any that keep to these rules, and one draw needn't show every extreme that they name: `segment_ids`: within each packed sequence of 256 tokens the id starts at 1 on its first token and rises by 0 or 1 from token to token, never above 16, except for a trailing run of up to a quarter of 256 tokens that are 0 (padding).
All inputs are finite; a program needn't handle non-finite values.
Results may differ from the reference program's by a relative error of at most 0.012.
The reference program's roundings to bfloat16 on the way count: a program that leaves them out, or rounds other values in their place, can miss the bound.
Values may be sent and summed in bfloat16 or wider, within the bound.
No kernel may reach another device: no remote copies, remote signals or barrier semaphores. Data moves between devices by JAX's collectives and lax.ppermute only.
A program may use at most 192 MiB of HBM per device.

```python
import jax
import jax.numpy as jnp
from jax import lax

D = 2048
H = 16
DH = 128
FF = 8192
LEN = 256
QB = 256
TOKENS = 2048


def draw_segment_ids(key, part):
    sequences = TOKENS // LEN
    rate_key, ticket_key, padding_key = jax.random.split(key, 3)
    exponent = jax.random.randint(rate_key, (sequences, 1), 3, 10)
    limit = jnp.right_shift(jnp.full((sequences, 1), 1024, jnp.int32), exponent.astype(jnp.int32))
    ticket = jax.random.randint(ticket_key, (sequences, LEN), 0, 1024)
    places = jnp.arange(LEN, dtype=jnp.int32)[None, :]
    rows = jnp.arange(sequences, dtype=jnp.int32)[:, None]
    forced = (rows == 0) & (places % 16 == 0)
    starts = ((ticket < limit) | (places == 0) | forced).astype(jnp.int32)
    numbers = jnp.minimum(jnp.cumsum(starts, axis=1), LEN // 16)
    padding = jax.random.randint(padding_key, (sequences, 1), 0, LEN // 4 + 1)
    padding = jnp.where(rows == 0, 0, jnp.where(rows == sequences - 1, LEN // 4, padding))
    numbers = jnp.where(places >= LEN - padding, 0, numbers)
    return numbers.reshape(TOKENS).astype(jnp.int32)


def raised(entries, own_key, source, target, shards_of, factor):
    owner, partner = [(jnp.arange(entries.shape[dim]) // (entries.shape[dim] // shards_of)).reshape([-1 if axis == dim else 1 for axis in range(entries.ndim)]) for dim in (source, target)]
    chosen = jax.random.permutation(own_key, shards_of)[partner]
    strong = (owner == chosen) | (owner == (partner + shards_of // 2) % shards_of)
    return jnp.where(strong, factor * entries, entries)


def steps_of(stream_key, shape, pieces, smallest, high):
    loudness = 1.0
    for axis_at, parts in pieces:
        draws = jax.random.uniform(jax.random.fold_in(jax.random.fold_in(stream_key, 6), axis_at), (parts,), jnp.float32, smallest / len(pieces), high / len(pieces))
        loudness = loudness * jnp.repeat(jnp.exp(draws), shape[axis_at] // parts).reshape((-1,) + (1,) * (len(shape) - 1 - axis_at))
    return loudness


def normal_values(stream_key, dims, scale, most, shards=(), held_as=jnp.bfloat16):
    array = jax.random.normal(stream_key, dims, jnp.float32) * scale
    if len(shards) > 0:
        array = steps_of(stream_key, dims, shards, -0.22, 0.18) * array
    return jnp.clip(array, min=-most, max=most).astype(held_as)


def bell_draw_with(rng, dims, deviation, most, pieces, heavy, held_as=jnp.bfloat16):
    array = deviation * jax.random.normal(rng, dims, jnp.float32)
    if pieces:
        array = array * steps_of(rng, dims, pieces, -0.22, 0.18)
    return jnp.clip(raised(array, jax.random.fold_in(rng, 3), *heavy), -most, most).astype(held_as)


def setup_inputs(seed: int = 0) -> dict:
    splits = jax.random.split(jax.random.key(seed), 17)
    inputs = bell_draw_with(splits[0], (TOKENS, D), 1.0, 6.0, ((0, 8),), (0, 1, 8, 2.0))
    segment_ids = draw_segment_ids(jax.random.fold_in(splits[16], 71), 0)
    first_gain = jnp.clip(1.0 + 0.15 * jax.random.normal(splits[2], (D,), jnp.float32), 0.25, 1.75).astype(jnp.bfloat16)
    first_shift = normal_values(splits[3], (D,), 0.3, 3.0)
    project_in = normal_values(splits[4], (3, D, H * DH), (D // 2) ** -0.5, 0.1875, ((1, 8), (2, 4)))
    query_bias = normal_values(splits[5], (H * DH,), 0.5, 3.0, ((0, 4),))
    value_bias = normal_values(splits[6], (H * DH,), 0.5, 3.0, ((0, 4),))
    project_out = normal_values(splits[7], (H * DH, D), (H * DH // 32) ** -0.5, 0.75, ((0, 4), (1, 8)))
    out_bias = normal_values(splits[8], (D,), 0.3, 3.0)
    second_gain = jnp.clip(1.0 + 0.15 * jax.random.normal(splits[9], (D,), jnp.float32), 0.25, 1.75).astype(jnp.bfloat16)
    second_shift = normal_values(splits[10], (D,), 0.3, 3.0)
    up_weight = normal_values(splits[11], (D, FF), D ** -0.5, 0.125, ((0, 8), (1, 4)))
    up_bias = normal_values(splits[12], (FF,), 0.5, 3.0, ((0, 4),))
    down_weight = normal_values(splits[13], (FF, D), FF ** -0.5, 0.0625, ((0, 4), (1, 8)))
    down_bias = normal_values(splits[14], (D,), 0.3, 3.0)
    cotangent = bell_draw_with(splits[15], (TOKENS, D), 1.0, 6.0, ((0, 8),), (0, 1, 8, 2.0))
    return dict(inputs=inputs, segment_ids=segment_ids, first_gain=first_gain, first_shift=first_shift, project_in=project_in, query_bias=query_bias, value_bias=value_bias, project_out=project_out, out_bias=out_bias, second_gain=second_gain, second_shift=second_shift, up_weight=up_weight, up_bias=up_bias, down_weight=down_weight, down_bias=down_bias, cotangent=cotangent)


@jax.custom_vjp
def low(v):
    return lax.optimization_barrier(v.astype(jnp.bfloat16)).astype(jnp.float32)

@jax.custom_vjp
def low_back(v):
    return v

def low_keep(v):
    return (low(v), None)

def low_pass(kept, grad):
    return (grad,)

def back_keep(v):
    return (v, None)

def back_low(kept, grad):
    return (low(grad),)
low.defvjp(low_keep, low_pass)
low_back.defvjp(back_keep, back_low)
EPSILON = 1e-05
NEGATIVE = -1e+30
HIGHEST = lax.Precision.HIGHEST

def matmul(left, right):
    return jnp.dot(left, right, precision=HIGHEST, preferred_element_type=jnp.float32)

def normalize(values, gain, shift):
    center = values - lax.optimization_barrier(jnp.mean(values, axis=-1, keepdims=True))
    variance = lax.optimization_barrier(jnp.mean(center * center, axis=-1, keepdims=True))
    return center * lax.rsqrt(variance + EPSILON) * gain + shift

def attend(query, key_heads, value_heads, segment_ids):
    places = jnp.arange(LEN, dtype=jnp.int32)

    def one_block(offset):
        query_block = lax.dynamic_slice_in_dim(query, offset, QB, 0)
        row_places = offset + jnp.arange(QB, dtype=jnp.int32)
        row_ids = lax.dynamic_slice_in_dim(segment_ids, offset, QB, 0)
        products = jnp.einsum('qhd,khd->hqk', query_block, key_heads, precision=HIGHEST)
        scores = low_back(products) * DH ** (-0.5)
        allowed = (row_ids[:, None] == segment_ids[None, :]) & (row_ids[:, None] != 0) & (places[None, :] <= row_places[:, None])
        allowed = allowed | (places[None, :] == row_places[:, None])
        scores = jnp.where(allowed[None], scores, NEGATIVE)
        largest = lax.optimization_barrier(jnp.max(scores, axis=-1, keepdims=True))
        weights = jnp.exp(scores - largest)
        probs = weights / lax.optimization_barrier(jnp.sum(weights, axis=-1, keepdims=True))
        return jnp.einsum('hqk,khd->qhd', low(probs), value_heads, precision=HIGHEST)
    offsets = jnp.arange(LEN // QB, dtype=jnp.int32) * QB
    mixed = lax.map(jax.checkpoint(one_block), offsets)
    return mixed.reshape(LEN, H * DH)

def layer(resid_in, params, segment_ids):
    first_gain, first_shift, project_in, query_bias, value_bias, project_out, out_bias, second_gain, second_shift, up_weight, up_bias, down_weight, down_bias = params
    first_low = low(normalize(resid_in, first_gain, first_shift))
    query = low(low_back(matmul(first_low, project_in[0])) + query_bias)
    key_proj = low(low_back(matmul(first_low, project_in[1])))
    value_proj = low(low_back(matmul(first_low, project_in[2])) + value_bias)
    mixed = attend(query.reshape(LEN, H, DH), key_proj.reshape(LEN, H, DH), value_proj.reshape(LEN, H, DH), segment_ids)
    mixed = low(low_back(mixed))
    hidden = resid_in + low_back(matmul(mixed, project_out)) + out_bias
    second_low = low(normalize(hidden, second_gain, second_shift))
    upper = low_back(matmul(second_low, up_weight)) + up_bias
    activated = low(jax.nn.gelu(upper, approximate=False))
    return hidden + low_back(matmul(activated, down_weight)) + down_bias

def reference(inputs, segment_ids, first_gain, first_shift, project_in, query_bias, value_bias, project_out, out_bias, second_gain, second_shift, up_weight, up_bias, down_weight, down_bias, cotangent):
    params = tuple((item.astype(jnp.float32) for item in (first_gain, first_shift, project_in, query_bias, value_bias, project_out, out_bias, second_gain, second_shift, up_weight, up_bias, down_weight, down_bias)))
    count = TOKENS // LEN
    sequences = inputs.astype(jnp.float32).reshape(count, LEN, D)
    upstream = cotangent.astype(jnp.float32).reshape(count, LEN, D)
    id_rows = segment_ids.astype(jnp.int32).reshape(count, LEN)

    def one_sequence(totals, item):
        values, grads_out, ids_here = item
        result, pull = jax.vjp(lambda first, second: layer(first, second, ids_here), values, params)
        input_grad, param_grads = pull(grads_out)
        totals = jax.tree.map(lambda left, right: left + right, totals, param_grads)
        return (totals, (result.astype(jnp.bfloat16), input_grad.astype(jnp.bfloat16)))
    zeros = tuple((jnp.zeros(item.shape, jnp.float32) for item in params))
    totals, (results, input_grads) = lax.scan(one_sequence, zeros, (sequences, upstream, id_rows))
    return (results.reshape(TOKENS, D), input_grads.reshape(TOKENS, D), totals[0], totals[1], totals[2], totals[3], totals[4], totals[5], totals[6], totals[7], totals[8], totals[9], totals[10], totals[11], totals[12])
```

```python
import jax
import jax.numpy as jnp
from jax import lax
from jax.sharding import PartitionSpec as P

DH = 128
EPSILON = 1e-05
NEGATIVE = -1e30
F32 = jnp.float32
BF16 = jnp.bfloat16


def exact_gelu(values):
    return jax.nn.gelu(values, approximate=False)


def dot(left, right, dims):
    return lax.dot_general(left, right, (dims, ((), ())), preferred_element_type=F32)


def split_at(values, pieces, axis):
    size = values.shape[axis] // pieces
    return [lax.slice_in_dim(values, i * size, (i + 1) * size, axis=axis) for i in range(pieces)]


class Places:
    def __init__(self, dp, tensor):
        self.dp, self.tensor, self.chips = dp, tensor, dp // 2
        self.rank = lax.axis_index("dp")
        self.part = lax.axis_index("tensor")
        self.chip, self.core = self.rank // 2, self.rank % 2
        chips = self.chips
        self.plus = [(i, (i // 2 + 1) % chips * 2 + i % 2) for i in range(dp)]
        self.minus = [(i, (i // 2 - 1) % chips * 2 + i % 2) for i in range(dp)]
        self.swap = [(i, i ^ 1) for i in range(dp)]

    def owner(self, place):
        other, hops = place // self.chips, place % self.chips
        return (self.chip + hops) % self.chips * 2 + (self.core ^ other)

    def place(self, owner):
        chip, core = owner // 2, owner % 2
        return (self.core ^ core) * self.chips + (chip - self.chip) % self.chips

    def features_in(self, values, axis):
        size = values.shape[axis] // self.dp
        return lax.concatenate(
            [
                lax.dynamic_slice_in_dim(values, self.owner(j) * size, size, axis)
                for j in range(self.dp)
            ],
            axis,
        )

    def features_out(self, values, axis):
        size = values.shape[axis] // self.dp
        return lax.concatenate(
            [
                lax.dynamic_slice_in_dim(values, self.place(j) * size, size, axis)
                for j in range(self.dp)
            ],
            axis,
        )

    def tokens_in(self, values):
        size = values.shape[0] // self.tensor
        return lax.concatenate(
            [
                lax.dynamic_slice_in_dim(values, (self.part ^ k) * size, size, 0)
                for k in range(self.tensor)
            ],
            0,
        )

    def send(self, values, pairs):
        return lax.ppermute(values, "dp", pairs)

    def to_peer(self, values, k):
        return lax.ppermute(values, "tensor", [(i, i ^ k) for i in range(self.tensor)])

    def gather_weight(self, block, axis):
        half = self.chips // 2
        pieces = {0: [block]}
        ahead = behind = block
        for step in range(1, half):
            behind = self.send(behind, self.plus)
            ahead = self.send(ahead, self.minus)
            pieces[self.chips - step], pieces[step] = [behind], [ahead]
        low = split_at(behind, 2, axis)[0]
        high = split_at(ahead, 2, axis)[1]
        pieces[half] = [self.send(low, self.plus), self.send(high, self.minus)]
        mine = [piece for hops in range(self.chips) for piece in pieces[hops]]
        theirs = [self.send(piece, self.swap) for piece in mine]
        return lax.concatenate(mine + theirs, axis)

    def scatter_grad(self, product, axis):
        chips, half = self.chips, self.chips // 2
        theirs = self.send(product(chips, 2 * chips).astype(BF16), self.swap)
        mine = product(0, chips) + theirs.astype(F32)
        blocks = split_at(mine, chips, axis)
        far = split_at(blocks[half].astype(BF16), 2, axis)
        low, high = self.send(far[0], self.plus), self.send(far[1], self.minus)
        for hops in range(half - 1, 0, -1):
            ahead, behind = blocks[hops], blocks[chips - hops]
            if hops == half - 1:
                a, b = split_at(ahead, 2, axis)
                ahead = lax.concatenate([a + low.astype(F32), b], axis)
                a, b = split_at(behind, 2, axis)
                behind = lax.concatenate([a, b + high.astype(F32)], axis)
            else:
                ahead, behind = ahead + low.astype(F32), behind + high.astype(F32)
            low = self.send(ahead.astype(BF16), self.plus)
            high = self.send(behind.astype(BF16), self.minus)
        return blocks[0] + low.astype(F32) + high.astype(F32)

    def scatter_tokens(self, values):
        chunks = split_at(values, self.tensor, 0)
        total = chunks[0]
        for k in range(1, self.tensor):
            total = total + self.to_peer(chunks[k].astype(BF16), k).astype(F32)
        return total

    def gather_tokens(self, chunk):
        return lax.concatenate(
            [chunk] + [self.to_peer(chunk, k) for k in range(1, self.tensor)], 0
        )

    def tokens_out(self, chunk):
        size = chunk.shape[0]
        result = jnp.zeros((size * self.tensor,) + chunk.shape[1:], chunk.dtype)
        for k in range(self.tensor):
            piece = chunk if k == 0 else self.to_peer(chunk, k)
            result = lax.dynamic_update_slice_in_dim(result, piece, (self.part ^ k) * size, 0)
        return result

    def sum_small(self, values, over_tensor):
        if over_tensor:
            values = values + sum(self.to_peer(values, k) for k in range(1, self.tensor))
        values = values + self.send(values, self.swap)
        total = values
        for hops in range(1, self.chips):
            total = total + self.send(
                values, [(i, (i // 2 + hops) % self.chips * 2 + i % 2) for i in range(self.dp)]
            )
        return total


def normalize(values):
    center = values - jnp.mean(values, axis=-1, keepdims=True)
    inverse = lax.rsqrt(jnp.mean(center * center, axis=-1, keepdims=True) + EPSILON)
    return (center * inverse, inverse)


def norm_back(norm_grad, normed, inverse, gain):
    scaled = norm_grad * gain
    return inverse * (
        scaled
        - jnp.mean(scaled, axis=-1, keepdims=True)
        - normed * jnp.mean(scaled * normed, axis=-1, keepdims=True)
    )


def mask_of(ids, places):
    allowed = (
        (ids[:, None] == ids[None, :])
        & (ids[:, None] != 0)
        & (places[None, :] <= places[:, None])
    )
    return allowed | (places[None, :] == places[:, None])


def heads_of(values):
    return values.reshape(values.shape[0], -1, DH).transpose(1, 0, 2)


def tokens_of(values):
    return values.transpose(1, 0, 2).reshape(values.shape[1], -1)


def batched(pattern, left, right):
    return jnp.einsum(pattern, left, right, preferred_element_type=F32)


def probabilities(query, key, allowed):
    scores = jnp.where(allowed[None], batched("hqd,hkd->hqk", query, key) * DH ** (-0.5), NEGATIVE)
    weights = jnp.exp(scores - jnp.max(scores, axis=-1, keepdims=True))
    return weights / jnp.sum(weights, axis=-1, keepdims=True)


def shards(
    dp,
    tensor,
    inputs,
    segment_ids,
    first_gain,
    first_shift,
    project_in,
    query_bias,
    value_bias,
    project_out,
    out_bias,
    second_gain,
    second_shift,
    up_weight,
    up_bias,
    down_weight,
    down_bias,
    cotangent,
):
    at = Places(dp, tensor)
    length = inputs.shape[0]
    own = length // tensor
    full_in = at.gather_weight(project_in, 1)
    full_out = at.gather_weight(project_out, 1)
    full_up = at.gather_weight(up_weight, 0)
    full_down = at.gather_weight(down_weight, 1)

    vectors = jnp.stack(
        [first_gain, first_shift, out_bias, second_gain, second_shift, down_bias]
    ).astype(F32)
    vectors = at.features_in(vectors, 1)
    gain_one, shift_one, bias_out, gain_two, shift_two, bias_down = [vectors[i] for i in range(6)]
    resid = at.features_in(at.tokens_in(inputs), 1)
    upstream = at.features_in(at.tokens_in(cotangent), 1)
    ids = at.tokens_in(segment_ids)
    places = at.tokens_in(jnp.arange(length, dtype=jnp.int32))
    allowed = mask_of(ids, places)

    normed_one, inverse_one = normalize(resid.astype(F32))
    first_low = (normed_one * gain_one + shift_one).astype(BF16)
    rows = ((1,), (0,))
    query = (dot(first_low, full_in[0], rows) + query_bias.astype(F32)).astype(BF16)
    key = dot(first_low, full_in[1], rows).astype(BF16)
    value = (dot(first_low, full_in[2], rows) + value_bias.astype(F32)).astype(BF16)
    query_heads, key_heads, value_heads = heads_of(query), heads_of(key), heads_of(value)
    probs = probabilities(query_heads, key_heads, allowed)
    probs_low = probs.astype(BF16)
    mixed = tokens_of(batched("hqk,hkd->hqd", probs_low, value_heads).astype(BF16))

    attention = at.scatter_tokens(dot(mixed, full_out, rows))
    hidden = resid[:own].astype(F32) + attention + bias_out
    normed_two, inverse_two = normalize(hidden)
    second_own = (normed_two * gain_two + shift_two).astype(BF16)
    second_low = at.gather_tokens(second_own)
    upper = dot(second_low, full_up, rows) + up_bias.astype(F32)
    activated = exact_gelu(upper).astype(BF16)

    act_grad = dot(upstream, full_down, ((1,), (1,)))
    upper_grad = jax.vjp(exact_gelu, upper)[1](act_grad)[0]
    upper_low = upper_grad.astype(BF16)
    second_grad = at.scatter_tokens(dot(upper_low, full_up, ((1,), (1,))))
    feed = at.scatter_tokens(dot(activated, full_down, rows))
    outputs_own = (hidden + feed + bias_down).astype(BF16)
    outputs = at.tokens_out(at.features_out(outputs_own, 1))

    upstream_own = upstream[:own].astype(F32)
    hidden_grad = upstream_own + norm_back(second_grad, normed_two, inverse_two, gain_two)
    hidden_low = at.gather_tokens(hidden_grad.astype(BF16))
    mixed_grad = dot(hidden_low, full_out, ((1,), (1,))).astype(BF16)

    mixed_heads = heads_of(mixed_grad)
    prob_grad = batched("hqd,hkd->hqk", mixed_heads, value_heads)
    score_grad = probs * (prob_grad - jnp.sum(probs * prob_grad, axis=-1, keepdims=True))
    score_low = (score_grad * DH ** (-0.5)).astype(BF16)
    query_grad = tokens_of(batched("hqk,hkd->hqd", score_low, key_heads))
    key_grad = tokens_of(batched("hqk,hqd->hkd", score_low, query_heads))
    value_grad = tokens_of(batched("hqk,hqd->hkd", probs_low, mixed_heads))
    lows = [query_grad.astype(BF16), key_grad.astype(BF16), value_grad.astype(BF16)]
    first_part = sum(dot(lows[j], full_in[j], ((1,), (1,))) for j in range(3))
    first_grad = at.scatter_tokens(first_part)
    input_grad_own = (
        hidden_grad + norm_back(first_grad, normed_one[:own], inverse_one[:own], gain_one)
    ).astype(BF16)
    input_gradient = at.tokens_out(at.features_out(input_grad_own, 1))

    size = full_up.shape[0] // dp
    over_tokens = ((0,), (0,))

    def columns(values, low, high):
        return values[:, low * size : high * size]

    grad_down = at.scatter_grad(
        lambda low, high: dot(activated, columns(upstream, low, high), over_tokens), 1
    )
    grad_up = at.scatter_grad(
        lambda low, high: dot(columns(second_low, low, high), upper_low, over_tokens), 0
    )
    grad_out = at.scatter_grad(
        lambda low, high: dot(mixed, columns(hidden_low, low, high), over_tokens), 1
    )
    stacked = jnp.stack(lows)
    grad_in = at.scatter_grad(
        lambda low, high: jnp.einsum(
            "rd,jrh->jdh", columns(first_low, low, high), stacked, preferred_element_type=F32
        ),
        1,
    )

    wide = jnp.stack(
        [
            jnp.sum(first_grad * normed_one[:own], axis=0),
            jnp.sum(first_grad, axis=0),
            jnp.sum(hidden_grad, axis=0),
            jnp.sum(second_grad * normed_two, axis=0),
            jnp.sum(second_grad, axis=0),
            jnp.sum(upstream_own, axis=0),
        ]
    )
    wide = at.sum_small(at.features_out(wide, 1), True)
    narrow = jnp.concatenate(
        [jnp.sum(query_grad, axis=0), jnp.sum(value_grad, axis=0), jnp.sum(upper_grad, axis=0)]
    )
    narrow = at.sum_small(narrow, False)
    heads = query.shape[1]
    return (
        outputs,
        input_gradient,
        wide[0],
        wide[1],
        grad_in,
        narrow[:heads],
        narrow[heads : 2 * heads],
        grad_out,
        wide[2],
        wide[3],
        wide[4],
        grad_up,
        narrow[2 * heads :],
        grad_down,
        wide[5],
    )


def solution(mesh):
    dp, tensor = mesh.shape["dp"], mesh.shape["tensor"]

    def program(*arguments):
        return shards(dp, tensor, *arguments)

    in_specs = (
        P("dp", None),
        P("dp"),
        P(),
        P(),
        P(None, "dp", "tensor"),
        P("tensor"),
        P("tensor"),
        P("tensor", "dp"),
        P(),
        P(),
        P(),
        P("dp", "tensor"),
        P("tensor"),
        P("tensor", "dp"),
        P(),
        P("dp", None),
    )
    out_specs = (
        P("dp", None),
        P("dp", None),
        P(),
        P(),
        P(None, "dp", "tensor"),
        P("tensor"),
        P("tensor"),
        P("tensor", "dp"),
        P(),
        P(),
        P(),
        P("dp", "tensor"),
        P("tensor"),
        P("tensor", "dp"),
        P(),
    )
    return jax.shard_map(program, mesh=mesh, in_specs=in_specs, out_specs=out_specs, check_vma=False)
```

```python
import functools

import jax
import jax.numpy as jnp
from jax import lax
from jax.experimental import pallas as pl
from jax.experimental.pallas import tpu as pltpu
from jax.sharding import PartitionSpec as P

DH = 128
EPSILON = 1e-05
NEGATIVE = -1e30
SCALE = DH ** (-0.5)
F32 = jnp.float32
BF16 = jnp.bfloat16
TILE = 256
ANY = pl.BlockSpec(memory_space=pl.ANY)
VMEM = pl.BlockSpec(memory_space=pltpu.VMEM)
SMEM = pl.BlockSpec(memory_space=pltpu.SMEM)


def nn(left, right):
    return lax.dot_general(left, right, (((1,), (0,)), ((), ())), preferred_element_type=F32)


def nt(left, right):
    return lax.dot_general(left, right, (((1,), (1,)), ((), ())), preferred_element_type=F32)


def tn(left, right):
    return lax.dot_general(left, right, (((0,), (0,)), ((), ())), preferred_element_type=F32)


def split_rows(values, parts):
    rows = values.shape[0] // parts
    return [values[i * rows : (i + 1) * rows] for i in range(parts)]


def shape(dims, dtype):
    return jax.ShapeDtypeStruct(tuple(dims), dtype)


def call(body, name, in_specs, outs, scratch, flops, args):
    moved = sum(a.size * a.dtype.itemsize for a in args)
    moved += sum(o.size * o.dtype.itemsize for o in outs)
    return pl.pallas_call(
        body,
        name=name,
        out_shape=outs,
        in_specs=in_specs,
        out_specs=[VMEM] * len(outs),
        scratch_shapes=scratch,
        cost_estimate=pl.CostEstimate(flops=flops, bytes_accessed=moved, transcendentals=0),
    )(*args)


class Places:
    def __init__(self, dp, tensor):
        self.dp, self.tensor, self.chips = dp, tensor, dp // 2
        self.rank = lax.axis_index("dp")
        self.part = lax.axis_index("tensor")
        self.chip, self.core = self.rank // 2, self.rank % 2
        chips = self.chips
        self.plus = [(i, (i // 2 + 1) % chips * 2 + i % 2) for i in range(dp)]
        self.minus = [(i, (i // 2 - 1) % chips * 2 + i % 2) for i in range(dp)]
        self.swap = [(i, i ^ 1) for i in range(dp)]

    def owner(self, place):
        other, hops = place // self.chips, place % self.chips
        return (self.chip + hops) % self.chips * 2 + (self.core ^ other)

    def table(self):
        blocks = self.owner(jnp.arange(self.dp, dtype=jnp.int32))
        chunks = self.part ^ jnp.arange(self.tensor, dtype=jnp.int32)
        return jnp.concatenate([blocks, chunks]).astype(jnp.int32)

    def tokens_in(self, values):
        size = values.shape[0] // self.tensor
        return jnp.take(
            values.reshape(self.tensor, size),
            self.part ^ jnp.arange(self.tensor, dtype=jnp.int32),
            axis=0,
        ).reshape(-1)

    def send(self, values, pairs):
        return lax.ppermute(values, "dp", pairs)

    def to_peer(self, values, k):
        return lax.ppermute(values, "tensor", [(i, i ^ k) for i in range(self.tensor)])

    def to_peers(self, values):
        many = isinstance(values, (list, tuple))
        return [
            self.to_peer(values[k - 1] if many else values, k)
            for k in range(self.tensor - 1, 0, -1)
        ][::-1]

    def first_hop(self, block):
        return self.send(block, self.plus), self.send(block, self.minus)

    def later_hops(self, block, hop):
        half = self.chips // 2
        pieces = {0: [block]}
        behind, ahead = hop
        for step in range(1, half):
            if step > 1:
                behind, ahead = self.send(behind, self.plus), self.send(ahead, self.minus)
            pieces[self.chips - step], pieces[step] = [behind], [ahead]
        axis = block.ndim - 2
        rows = block.shape[axis] // 2
        low = lax.slice_in_dim(behind, 0, rows, axis=axis)
        high = lax.slice_in_dim(ahead, rows, 2 * rows, axis=axis)
        pieces[half] = [self.send(low, self.plus), self.send(high, self.minus)]
        return [piece for hops in range(self.chips) for piece in pieces[hops]]

    def both_cores(self, pieces):
        return pieces + [self.send(piece, self.swap) for piece in pieces]

    def sum_small(self, values, over_tensor):
        if over_tensor:
            values = values + sum(self.to_peer(values, k) for k in range(1, self.tensor))
        values = values + self.send(values, self.swap)
        total = values
        for hops in range(1, self.chips):
            total = total + self.send(
                values, [(i, (i // 2 + hops) % self.chips * 2 + i % 2) for i in range(self.dp)]
            )
        return total


def piece_places(chips, size, parts):
    places = []
    rows = size // parts
    for part in range(parts):
        mine = []
        for hops in range(chips):
            start = part * rows
            if hops == chips // 2:
                mine += [(hops, start, rows // 2), (hops, start + rows // 2, rows // 2)]
            else:
                mine += [(hops, start, rows)]
        places += mine + [(chips + block, start, height) for block, start, height in mine]
    return places


def by_block(places):
    return [
        [p for p, place in enumerate(places) if place[0] == block]
        for block in range(1 + max(place[0] for place in places))
    ]


def after(values, *events):
    values, _ = lax.optimization_barrier((values, events))
    return values


def center_of(values):
    center = values - jnp.mean(values, axis=-1, keepdims=True)
    inverse = lax.rsqrt(jnp.mean(center * center, axis=-1, keepdims=True) + EPSILON)
    return center * inverse, inverse


def norm_back(norm_grad, normed, inverse, gain):
    scaled = norm_grad * gain
    return inverse * (
        scaled
        - jnp.mean(scaled, axis=-1, keepdims=True)
        - normed * jnp.mean(scaled * normed, axis=-1, keepdims=True)
    )


def prologue_body(dp, tensor, table, x, g, vec, x_rel, g_rel, low, vec_rel):
    width, rows = x.shape[1] // dp, x.shape[0] // tensor
    for j in range(dp):
        cols = pl.ds(pl.multiple_of(table[j] * width, width), width)
        here = slice(j * width, (j + 1) * width)
        vec_rel[:, here] = vec[:, cols]
        for k in range(tensor):
            start = pl.ds(pl.multiple_of(table[dp + k] * rows, rows), rows)
            there = slice(k * rows, (k + 1) * rows)
            x_rel[there, here] = x[start, cols]
            g_rel[there, here] = g[start, cols]
    for k in range(tensor):
        there = slice(k * rows, (k + 1) * rows)
        normed, _ = center_of(x_rel[there, :].astype(F32))
        low[there, :] = (normed * vec_rel[0:1, :] + vec_rel[1:2, :]).astype(BF16)


def attend_body(places, x, q_bias, v_bias, allowed, *refs):
    count = len(places)
    pieces, (q, k, v, probs, mixed), (weight, sems) = refs[:count], refs[count:-2], refs[-2:]
    size = block_rows(places)

    def copy(j, p):
        block, start, rows = places[p]
        return pltpu.make_async_copy(
            pieces[p].at[j], weight.at[j, pl.ds(block * size + start, rows)], sems.at[j, p]
        )

    for j in range(3):
        for p in range(count):
            copy(j, p).start()
    columns = q.shape[1]
    tile = min(TILE, columns)
    for j, out in enumerate((q, k, v)):
        for p in range(count):
            copy(j, p).wait()
        for start in range(0, columns, tile):
            cols = slice(start, start + tile)
            total = nn(x[...], weight[j, :, cols])
            if j == 0:
                total = total + q_bias[:, cols].astype(F32)
            if j == 2:
                total = total + v_bias[:, cols].astype(F32)
            out[:, cols] = total.astype(BF16)
    for h in range(columns // DH):
        cols = slice(h * DH, (h + 1) * DH)
        scores = jnp.where(allowed[...] > 0, nt(q[:, cols], k[:, cols]) * SCALE, NEGATIVE)
        weights = jnp.exp(scores - jnp.max(scores, axis=-1, keepdims=True))
        prob = weights / jnp.sum(weights, axis=-1, keepdims=True)
        probs[h] = prob
        mixed[:, cols] = nn(prob.astype(BF16), v[:, cols]).astype(BF16)


def put_chunks(total, cols, own, sends):
    rows = own.shape[0]
    own[:, cols] = total[:rows]
    for k, ref in enumerate(sends):
        ref[:, cols] = total[(k + 1) * rows : (k + 2) * rows].astype(BF16)


def block_rows(places):
    return max(start + rows for _, start, rows in places)


def column_copies(places, pieces, weight, sems):
    width = pieces[0].shape[1]
    return [
        pltpu.make_async_copy(
            pieces[p],
            weight.at[pl.ds(start, rows), pl.ds(block * width, width)],
            sems.at[p],
        )
        for p, (block, start, rows) in enumerate(places)
    ]


def row_copies(places, pieces, weight, sems):
    size = block_rows(places)
    return [
        pltpu.make_async_copy(
            pieces[p], weight.at[pl.ds(block * size + start, rows)], sems.at[p]
        )
        for p, (block, start, rows) in enumerate(places)
    ]


def start_all(places, copies):
    for group in by_block(places):
        for p in group:
            copies[p].start()


def project_body(places, left, *refs):
    count = len(places)
    pieces, (own, *sends), (weight, sems) = refs[:count], refs[count:-2], refs[-2:]
    copies = column_copies(places, pieces, weight, sems)
    start_all(places, copies)
    width = pieces[0].shape[1]
    for block, group in enumerate(by_block(places)):
        for p in group:
            copies[p].wait()
        cols = slice(block * width, (block + 1) * width)
        put_chunks(nn(left[...], weight[:, cols]), cols, own, sends)


def second_body(tensor, own, x_rel, vec, *refs):
    received, (hidden, normed_out, inverse_out, low) = refs[: tensor - 1], refs[tensor - 1 :]
    rows = own.shape[0]
    total = own[...]
    for ref in received:
        total = total + ref[...].astype(F32)
    value = x_rel[0:rows, :].astype(F32) + total + vec[2:3, :]
    hidden[...] = value
    normed, inverse = center_of(value)
    normed_out[...] = normed
    inverse_out[...] = jnp.broadcast_to(inverse, inverse_out.shape)
    low[...] = (normed * vec[3:4, :] + vec[4:5, :]).astype(BF16)


def upper_body(places, tensor, bias, *refs):
    chunks, refs = refs[:tensor], refs[tensor:]
    count = len(places)
    pieces, (low, activated, slope), (weight, sems) = refs[:count], refs[count:-2], refs[-2:]
    copies = row_copies(places, pieces, weight, sems)
    for copy in copies:
        copy.start()
    rows = chunks[0].shape[0]
    for k, chunk in enumerate(chunks):
        low[k * rows : (k + 1) * rows, :] = chunk[...]
    for copy in copies:
        copy.wait()
    columns = weight.shape[1]
    tile = min(TILE, columns)

    @pl.loop(0, columns // tile)
    def _(i):
        cols = pl.ds(pl.multiple_of(i * tile, tile), tile)
        value = nn(low[...], weight[:, cols]) + bias[:, cols].astype(F32)
        below = 0.5 * (1.0 + lax.erf(value * (0.5**0.5)))
        activated[:, cols] = (value * below).astype(BF16)
        density = jnp.exp(-0.5 * value * value) * 0.3989422804014327
        slope[:, cols] = below + value * density


def upper_grad_body(places, g, slope, *refs):
    count = len(places)
    pieces, (low, bias_grad), (weight, sems) = refs[:count], refs[count:-2], refs[-2:]
    copies = column_copies(places, pieces, weight, sems)
    for copy in copies:
        copy.start()
    for copy in copies:
        copy.wait()
    hidden = weight.shape[0]
    tile = min(TILE, hidden)

    @pl.loop(0, hidden // tile)
    def _(i):
        cols = pl.ds(pl.multiple_of(i * tile, tile), tile)
        grad = nt(g[...], weight[cols, :]) * slope[:, cols]
        low[:, cols] = grad.astype(BF16)
        bias_grad[:, cols] = jnp.sum(grad, axis=0, keepdims=True)


def second_part_body(places, left, *refs):
    count = len(places)
    pieces, (own, *sends), (weight, sems) = refs[:count], refs[count:-2], refs[-2:]
    copies = row_copies(places, pieces, weight, sems)
    start_all(places, copies)
    size = block_rows(places)
    for block, group in enumerate(by_block(places)):
        for p in group:
            copies[p].wait()
        cols = slice(block * size, (block + 1) * size)
        put_chunks(nt(left[...], weight[cols, :]), cols, own, sends)


def put_features(table, dp, out, rows, values):
    width = out.shape[1] // dp
    for j in range(dp):
        cols = pl.ds(pl.multiple_of(table[j] * width, width), width)
        out[rows, cols] = values[:, j * width : (j + 1) * width]


def second_back_body(dp, tensor, table, own, g_rel, vec, normed, inverse, *refs):
    received, (hidden_grad, low, sums) = refs[: tensor - 1], refs[tensor - 1 :]
    rows = own.shape[0]
    total = own[...]
    for ref in received:
        total = total + ref[...].astype(F32)
    upstream = g_rel[0:rows, :].astype(F32)
    grad = upstream + norm_back(total, normed[...], inverse[:, 0:1], vec[3:4, :])
    hidden_grad[...] = grad
    low[...] = grad.astype(BF16)
    for i, values in enumerate((grad, total * normed[...], total, upstream)):
        put_features(
            table, dp, sums, slice(i, i + 1), jnp.sum(values, axis=0, keepdims=True)
        )


def attend_back_body(in_places, out_places, tensor, q, k, v, probs, *refs):
    chunks, refs = refs[:tensor], refs[tensor:]
    outs_p, refs = refs[: len(out_places)], refs[len(out_places) :]
    ins_p, refs = refs[: len(in_places)], refs[len(in_places) :]
    (low, q_low, k_low, v_low, bias_grad, own, *sends) = refs[:-5]
    out_weight, in_weight, mixed_grad, out_sems, in_sems = refs[-5:]
    copies = column_copies(out_places, outs_p, out_weight, out_sems)
    for copy in copies:
        copy.start()
    size = block_rows(in_places)
    ins = [
        pltpu.make_async_copy(
            ins_p[p], in_weight.at[:, pl.ds(block * size + start, rows)], in_sems.at[p]
        )
        for p, (block, start, rows) in enumerate(in_places)
    ]
    start_all(in_places, ins)
    rows = chunks[0].shape[0]
    for j, chunk in enumerate(chunks):
        low[j * rows : (j + 1) * rows, :] = chunk[...]
    for copy in copies:
        copy.wait()
    columns = q.shape[1]
    tile = min(TILE, columns)
    for start in range(0, columns, tile):
        cols = slice(start, start + tile)
        mixed_grad[:, cols] = nt(low[...], out_weight[cols, :]).astype(BF16)
    for h in range(columns // DH):
        cols = slice(h * DH, (h + 1) * DH)
        there = slice(columns + h * DH, columns + (h + 1) * DH)
        prob, down = probs[h], mixed_grad[:, cols]
        prob_grad = nt(down, v[:, cols])
        inner = jnp.sum(prob * prob_grad, axis=-1, keepdims=True)
        score_low = (prob * (prob_grad - inner) * SCALE).astype(BF16)
        query_grad = nn(score_low, k[:, cols])
        q_low[:, cols] = query_grad.astype(BF16)
        bias_grad[:, cols] = jnp.sum(query_grad, axis=0, keepdims=True)
        k_low[:, cols] = tn(score_low, q[:, cols]).astype(BF16)
        value_grad = tn(prob.astype(BF16), down)
        v_low[:, cols] = value_grad.astype(BF16)
        bias_grad[:, there] = jnp.sum(value_grad, axis=0, keepdims=True)
    for block, group in enumerate(by_block(in_places)):
        for p in group:
            ins[p].wait()
        cols = slice(block * size, (block + 1) * size)
        total = nt(q_low[...], in_weight[0, cols, :])
        total = total + nt(k_low[...], in_weight[1, cols, :])
        total = total + nt(v_low[...], in_weight[2, cols, :])
        put_chunks(total, cols, own, sends)


def first_back_body(dp, tensor, table, own, x_rel, vec, hidden_grad, *refs):
    received, (result, sums) = refs[: tensor - 1], refs[tensor - 1 :]
    rows = own.shape[0]
    total = own[...]
    for ref in received:
        total = total + ref[...].astype(F32)
    normed, inverse = center_of(x_rel[0:rows, :].astype(F32))
    grad = hidden_grad[...] + norm_back(total, normed, inverse, vec[0:1, :])
    put_features(table, dp, result, slice(0, rows), grad.astype(BF16))
    for i, values in enumerate((total * normed, total)):
        put_features(
            table, dp, sums, slice(i, i + 1), jnp.sum(values, axis=0, keepdims=True)
        )


def output_body(dp, tensor, table, own, hidden, vec, *refs):
    received, (result,) = refs[: tensor - 1], refs[tensor - 1 :]
    total = own[...]
    for ref in received:
        total = total + ref[...].astype(F32)
    value = hidden[...] + total + vec[5:6, :]
    put_features(table, dp, result, slice(0, own.shape[0]), value.astype(BF16))


def assemble_body(dp, tensor, table, *refs):
    chunks, (result,) = refs[:tensor], refs[tensor:]
    rows = chunks[0].shape[0]
    for k, chunk in enumerate(chunks):
        result[pl.ds(pl.multiple_of(table[dp + k] * rows, rows), rows), :] = chunk[...]


def grad_blocks(left, right, by_rows, first, chips, size, put):
    if by_rows:
        columns = sum(r.shape[1] for r in right)
        width = right[0].shape[1]
        tile = min(TILE, width)
        for block in range(chips):
            start = (first + block) * size
            turned = left[:, start : start + size].T
            for j, ref in enumerate(right):
                for c in range(0, width, tile):
                    put(block, 0, size, j * width + c, nn(turned, ref[:, c : c + tile]))
        del columns
    else:
        hidden = left.shape[1]
        step = min(512, hidden // 2)
        for r in range(0, hidden, step):
            turned = left[:, r : r + step].T
            for block in range(chips):
                start = (first + block) * size
                put(block, r, r + step, 0, nn(turned, right[0][:, start : start + size]))


def grad_far_body(by_rows, chips, size, count, left, *refs):
    right, out = refs[:count], refs[count]
    height = out.shape[0] // chips

    def put(block, low, high, column, value):
        out[block * height + low : block * height + high, column : column + value.shape[1]] = (
            value.astype(BF16)
        )

    grad_blocks(left, right, by_rows, chips, chips, size, put)


def half_plan(chips):
    h = chips // 2
    plan, keeps = {(0, 0): ("own", 0), (0, 1): ("own", 1)}, []
    plan[(h, 0)], plan[(h, 1)] = ("plus", 0), ("minus", 0)
    if h > 1:
        plan[(h - 1, 1)], plan[(chips - h + 1, 0)] = ("plus", 1), ("minus", 1)
    for key in [(b, s) for b in range(chips) for s in range(2)]:
        if key not in plan:
            plan[key] = (len(keeps), None)
            keeps.append(key)
    return plan, keeps


def grad_near_body(by_rows, chips, size, count, left, theirs, *refs):
    right, (own, plus, minus, *keeps) = refs[:count], refs[count:]
    plan, _ = half_plan(chips)
    height = own.shape[0]
    middle = height // 2

    def put(block, low, high, column, value):
        cols = slice(column, column + value.shape[1])
        value = value + theirs[block * height + low : block * height + high, cols].astype(F32)
        for half in range(2):
            start, stop = max(low, half * middle), min(high, (half + 1) * middle)
            if start >= stop:
                continue
            part = value[start - low : stop - low]
            name, place = plan[(block, half)]
            ref = {"own": own, "plus": plus, "minus": minus}.get(name)
            ref = keeps[name] if ref is None else ref
            base = (place or 0) * middle - half * middle
            ref[start + base : stop + base, cols] = part.astype(ref.dtype)

    grad_blocks(left, right, by_rows, 0, chips, size, put)


def finish_body(planes, own, low_a, low_b, high_a, high_b, out):
    half = own.shape[0] // 2
    for s, parts in enumerate(((low_a, low_b), (high_a, high_b))):
        rows = slice(s * half, (s + 1) * half)
        total = own[rows, :]
        for ref, start in parts:
            total = total + ref[start : start + half, :].astype(F32)
        if planes == 1:
            out[rows, :] = total
        else:
            width = own.shape[1] // planes
            for j in range(planes):
                out[j, rows, :] = total[:, j * width : (j + 1) * width]


def sems(*dims):
    return pltpu.SemaphoreType.DMA(tuple(dims))


class Layer:
    def __init__(self, at, length, features):
        self.at = at
        self.length, self.features = length, features
        self.own = length // at.tensor

    def chunk_outs(self):
        return [shape((self.own, self.features), F32)] + [
            shape((self.own, self.features), BF16)
        ] * (self.at.tensor - 1)

    def project(self, name, left, pieces, places, by_rows):
        inner = left.shape[1]
        weight = (self.features, inner) if by_rows else (inner, self.features)
        body = second_part_body if by_rows else project_body
        return call(
            functools.partial(body, places),
            name,
            [VMEM] + [ANY] * len(places),
            self.chunk_outs(),
            [pltpu.VMEM(weight, BF16), sems(len(places))],
            2 * self.length * inner * self.features,
            [left] + list(pieces),
        )

    def swapped(self, far):
        return self.at.send(far, self.at.swap)

    def grad_far(self, name, left, right, by_rows):
        at = self.at
        size = self.features // at.dp
        height = size if by_rows else left.shape[1]
        width = sum(r.shape[1] for r in right) if by_rows else size
        return call(
            functools.partial(grad_far_body, by_rows, at.chips, size, len(right)),
            name + "_far",
            [VMEM] * (1 + len(right)),
            [shape((at.chips * height, width), BF16)],
            [],
            2 * self.length * at.chips * height * width,
            [left] + list(right),
        )[0]

    def grad_near(self, name, left, right, by_rows, theirs):
        at = self.at
        size = self.features // at.dp
        height = size if by_rows else left.shape[1]
        width = sum(r.shape[1] for r in right) if by_rows else size
        _, keeps = half_plan(at.chips)
        return call(
            functools.partial(grad_near_body, by_rows, at.chips, size, len(right)),
            name + "_near",
            [VMEM] * (2 + len(right)),
            [shape((height, width), F32)]
            + [shape((height, width), BF16)] * 2
            + [shape((height // 2, width), F32)] * len(keeps),
            [],
            2 * self.length * at.chips * height * width,
            [left, theirs] + list(right),
        )

    def ring_start(self, blocks):
        own, plus, minus, *keeps = blocks
        at = self.at
        return blocks, (at.send(plus, at.plus), at.send(minus, at.minus))

    def ring_rest(self, ring):
        at = self.at
        (own, _, _, *keeps), (from_behind, from_ahead) = ring
        _, order = half_plan(at.chips)
        kept = dict(zip(order, keeps))
        h, n = at.chips // 2, at.chips
        middle = own.shape[0] // 2
        last_b = (from_behind, middle), (from_ahead, middle)
        for step in range(2, h + 1):
            d, e = h - step + 1, h - step
            up = [kept[(d, 0)] + from_behind[:middle].astype(F32)]
            down = [kept[(n - d, 1)] + from_ahead[:middle].astype(F32)]
            if e >= 1:
                up.append(kept[(e, 1)] + from_behind[middle:].astype(F32))
                down.append(kept[(n - e, 0)] + from_ahead[middle:].astype(F32))
            up = up[0] if len(up) == 1 else jnp.concatenate(up, 0)
            down = down[0] if len(down) == 1 else jnp.concatenate(down, 0)
            if e == 0:
                last_b = (from_behind, middle), (from_ahead, middle)
            from_behind = at.send(up.astype(BF16), at.plus)
            from_ahead = at.send(down.astype(BF16), at.minus)
        return own, (from_behind, last_b[1][0]), (last_b[0][0], from_ahead)

    def grad_finish(self, name, ring, planes):
        own, low, high = ring
        out = own.shape if planes == 1 else (planes, own.shape[0], own.shape[1] // planes)
        middle = own.shape[0] // 2
        refs = [low[0], low[1], high[0], high[1]]
        starts = [0, middle, middle, 0]

        def body(own_ref, a, b, c, d, out_ref):
            finish_body(
                planes,
                own_ref,
                (a, starts[0]),
                (b, starts[1]),
                (c, starts[2]),
                (d, starts[3]),
                out_ref,
            )

        return call(
            body,
            name + "_finish",
            [VMEM] * 5,
            [shape(out, F32)],
            [],
            4 * own.size,
            [own] + refs,
        )[0]


def shards(
    dp,
    tensor,
    inputs,
    segment_ids,
    first_gain,
    first_shift,
    project_in,
    query_bias,
    value_bias,
    project_out,
    out_bias,
    second_gain,
    second_shift,
    up_weight,
    up_bias,
    down_weight,
    down_bias,
    cotangent,
):
    at = Places(dp, tensor)
    length, features = inputs.shape
    heads = query_bias.shape[0]
    hidden_units = up_bias.shape[0]
    layer = Layer(at, length, features)
    own = layer.own
    table = at.table()
    chunk32, chunk16 = shape((own, features), F32), shape((own, features), BF16)
    tokens16 = shape((length, features), BF16)
    size = features // dp
    in_places = piece_places(at.chips, size, 1)
    out_places = piece_places(at.chips, heads, 1)
    up_places = piece_places(at.chips, size, 2)
    down_places = piece_places(at.chips, hidden_units, 2)

    hop_in = at.first_hop(project_in)
    vectors = jnp.stack(
        [
            first_gain,
            first_shift,
            out_bias,
            second_gain,
            second_shift,
            down_bias,
            down_bias,
            down_bias,
        ]
    ).astype(F32)
    x_rel, g_rel, first_low, vec = call(
        functools.partial(prologue_body, dp, tensor),
        "prologue",
        [SMEM] + [VMEM] * 3,
        [tokens16] * 3 + [shape(vectors.shape, F32)],
        [],
        20 * length * features,
        [table, inputs, cotangent, vectors],
    )
    ids = at.tokens_in(segment_ids)
    order = at.tokens_in(jnp.arange(length, dtype=jnp.int32))
    allowed = (
        (ids[:, None] == ids[None, :])
        & (ids[:, None] != 0)
        & (order[None, :] <= order[:, None])
    )
    allowed = (allowed | (order[None, :] == order[:, None])).astype(F32)
    biases = (query_bias[None], value_bias[None], up_bias[None])

    hop_in = after(hop_in, first_low, allowed, biases)
    mine_in = at.later_hops(project_in, hop_in)
    hop_out = at.first_hop(after(project_out, hop_in))
    up_parts, down_parts = split_rows(up_weight, 2), split_rows(down_weight, 2)
    hop_up = [at.first_hop(after(up_parts[0], mine_in))]
    mine_out = at.later_hops(project_out, hop_out)
    all_in = at.both_cores(mine_in)

    low_heads = shape((length, heads), BF16)
    query, key, value, probs, mixed = call(
        functools.partial(attend_body, in_places),
        "attend",
        [VMEM] * 4 + [ANY] * len(in_places),
        [low_heads] * 3 + [shape((heads // DH, length, length), F32), low_heads],
        [pltpu.VMEM((3, features, heads), BF16), sems(3, len(in_places))],
        6 * length * heads * features,
        [after(first_low, hop_out), biases[0], biases[1], allowed] + all_in,
    )
    all_out = at.both_cores(mine_out)
    mixed = after(mixed, hop_up[0])
    mine_up = [at.later_hops(up_parts[0], hop_up[0])]
    hop_up += [at.first_hop(after(up_parts[1], hop_up[0]))]
    part = layer.project("project_out", mixed, all_out, out_places, False)
    received = at.to_peers(part[1:])
    hidden, normed_two, inverse_two, second_own = call(
        functools.partial(second_body, tensor),
        "second_norm",
        [VMEM] * (2 + tensor),
        [chunk32, chunk32, shape((own, 128), F32), chunk16],
        [],
        20 * own * features,
        [after(part[0], mine_up[0], hop_up[1]), x_rel, vec] + received,
    )
    mine_up += [at.later_hops(up_parts[1], hop_up[1])]
    hop_down = [at.first_hop(after(down_parts[0], hop_up[1]))]
    all_up = at.both_cores(mine_up[0]) + at.both_cores(mine_up[1])
    second_low, activated, slope = call(
        functools.partial(upper_body, up_places, tensor),
        "upper",
        [VMEM] * (1 + tensor) + [ANY] * len(up_places),
        [
            tokens16,
            shape((length, hidden_units), BF16),
            shape((length, hidden_units), F32),
        ],
        [pltpu.VMEM((features, hidden_units), BF16), sems(len(up_places))],
        2 * length * features * hidden_units,
        [after(biases[2], hop_down[0]), second_own] + at.to_peers(second_own) + all_up,
    )
    mine_down = [at.later_hops(down_parts[0], hop_down[0])]
    hop_down += [at.first_hop(after(down_parts[1], hop_down[0]))]
    far_down = layer.grad_far(
        "grad_down", after(activated, mine_down[0], hop_down[1]), [g_rel], False
    )
    mine_down += [at.later_hops(down_parts[1], hop_down[1])]
    all_down = at.both_cores(mine_down[0]) + at.both_cores(mine_down[1])
    near_down = layer.grad_near(
        "grad_down", after(activated, far_down), [g_rel], False, layer.swapped(far_down)
    )
    upper_low, up_bias_grad = call(
        functools.partial(upper_grad_body, down_places),
        "upper_grad",
        [VMEM] * 2 + [ANY] * len(down_places),
        [shape((length, hidden_units), BF16), shape((1, hidden_units), F32)],
        [pltpu.VMEM((hidden_units, features), BF16), sems(len(down_places))],
        2 * length * features * hidden_units,
        [after(g_rel, near_down), slope] + all_down,
    )
    ring_down = layer.ring_start(near_down)
    part = layer.project("second_part", upper_low, all_up, up_places, True)
    received = at.to_peers(part[1:])
    far_up = layer.grad_far("grad_up", second_low, after([upper_low], part), True)
    feed = layer.project("feed", after(activated, far_up), all_down, down_places, False)
    hidden_grad, hidden_low_own, sums_two = call(
        functools.partial(second_back_body, dp, tensor),
        "second_back",
        [SMEM] + [VMEM] * (4 + tensor),
        [chunk32, chunk16, shape((8, features), F32)],
        [],
        20 * own * features,
        [table, after(part[0], ring_down[1], feed), g_rel, vec, normed_two, inverse_two] + received,
    )
    ring_down = layer.ring_rest(ring_down)
    hidden_pieces = at.to_peers(hidden_low_own)
    near_up = layer.grad_near(
        "grad_up", second_low, after([upper_low], hidden_low_own), True, layer.swapped(far_up)
    )
    back = call(
        functools.partial(attend_back_body, in_places, out_places, tensor),
        "attend_back",
        [VMEM] * (4 + tensor) + [ANY] * (len(out_places) + len(in_places)),
        [tokens16, low_heads, low_heads, low_heads, shape((1, 2 * heads), F32)]
        + layer.chunk_outs(),
        [
            pltpu.VMEM((heads, features), BF16),
            pltpu.VMEM((3, features, heads), BF16),
            pltpu.VMEM((length, heads), BF16),
            sems(len(out_places)),
            sems(len(in_places)),
        ],
        8 * length * heads * features,
        [after(query, ring_down[1:], near_up), key, value, probs, hidden_low_own]
        + hidden_pieces
        + all_out
        + all_in,
    )
    hidden_low, q_low, k_low, v_low, heads_grad, *part = back
    ring_up = layer.ring_start(after(near_up, ring_down[1:]))
    feed_received = at.to_peers(after(feed[1:], hidden_pieces))
    outputs_own = call(
        functools.partial(output_body, dp, tensor),
        "outputs_own",
        [SMEM] + [VMEM] * (2 + tensor),
        [chunk16],
        [],
        4 * own * features,
        [table, after(feed[0], part), hidden, vec] + feed_received,
    )[0]
    received = at.to_peers(after(part[1:], feed_received))
    lows = [q_low, k_low, v_low]
    far_in = layer.grad_far("grad_in", first_low, after(lows, part), True)
    far_out = layer.grad_far("grad_out", mixed, after([hidden_low], far_in), False)
    near_in = layer.grad_near(
        "grad_in", first_low, after(lows, far_out), True, layer.swapped(far_in)
    )
    near_out = layer.grad_near(
        "grad_out", mixed, after([hidden_low], near_in), False, layer.swapped(far_out)
    )
    input_own, sums_one = call(
        functools.partial(first_back_body, dp, tensor),
        "first_back",
        [SMEM] + [VMEM] * (3 + tensor),
        [chunk16, shape((8, features), F32)],
        [],
        20 * own * features,
        [table, after(part[0], ring_up[1], near_out), x_rel, vec, hidden_grad] + received,
    )
    ring_in = layer.ring_start(after(near_in, ring_up[1]))
    ring_out = layer.ring_start(after(near_out, ring_up[1]))
    ring_up = layer.ring_rest(ring_up)

    def assemble(name, chunk, others):
        return call(
            functools.partial(assemble_body, dp, tensor),
            name,
            [SMEM] + [VMEM] * tensor,
            [tokens16],
            [],
            length * features,
            [table, chunk] + others,
        )[0]

    input_others = at.to_peers(input_own)
    output_others = at.to_peers(after(outputs_own, input_others))
    input_gradient = assemble("input_gradient", input_own, input_others)
    outputs = assemble("outputs", outputs_own, output_others)
    ring_in = layer.ring_rest(ring_in)
    ring_out = layer.ring_rest(ring_out)
    grad_down = layer.grad_finish("grad_down", ring_down, 1)
    grad_up = layer.grad_finish("grad_up", ring_up, 1)
    grad_out = layer.grad_finish("grad_out", ring_out, 1)
    grad_in = layer.grad_finish("grad_in", ring_in, 3)

    wide = at.sum_small(jnp.concatenate([sums_one[:2], sums_two[:4]]), True)
    narrow = at.sum_small(jnp.concatenate([heads_grad[0], up_bias_grad[0]]), False)
    return (
        outputs,
        input_gradient,
        wide[0],
        wide[1],
        grad_in,
        narrow[:heads],
        narrow[heads : 2 * heads],
        grad_out,
        wide[2],
        wide[3],
        wide[4],
        grad_up,
        narrow[2 * heads :],
        grad_down,
        wide[5],
    )


def solution(mesh):
    dp, tensor = mesh.shape["dp"], mesh.shape["tensor"]

    def program(*arguments):
        return shards(dp, tensor, *arguments)

    in_specs = (
        P("dp", None),
        P("dp"),
        P(),
        P(),
        P(None, "dp", "tensor"),
        P("tensor"),
        P("tensor"),
        P("tensor", "dp"),
        P(),
        P(),
        P(),
        P("dp", "tensor"),
        P("tensor"),
        P("tensor", "dp"),
        P(),
        P("dp", None),
    )
    out_specs = (
        P("dp", None),
        P("dp", None),
        P(),
        P(),
        P(None, "dp", "tensor"),
        P("tensor"),
        P("tensor"),
        P("tensor", "dp"),
        P(),
        P(),
        P(),
        P("dp", "tensor"),
        P("tensor"),
        P("tensor", "dp"),
        P(),
    )
    return jax.shard_map(program, mesh=mesh, in_specs=in_specs, out_specs=out_specs, check_vma=False)
```

```python
import functools

import jax
import jax.numpy as jnp
from jax import lax
from jax.experimental import pallas as pl
from jax.experimental.pallas import tpu as pltpu
from jax.sharding import PartitionSpec as P

DH = 128
EPSILON = 1e-05
NEGATIVE = -1e30
SCALE = DH ** (-0.5)
F32 = jnp.float32
BF16 = jnp.bfloat16
TILE = 256
ANY = pl.BlockSpec(memory_space=pl.ANY)
VMEM = pl.BlockSpec(memory_space=pltpu.VMEM)
SMEM = pl.BlockSpec(memory_space=pltpu.SMEM)


def nn(left, right):
    return lax.dot_general(left, right, (((1,), (0,)), ((), ())), preferred_element_type=F32)


def nt(left, right):
    return lax.dot_general(left, right, (((1,), (1,)), ((), ())), preferred_element_type=F32)


def tn(left, right):
    return lax.dot_general(left, right, (((0,), (0,)), ((), ())), preferred_element_type=F32)


def shape(dims, dtype):
    return jax.ShapeDtypeStruct(tuple(dims), dtype)


def call(body, name, in_specs, outs, scratch, flops, args):
    moved = sum(a.size * a.dtype.itemsize for a in args)
    moved += sum(o.size * o.dtype.itemsize for o in outs)
    return pl.pallas_call(
        body,
        name=name,
        out_shape=outs,
        in_specs=in_specs,
        out_specs=[VMEM] * len(outs),
        scratch_shapes=scratch,
        cost_estimate=pl.CostEstimate(flops=flops, bytes_accessed=moved, transcendentals=0),
    )(*args)


class Places:
    def __init__(self, dp, tensor):
        self.dp, self.tensor, self.chips = dp, tensor, dp // 2
        self.rank = lax.axis_index("dp")
        self.part = lax.axis_index("tensor")
        self.chip, self.core = self.rank // 2, self.rank % 2
        self.side = self.chip % 2
        self.swap = [(i, i ^ 1) for i in range(dp)]

    def table(self):
        owners = jnp.arange(self.chips, dtype=jnp.int32) * 2
        chunks = self.part ^ jnp.arange(self.tensor, dtype=jnp.int32)
        return jnp.concatenate(
            [owners + self.core, owners + (1 - self.core), chunks, self.side[None]]
        ).astype(jnp.int32)

    def tokens_in(self, values):
        size = values.shape[0] // self.tensor
        return jnp.take(
            values.reshape(self.tensor, size),
            self.part ^ jnp.arange(self.tensor, dtype=jnp.int32),
            axis=0,
        ).reshape(-1)

    def chunk_of(self, values):
        size = values.shape[0] // self.tensor
        return lax.dynamic_slice_in_dim(values, self.part * size, size, 0)

    def half_of(self, values):
        size = values.shape[0] // 2
        return lax.dynamic_slice_in_dim(values, self.side * size, size, 0)

    def to_core(self, values):
        return lax.ppermute(values, "dp", self.swap)

    def to_chip(self, values, k):
        return lax.ppermute(values, "dp", [(i, i ^ (2 * k)) for i in range(self.dp)])

    def to_mate(self, values):
        return self.to_chip(values, 1)

    def to_peer(self, values, k):
        return lax.ppermute(values, "tensor", [(i, i ^ k) for i in range(self.tensor)])

    def to_peers(self, values):
        many = isinstance(values, (list, tuple))
        return [
            self.to_peer(values[k - 1] if many else values, k)
            for k in range(self.tensor - 1, 0, -1)
        ][::-1]

    def exchange(self, blocks):
        groups = [[2 * j + core for j in range(self.chips)] for core in range(2)]
        return lax.all_to_all(blocks, "dp", 0, 0, axis_index_groups=groups, tiled=True)

    def halves(self, block, axis):
        halves = jnp.split(block, 2, axis)
        return jnp.stack([halves[j % 2] for j in range(self.chips)])

    def both_cores(self, blocks):
        return [blocks, self.to_core(blocks)]

    def spread(self, chunk):
        own = self.to_peers(chunk)
        mate = after(self.to_mate(chunk), own)
        return [chunk] + own + [mate] + self.to_peers(mate)

    def sum_small(self, wide, narrow):
        step = 1
        while step < self.tensor:
            wide = wide + self.to_peer(wide, step)
            step *= 2
        values = jnp.concatenate([wide, narrow])
        values = values + self.to_core(values)
        step = 1
        while step < self.chips:
            values = values + self.to_chip(values, step)
            step *= 2
        return values


def after(values, *events):
    values, _ = lax.optimization_barrier((values, events))
    return values


def center_of(values):
    center = values - jnp.mean(values, axis=-1, keepdims=True)
    inverse = lax.rsqrt(jnp.mean(center * center, axis=-1, keepdims=True) + EPSILON)
    return center * inverse, inverse


def norm_back(norm_grad, normed, inverse, gain):
    scaled = norm_grad * gain
    return inverse * (
        scaled
        - jnp.mean(scaled, axis=-1, keepdims=True)
        - normed * jnp.mean(scaled * normed, axis=-1, keepdims=True)
    )


def place(table, p, size):
    return pl.ds(pl.multiple_of(table[p] * size, size), size)


def collect_body(dp, tensor, norm, table, own, vec, *refs):
    chunks, (out,) = refs[:tensor], refs[tensor:]
    rows = chunks[0].shape[0] // 2
    first = 0 if norm else rows
    for s in range(2):
        for k in range(tensor):
            value = own[place(table, dp + k, rows), :] if s == 0 else chunks[k][first : first + rows, :]
            if norm:
                normed, _ = center_of(value.astype(F32))
                value = (normed * vec[0:1, :] + vec[1:2, :]).astype(BF16)
            start = (s * tensor + k) * rows
            out[start : start + rows, :] = value


def blocks_of(arrays):
    return [ref.at[j] for ref in arrays for j in range(ref.shape[0])]


def attend_body(table, x, q_bias, v_bias, allowed, *refs):
    pieces, (q, k, v, probs, mixed), (weight, sems) = blocks_of(refs[:2]), refs[2:-2], refs[-2:]
    count, size = len(pieces), refs[0].shape[2]

    def copy(j, p):
        return pltpu.make_async_copy(
            pieces[p].at[j], weight.at[j, place(table, p, size)], sems.at[j, p]
        )

    for j in range(3):
        for p in range(count):
            copy(j, p).start()
    columns = q.shape[1]
    tile = min(TILE, columns)
    for j, out in enumerate((q, k, v)):
        for p in range(count):
            copy(j, p).wait()
        for start in range(0, columns, tile):
            cols = slice(start, start + tile)
            total = nn(x[...], weight[j, :, cols])
            if j == 0:
                total = total + q_bias[:, cols].astype(F32)
            if j == 2:
                total = total + v_bias[:, cols].astype(F32)
            out[:, cols] = total.astype(BF16)
    heads = columns // DH
    length = allowed.shape[1]
    for s in range(2):
        rows = slice(s * length, (s + 1) * length)
        for h in range(heads):
            cols = slice(h * DH, (h + 1) * DH)
            scores = nt(q[rows, cols], k[rows, cols]) * SCALE
            scores = jnp.where(allowed[s] > 0, scores, NEGATIVE)
            weights = jnp.exp(scores - jnp.max(scores, axis=-1, keepdims=True))
            prob = weights / jnp.sum(weights, axis=-1, keepdims=True)
            probs[s * heads + h] = prob
            mixed[rows, cols] = nn(prob.astype(BF16), v[rows, cols]).astype(BF16)


def put_chunks(total, cols, own, mate, sends):
    rows = own.shape[0]
    length = total.shape[0] // 2
    chunks = length // rows
    own[:, cols] = total[:rows]
    mate[:, cols] = total[length : length + rows]
    for k in range(1, chunks):
        for s in range(2):
            part = total[s * length + k * rows : s * length + (k + 1) * rows].astype(BF16)
            if len(sends) == chunks - 1:
                sends[k - 1][s * rows : (s + 1) * rows, cols] = part
            else:
                sends[s * (chunks - 1) + k - 1][:, cols] = part


def column_copies(table, arrays, weight, sems):
    width = arrays[0].shape[2]
    return [
        pltpu.make_async_copy(piece, weight.at[:, place(table, p, width)], sems.at[p])
        for p, piece in enumerate(blocks_of(arrays))
    ]


def row_copies(table, arrays, weight, sems):
    size = arrays[0].shape[1]
    return [
        pltpu.make_async_copy(piece, weight.at[place(table, p, size)], sems.at[p])
        for p, piece in enumerate(blocks_of(arrays))
    ]


def project_body(by_rows, table, left, *refs):
    pieces, (own, mate, *sends), (weight, sems) = refs[:2], refs[2:-2], refs[-2:]
    copies = (row_copies if by_rows else column_copies)(table, pieces, weight, sems)
    for copy in copies:
        copy.start()
    size = pieces[0].shape[1 if by_rows else 2]
    for p, copy in enumerate(copies):
        copy.wait()
        cols = place(table, p, size)
        if by_rows:
            total = nt(left[...], weight[cols, :])
        else:
            total = nn(left[...], weight[:, cols])
        put_chunks(total, cols, own, mate, sends)


def fold_body(mate, *refs):
    received, (out,) = refs[:-1], refs[-1:]
    total = mate[...]
    rows = mate.shape[0]
    for ref in received:
        total = total + ref[ref.shape[0] - rows :, :].astype(F32)
    out[...] = total.astype(BF16)


def summed(own, received):
    total = own[...]
    rows = own.shape[0]
    for ref in received:
        total = total + ref[:rows, :].astype(F32)
    return total


def second_body(count, own, x, vec, *refs):
    received, (hidden, normed_out, inverse_out, low) = refs[:count], refs[count:]
    value = x[...].astype(F32) + summed(own, received) + vec[2:3, :]
    hidden[...] = value
    normed, inverse = center_of(value)
    normed_out[...] = normed
    inverse_out[...] = jnp.broadcast_to(inverse, inverse_out.shape)
    low[...] = (normed * vec[3:4, :] + vec[4:5, :]).astype(BF16)


def upper_body(chunk_count, table, bias, *refs):
    chunks, refs = refs[:chunk_count], refs[chunk_count:]
    pieces, (low, activated, slope), (weight, sems) = refs[:2], refs[2:-2], refs[-2:]
    copies = row_copies(table, pieces, weight, sems)
    for copy in copies:
        copy.start()
    rows = chunks[0].shape[0]
    for k, chunk in enumerate(chunks):
        low[k * rows : (k + 1) * rows, :] = chunk[...]
    for copy in copies:
        copy.wait()
    columns = weight.shape[1]
    tile = min(TILE, columns)

    @pl.loop(0, columns // tile)
    def _(i):
        cols = pl.ds(pl.multiple_of(i * tile, tile), tile)
        value = nn(low[...], weight[:, cols]) + bias[:, cols].astype(F32)
        below = 0.5 * (1.0 + lax.erf(value * (0.5**0.5)))
        activated[:, cols] = (value * below).astype(BF16)
        density = jnp.exp(-0.5 * value * value) * 0.3989422804014327
        slope[:, cols] = below + value * density


def upper_grad_body(side_at, table, g, slope, *refs):
    pieces, (low, bias_grad), (weight, sems) = refs[:2], refs[2:-2], refs[-2:]
    copies = column_copies(table, pieces, weight, sems)
    for copy in copies:
        copy.start()
    bias_grad[...] = jnp.zeros(bias_grad.shape, F32)
    for copy in copies:
        copy.wait()
    hidden = weight.shape[0]
    tile = min(TILE, hidden)
    first = table[side_at] * hidden

    @pl.loop(0, hidden // tile)
    def _(i):
        cols = pl.ds(pl.multiple_of(i * tile, tile), tile)
        grad = nt(g[...], weight[cols, :]) * slope[:, cols]
        low[:, cols] = grad.astype(BF16)
        there = pl.ds(pl.multiple_of(first + i * tile, tile), tile)
        bias_grad[:, there] = jnp.sum(grad, axis=0, keepdims=True)


def second_back_body(count, own, g, vec, normed, inverse, *refs):
    received, (hidden_grad, low, sums) = refs[:count], refs[count:]
    total = summed(own, received)
    upstream = g[...].astype(F32)
    grad = upstream + norm_back(total, normed[...], inverse[:, 0:1], vec[3:4, :])
    hidden_grad[...] = grad
    low[...] = grad.astype(BF16)
    for i, values in enumerate((grad, total * normed[...], total, upstream)):
        sums[i : i + 1, :] = jnp.sum(values, axis=0, keepdims=True)


def attend_back_body(side_at, chunk_count, table, q, k, v, probs, *refs):
    chunks, refs = refs[:chunk_count], refs[chunk_count:]
    outs_p, ins_p, refs = refs[:2], refs[2:4], refs[4:]
    (low, q_low, k_low, v_low, bias_grad, own, mate, *sends) = refs[:-5]
    out_weight, in_weight, mixed_grad, out_sems, in_sems = refs[-5:]
    copies = column_copies(table, outs_p, out_weight, out_sems)
    for copy in copies:
        copy.start()
    size = ins_p[0].shape[2]
    ins = [
        pltpu.make_async_copy(piece, in_weight.at[:, place(table, p, size)], in_sems.at[p])
        for p, piece in enumerate(blocks_of(ins_p))
    ]
    for copy in ins:
        copy.start()
    rows = chunks[0].shape[0]
    for j, chunk in enumerate(chunks):
        low[j * rows : (j + 1) * rows, :] = chunk[...]
    bias_grad[...] = jnp.zeros(bias_grad.shape, F32)
    for copy in copies:
        copy.wait()
    columns = q.shape[1]
    tile = min(TILE, columns)
    for start in range(0, columns, tile):
        cols = slice(start, start + tile)
        mixed_grad[:, cols] = nt(low[...], out_weight[cols, :]).astype(BF16)
    heads = columns // DH
    length = probs.shape[1]
    first = table[side_at] * columns
    for h in range(heads):
        cols = slice(h * DH, (h + 1) * DH)
        q_sum = v_sum = 0.0
        for s in range(2):
            rows = slice(s * length, (s + 1) * length)
            prob, down = probs[s * heads + h], mixed_grad[rows, cols]
            prob_grad = nt(down, v[rows, cols])
            inner = jnp.sum(prob * prob_grad, axis=-1, keepdims=True)
            score_low = (prob * (prob_grad - inner) * SCALE).astype(BF16)
            query_grad = nn(score_low, k[rows, cols])
            q_low[rows, cols] = query_grad.astype(BF16)
            q_sum = q_sum + jnp.sum(query_grad, axis=0, keepdims=True)
            k_low[rows, cols] = tn(score_low, q[rows, cols]).astype(BF16)
            value_grad = tn(prob.astype(BF16), down)
            v_low[rows, cols] = value_grad.astype(BF16)
            v_sum = v_sum + jnp.sum(value_grad, axis=0, keepdims=True)
        there = pl.multiple_of(first + h * DH, DH)
        bias_grad[:, pl.ds(there, DH)] = q_sum
        bias_grad[:, pl.ds(pl.multiple_of(there + 2 * columns, DH), DH)] = v_sum
    for p, copy in enumerate(ins):
        copy.wait()
        cols = place(table, p, size)
        total = nt(q_low[...], in_weight[0, cols, :])
        total = total + nt(k_low[...], in_weight[1, cols, :])
        total = total + nt(v_low[...], in_weight[2, cols, :])
        put_chunks(total, cols, own, mate, sends)


def first_back_body(count, own, x, vec, hidden_grad, *refs):
    received, (result, sums) = refs[:count], refs[count:]
    total = summed(own, received)
    normed, inverse = center_of(x[...].astype(F32))
    grad = hidden_grad[...] + norm_back(total, normed, inverse, vec[0:1, :])
    result[...] = grad.astype(BF16)
    for i, values in enumerate((total * normed, total)):
        sums[i : i + 1, :] = jnp.sum(values, axis=0, keepdims=True)


def output_body(count, own, hidden, vec, *refs):
    received, (result,) = refs[:count], refs[count:]
    result[...] = (hidden[...] + summed(own, received) + vec[5:6, :]).astype(BF16)


def assemble_body(dp, tensor, table, *refs):
    chunks, (result,) = refs[:tensor], refs[tensor:]
    rows = chunks[0].shape[0]
    for k, chunk in enumerate(chunks):
        result[place(table, dp + k, rows), :] = chunk[...]


def grad_blocks(table, left, right, by_rows, first, chips, size, put):
    if by_rows:
        width = right[0].shape[1]
        tile = min(TILE, width)
        for block in range(chips):
            turned = left[:, place(table, first + block, size)].T
            for j, ref in enumerate(right):
                for c in range(0, width, tile):
                    put(block, 0, j * width + c, nn(turned, ref[:, c : c + tile]))
    else:
        hidden = left.shape[1]
        step = min(512, hidden)
        for r in range(0, hidden, step):
            turned = left[:, r : r + step].T
            for block in range(chips):
                put(block, r, 0, nn(turned, right[0][:, place(table, first + block, size)]))


def grad_body(by_rows, first, chips, size, count, table, left, *refs):
    right, theirs, out = refs[:count], refs[count:-1], refs[-1]

    def put(block, low, column, value):
        rows, cols = slice(low, low + value.shape[0]), slice(column, column + value.shape[1])
        for ref in theirs:
            value = value + ref[block, rows, cols].astype(F32)
        out[block, rows, cols] = value.astype(BF16)

    grad_blocks(table, left, right, by_rows, first, chips, size, put)


def finish_body(by_rows, planes, first, cols, blocks, out):
    chips, rows, _ = blocks.shape
    here = slice(first, first + cols)
    for half in range(2):
        total = blocks[half, :, here].astype(F32)
        for j in range(half + 2, chips, 2):
            total = total + blocks[j, :, here].astype(F32)
        if not by_rows:
            out[half * rows : (half + 1) * rows, :] = total
        elif planes == 1:
            out[:, half * cols : (half + 1) * cols] = total
        else:
            width = cols // planes
            for j in range(planes):
                out[j, :, half * width : (half + 1) * width] = total[:, j * width : (j + 1) * width]


def sems(*dims):
    return pltpu.SemaphoreType.DMA(tuple(dims))


class Layer:
    def __init__(self, at, length, features):
        self.at, self.table = at, at.table()
        self.length, self.features = length, features
        self.own = length // at.tensor
        self.side_at = at.dp + at.tensor

    def chunk_outs(self, split):
        count = self.at.tensor - 1
        sends = [shape((self.own, self.features), BF16)] * (2 * count)
        if not split:
            sends = [shape((2 * self.own, self.features), BF16)] * count
        return [shape((self.own, self.features), F32)] * 2 + sends

    def collect(self, name, own, vec, chunks, norm):
        at = self.at
        return call(
            functools.partial(collect_body, at.dp, at.tensor, norm),
            name,
            [SMEM] + [VMEM] * (2 + at.tensor),
            [shape((2 * self.length, self.features), BF16)],
            [],
            20 * self.length * self.features,
            [self.table, own, vec] + chunks,
        )[0]

    def project(self, name, left, blocks, by_rows, split):
        inner = left.shape[1]
        weight = (self.features, inner) if by_rows else (inner, self.features)
        return call(
            functools.partial(project_body, by_rows),
            name,
            [SMEM, VMEM] + [ANY] * 2,
            self.chunk_outs(split),
            [pltpu.VMEM(weight, BF16), sems(self.at.dp)],
            4 * self.length * inner * self.features,
            [self.table, left] + blocks,
        )

    def fold(self, name, mate, received):
        return call(
            fold_body,
            name,
            [VMEM] * (1 + len(received)),
            [shape(mate.shape, BF16)],
            [],
            mate.size * 4,
            [mate] + received,
        )[0]

    def trade(self, part, split):
        count = self.at.tensor - 1
        if not split:
            received = self.at.to_peers(part[2:])
            return received, received
        return self.at.to_peers(part[2 + count :]), self.at.to_peers(part[2 : 2 + count])

    def reduce(self, name, part, traded):
        for_mate, others = traded
        folded = self.fold(name + "_fold", part[1], for_mate)
        return others + [self.at.to_mate(folded)], folded

    def block_shape(self, left, right, by_rows):
        size = self.features // self.at.dp
        if by_rows:
            return size, (size, sum(r.shape[1] for r in right))
        return size, (left.shape[1], size)

    def grad(self, name, left, right, by_rows, *theirs):
        chips = self.at.chips
        size, block = self.block_shape(left, right, by_rows)
        return call(
            functools.partial(grad_body, by_rows, 0 if theirs else chips, chips, size, len(right)),
            name + ("_near" if theirs else "_far"),
            [SMEM] + [VMEM] * (1 + len(right) + len(theirs)),
            [shape((chips,) + block, BF16)],
            [],
            4 * self.length * chips * block[0] * block[1],
            [self.table, left] + list(right) + list(theirs),
        )[0]

    def grad_far(self, name, left, right, by_rows):
        return self.grad(name, left, right, by_rows)

    def grad_near(self, name, left, right, by_rows, theirs):
        return self.grad(name, left, right, by_rows, theirs)

    def grad_finish(self, name, blocks, by_rows, where, planes=1):
        _, rows, width = blocks.shape
        first, cols = where[0] % width, where[1]
        out = (rows, 2 * cols) if by_rows else (2 * rows, cols)
        if planes > 1:
            out = (planes, rows, 2 * cols // planes)
        return call(
            functools.partial(finish_body, by_rows, planes, first, cols),
            name + "_finish",
            [VMEM],
            [shape(out, F32)],
            [],
            blocks.size,
            [blocks],
        )[0]


def shards(
    dp,
    tensor,
    inputs,
    segment_ids,
    first_gain,
    first_shift,
    project_in,
    query_bias,
    value_bias,
    project_out,
    out_bias,
    second_gain,
    second_shift,
    up_weight,
    up_bias,
    down_weight,
    down_bias,
    cotangent,
):
    at = Places(dp, tensor)
    length, features = inputs.shape
    layer = Layer(at, length, features)
    own, table, side_at = layer.own, layer.table, layer.side_at
    heads, hidden_units = query_bias.shape[0] // 2, up_bias.shape[0] // 2
    both = 2 * length
    chunk_count, size = 2 * tensor, features // dp
    chunk32, chunk16 = shape((own, features), F32), shape((own, features), BF16)
    tokens16 = shape((both, features), BF16)

    x_own, g_own = at.chunk_of(inputs), at.chunk_of(cotangent)
    mate = at.to_mate(jnp.concatenate([x_own, g_own]))
    ids = at.tokens_in(segment_ids)
    mate_ids = at.to_mate(ids)
    mine_in = at.exchange(after(at.halves(project_in, 2), mate, mate_ids))
    mate_chunks = [mate] + at.to_peers(mate)
    out_blocks, up_blocks = at.halves(project_out, 0), at.halves(up_weight, 1)
    down_blocks = at.halves(down_weight, 0)
    mate_chunks = after(mate_chunks, out_blocks, up_blocks, down_blocks)
    vec = jnp.stack(
        [
            first_gain,
            first_shift,
            out_bias,
            second_gain,
            second_shift,
            down_bias,
            down_bias,
            down_bias,
        ]
    ).astype(F32)
    biases = [at.half_of(b)[None] for b in (query_bias, value_bias, up_bias)]
    order = at.tokens_in(jnp.arange(length, dtype=jnp.int32))
    ids = jnp.stack([ids, mate_ids])
    allowed = (
        (ids[:, :, None] == ids[:, None, :])
        & (ids[:, :, None] != 0)
        & (order[None, None, :] <= order[None, :, None])
    )
    allowed = (allowed | (order[None, None, :] == order[None, :, None])).astype(F32)
    first_low = layer.collect("first_norm", inputs, vec, mate_chunks, True)
    g = layer.collect("upstream", cotangent, vec, mate_chunks, False)
    mine_in = after(mine_in, first_low, allowed, biases, g)
    mine_out = at.exchange(after(out_blocks, mine_in))

    all_in = at.both_cores(mine_in)
    low_heads = shape((both, heads), BF16)
    query, key, value, probs, mixed = call(
        attend_body,
        "attend",
        [SMEM] + [VMEM] * 4 + [ANY] * 2,
        [low_heads] * 3 + [shape((2 * heads // DH, length, length), F32), low_heads],
        [pltpu.VMEM((3, features, heads), BF16), sems(3, dp)],
        12 * length * heads * features,
        [table, first_low, biases[0], biases[1], allowed] + all_in,
    )
    mine_out = after(mine_out, mixed)
    mine_up = at.exchange(after(up_blocks, mine_out))
    all_out = at.both_cores(mine_out)
    part = layer.project("project_out", mixed, all_out, False, True)
    received, _ = layer.reduce("project_out", part, layer.trade(part, True))
    hidden, normed_two, inverse_two, second_own = call(
        functools.partial(second_body, len(received)),
        "second_norm",
        [VMEM] * (3 + len(received)),
        [chunk32, chunk32, shape((own, 128), F32), chunk16],
        [],
        20 * own * features,
        [part[0], x_own, vec] + received,
    )
    second_chunks = at.spread(second_own)
    mine_up = after(mine_up, second_own)
    mine_down = at.exchange(after(down_blocks, mine_up, second_chunks[tensor]))
    all_up = at.both_cores(mine_up)
    second_low, activated, slope = call(
        functools.partial(upper_body, chunk_count),
        "upper",
        [SMEM] + [VMEM] * (1 + chunk_count) + [ANY] * 2,
        [tokens16, shape((both, hidden_units), BF16), shape((both, hidden_units), F32)],
        [pltpu.VMEM((features, hidden_units), BF16), sems(dp)],
        4 * length * features * hidden_units,
        [table, biases[2]] + second_chunks + all_up,
    )
    far_down = layer.grad_far("grad_down", activated, [g], False)
    near_down = layer.grad_near("grad_down", activated, [g], False, at.to_core(far_down))
    mine_down = after(mine_down, near_down)
    ring_down = at.exchange(after(near_down, mine_down))
    all_down = at.both_cores(mine_down)
    upper_low, up_bias_grad = call(
        functools.partial(upper_grad_body, side_at),
        "upper_grad",
        [SMEM] + [VMEM] * 2 + [ANY] * 2,
        [shape((both, hidden_units), BF16), shape((1, 2 * hidden_units), F32)],
        [pltpu.VMEM((hidden_units, features), BF16), sems(dp)],
        4 * length * features * hidden_units,
        [table, g, slope] + all_down,
    )
    part = layer.project("second_part", upper_low, all_up, True, True)
    traded = layer.trade(part, True)
    far_up = layer.grad_far("grad_up", second_low, after([upper_low], traded[0][0]), True)
    received, folded = layer.reduce("second_part", part, traded)
    near_up = layer.grad_near(
        "grad_up", second_low, after([upper_low], folded), True, at.to_core(far_up)
    )
    hidden_grad, hidden_low_own, sums_two = call(
        functools.partial(second_back_body, len(received)),
        "second_back",
        [VMEM] * (5 + len(received)),
        [chunk32, chunk16, shape((8, features), F32)],
        [],
        20 * own * features,
        [after(part[0], near_up), g_own, vec, normed_two, inverse_two] + received,
    )
    hidden_chunks = at.spread(hidden_low_own)
    ring_up = at.exchange(after(near_up, ring_down, hidden_chunks[tensor]))
    feed = layer.project("feed", after(activated, hidden_low_own), all_down, False, False)
    feed_traded = layer.trade(after(feed, hidden_chunks), False)
    back = call(
        functools.partial(attend_back_body, side_at, chunk_count),
        "attend_back",
        [SMEM] + [VMEM] * (4 + chunk_count) + [ANY] * 4,
        [tokens16, low_heads, low_heads, low_heads, shape((1, 4 * heads), F32)]
        + layer.chunk_outs(True),
        [
            pltpu.VMEM((heads, features), BF16),
            pltpu.VMEM((3, features, heads), BF16),
            pltpu.VMEM((both, heads), BF16),
            sems(dp),
            sems(dp),
        ],
        16 * length * heads * features,
        [table, after(query, feed, ring_down), key, value, probs]
        + hidden_chunks
        + all_out
        + all_in,
    )
    hidden_low, q_low, k_low, v_low, heads_grad, *part = back
    lows = [q_low, k_low, v_low]
    part, feed_traded = after(part, feed_traded), after(feed_traded, part)
    traded = layer.trade(part, True)
    feed_received, feed_folded = layer.reduce("feed", feed, feed_traded)
    far_in = layer.grad_far("grad_in", first_low, after(lows, feed_folded, traded[0][0]), True)
    far_out = layer.grad_far("grad_out", mixed, after([hidden_low], far_in), False)
    received, folded = layer.reduce("first_part", part, traded)
    near_in = layer.grad_near(
        "grad_in", first_low, after(lows, far_out, folded, traded[1][0]), True, at.to_core(far_in)
    )
    near_out = layer.grad_near(
        "grad_out", mixed, after([hidden_low], near_in), False, at.to_core(far_out)
    )
    width = near_in.shape[2]
    if near_in.shape[1] == near_out.shape[1]:
        blocks = jnp.concatenate([near_in, near_out], 2)
        ring_in = ring_out = at.exchange(after(blocks, ring_up, received[-1]))
    else:
        ring_in = at.exchange(after(near_in, ring_up, received[-1]))
        ring_out = at.exchange(after(near_out, ring_in))
    input_own, sums_one = call(
        functools.partial(first_back_body, len(received)),
        "first_back",
        [VMEM] * (4 + len(received)),
        [chunk16, shape((8, features), F32)],
        [],
        20 * own * features,
        [part[0], x_own, vec, hidden_grad] + received,
    )
    outputs_own = call(
        functools.partial(output_body, len(feed_received)),
        "outputs_own",
        [VMEM] * (3 + len(feed_received)),
        [chunk16],
        [],
        4 * own * features,
        [feed[0], hidden, vec] + feed_received,
    )[0]

    def assemble(name, chunk):
        return call(
            functools.partial(assemble_body, dp, tensor),
            name,
            [SMEM] + [VMEM] * tensor,
            [shape((length, features), BF16)],
            [],
            length * features,
            [table, chunk] + at.to_peers(chunk),
        )[0]

    input_gradient = assemble("input_gradient", input_own)
    outputs = assemble("outputs", outputs_own)
    grad_down = layer.grad_finish("grad_down", ring_down, False, (0, size))
    grad_up = layer.grad_finish("grad_up", ring_up, True, (0, hidden_units))
    grad_out = layer.grad_finish("grad_out", ring_out, False, (-size, size))
    grad_in = layer.grad_finish("grad_in", ring_in, True, (0, width), 3)

    narrow = jnp.concatenate([heads_grad[0], up_bias_grad[0]])
    rows = -(-narrow.shape[0] // features)
    narrow = jnp.pad(narrow, (0, rows * features - narrow.shape[0])).reshape(rows, features)
    sums = at.sum_small(jnp.concatenate([sums_one[:2], sums_two[:4]]), narrow)
    narrow = sums[6:].reshape(-1)
    heads, hidden_units = 2 * heads, 2 * hidden_units
    return (
        outputs,
        input_gradient,
        sums[0],
        sums[1],
        grad_in,
        narrow[:heads],
        narrow[heads : 2 * heads],
        grad_out,
        sums[2],
        sums[3],
        sums[4],
        grad_up,
        narrow[2 * heads : 2 * heads + hidden_units],
        grad_down,
        sums[5],
    )


def solution(mesh):
    dp, tensor = mesh.shape["dp"], mesh.shape["tensor"]

    def program(*arguments):
        return shards(dp, tensor, *arguments)

    in_specs = (
        P("dp", None),
        P("dp"),
        P(),
        P(),
        P(None, "dp", "tensor"),
        P("tensor"),
        P("tensor"),
        P("tensor", "dp"),
        P(),
        P(),
        P(),
        P("dp", "tensor"),
        P("tensor"),
        P("tensor", "dp"),
        P(),
        P("dp", None),
    )
    out_specs = (
        P("dp", None),
        P("dp", None),
        P(),
        P(),
        P(None, "dp", "tensor"),
        P("tensor"),
        P("tensor"),
        P("tensor", "dp"),
        P(),
        P(),
        P(),
        P("dp", "tensor"),
        P("tensor"),
        P("tensor", "dp"),
        P(),
    )
    return jax.shard_map(program, mesh=mesh, in_specs=in_specs, out_specs=out_specs, check_vma=False)
```

```python
import functools

import jax
import jax.numpy as jnp
from jax import lax
from jax.experimental import pallas as pl
from jax.experimental.pallas import tpu as pltpu
from jax.sharding import PartitionSpec as P

DH = 128
EPSILON = 1e-05
NEGATIVE = -1e30
SCALE = DH ** (-0.5)
F32 = jnp.float32
BF16 = jnp.bfloat16
TILE = 512
ANY = pl.BlockSpec(memory_space=pl.ANY)
VMEM = pl.BlockSpec(memory_space=pltpu.VMEM)
SMEM = pl.BlockSpec(memory_space=pltpu.SMEM)


def nn(left, right):
    return lax.dot_general(left, right, (((1,), (0,)), ((), ())), preferred_element_type=F32)


def nt(left, right):
    return lax.dot_general(left, right, (((1,), (1,)), ((), ())), preferred_element_type=F32)


def tn(left, right):
    return lax.dot_general(left, right, (((0,), (0,)), ((), ())), preferred_element_type=F32)


def shape(dims, dtype):
    return jax.ShapeDtypeStruct(tuple(dims), dtype)


def call(body, name, in_specs, outs, scratch, flops, args):
    moved = sum(a.size * a.dtype.itemsize for a in args)
    moved += sum(o.size * o.dtype.itemsize for o in outs)
    return pl.pallas_call(
        body,
        name=name,
        out_shape=outs,
        in_specs=in_specs,
        out_specs=[VMEM] * len(outs),
        scratch_shapes=scratch,
        cost_estimate=pl.CostEstimate(flops=flops, bytes_accessed=moved, transcendentals=0),
    )(*args)


class Places:
    def __init__(self, dp, tensor):
        self.dp, self.tensor, self.chips = dp, tensor, dp // 2
        self.rank = lax.axis_index("dp")
        self.part = lax.axis_index("tensor")
        self.chip, self.core = self.rank // 2, self.rank % 2
        self.side = self.chip % 2
        self.swap = [(i, i ^ 1) for i in range(dp)]

    def table(self):
        owners = jnp.arange(self.chips, dtype=jnp.int32) * 2
        chunks = self.part ^ jnp.arange(self.tensor, dtype=jnp.int32)
        return jnp.concatenate(
            [owners + self.core, owners + (1 - self.core), chunks, self.side[None]]
        ).astype(jnp.int32)

    def tokens_in(self, values):
        size = values.shape[0] // self.tensor
        return jnp.take(
            values.reshape(self.tensor, size),
            self.part ^ jnp.arange(self.tensor, dtype=jnp.int32),
            axis=0,
        ).reshape(-1)

    def chunk_of(self, values):
        size = values.shape[0] // self.tensor
        return lax.dynamic_slice_in_dim(values, self.part * size, size, 0)

    def half_of(self, values):
        size = values.shape[0] // 2
        return lax.dynamic_slice_in_dim(values, self.side * size, size, 0)

    def to_core(self, values):
        return lax.ppermute(values, "dp", self.swap)

    def to_chip(self, values, k):
        return lax.ppermute(values, "dp", [(i, i ^ (2 * k)) for i in range(self.dp)])

    def to_mate(self, values):
        return self.to_chip(values, 1)

    def to_peer(self, values, k):
        return lax.ppermute(values, "tensor", [(i, i ^ k) for i in range(self.tensor)])

    def to_peers(self, values):
        many = isinstance(values, (list, tuple))
        return [
            self.to_peer(values[k - 1] if many else values, k)
            for k in range(self.tensor - 1, 0, -1)
        ][::-1]

    def exchange(self, blocks):
        groups = [[2 * j + core for j in range(self.chips)] for core in range(2)]
        return lax.all_to_all(blocks, "dp", 0, 0, axis_index_groups=groups, tiled=True)

    def halves(self, block, axis):
        halves = jnp.split(block, 2, axis)
        return jnp.stack([halves[j % 2] for j in range(self.chips)])

    def both_cores(self, blocks):
        return [blocks, self.to_core(blocks)]

    def spread(self, chunk):
        own = self.to_peers(chunk)
        mate = after(self.to_mate(chunk), own[:-1])
        return [chunk] + own + [mate] + self.to_peers(mate)

    def sum_small(self, wide, narrow):
        step = 1
        while step < self.tensor:
            wide = wide + self.to_peer(wide, step)
            step *= 2
        values = jnp.concatenate([wide, narrow])
        values = values + self.to_core(values)
        step = 1
        while step < self.chips:
            values = values + self.to_chip(values, step)
            step *= 2
        return values


def after(values, *events):
    values, _ = lax.optimization_barrier((values, events))
    return values


def center_of(values):
    center = values - jnp.mean(values, axis=-1, keepdims=True)
    inverse = lax.rsqrt(jnp.mean(center * center, axis=-1, keepdims=True) + EPSILON)
    return center * inverse, inverse


def norm_back(norm_grad, normed, inverse, gain):
    scaled = norm_grad * gain
    return inverse * (
        scaled
        - jnp.mean(scaled, axis=-1, keepdims=True)
        - normed * jnp.mean(scaled * normed, axis=-1, keepdims=True)
    )


def place(table, p, size):
    return pl.ds(pl.multiple_of(table[p] * size, size), size)


def collect_body(dp, tensor, norm, table, own, vec, *refs):
    chunks, (out,) = refs[:tensor], refs[tensor:]
    rows = chunks[0].shape[0] // 2
    first = 0 if norm else rows
    for s in range(2):
        for k in range(tensor):
            value = own[place(table, dp + k, rows), :] if s == 0 else chunks[k][first : first + rows, :]
            if norm:
                normed, _ = center_of(value.astype(F32))
                value = (normed * vec[0:1, :] + vec[1:2, :]).astype(BF16)
            start = (s * tensor + k) * rows
            out[start : start + rows, :] = value


def blocks_of(arrays):
    return [ref.at[j] for ref in arrays for j in range(ref.shape[0])]


def attend_body(table, x, q_bias, v_bias, allowed, *refs):
    pieces, (q, k, v, probs, mixed), (weight, sems) = blocks_of(refs[:2]), refs[2:-2], refs[-2:]
    count, size = len(pieces), refs[0].shape[2]

    def copy(j, p):
        return pltpu.make_async_copy(
            pieces[p].at[j], weight.at[j, place(table, p, size)], sems.at[j, p]
        )

    for j in range(3):
        for p in range(count):
            copy(j, p).start()
    columns = q.shape[1]
    tile = min(TILE, columns)
    for j, out in enumerate((q, k, v)):
        for p in range(count):
            copy(j, p).wait()
        for start in range(0, columns, tile):
            cols = slice(start, start + tile)
            total = nn(x[...], weight[j, :, cols])
            if j == 0:
                total = total + q_bias[:, cols].astype(F32)
            if j == 2:
                total = total + v_bias[:, cols].astype(F32)
            out[:, cols] = total.astype(BF16)
    heads = columns // DH
    length = allowed.shape[1]
    for s in range(2):
        rows = slice(s * length, (s + 1) * length)
        for h in range(heads):
            cols = slice(h * DH, (h + 1) * DH)
            scores = nt(q[rows, cols], k[rows, cols]) * SCALE
            scores = jnp.where(allowed[s] > 0, scores, NEGATIVE)
            weights = jnp.exp(scores - jnp.max(scores, axis=-1, keepdims=True))
            prob = weights / jnp.sum(weights, axis=-1, keepdims=True)
            probs[s * heads + h] = prob
            mixed[rows, cols] = nn(prob.astype(BF16), v[rows, cols]).astype(BF16)


def put_chunks(total, cols, own, mate, sends):
    rows = own.shape[0]
    length = total.shape[0] // 2
    chunks = length // rows
    own[:, cols] = total[:rows]
    mate[:, cols] = total[length : length + rows]
    for k in range(1, chunks):
        for s in range(2):
            part = total[s * length + k * rows : s * length + (k + 1) * rows].astype(BF16)
            sends[s * (chunks - 1) + k - 1][:, cols] = part


def column_copies(table, arrays, weight, sems):
    width = arrays[0].shape[-1]
    blocks = blocks_of(arrays)
    if len(arrays[0].shape) == 4:
        blocks = [block.at[3] for block in blocks]
    return [
        pltpu.make_async_copy(block, weight.at[:, place(table, p, width)], sems.at[p])
        for p, block in enumerate(blocks)
    ]


def row_copies(table, arrays, weight, sems):
    size = arrays[0].shape[1]
    return [
        pltpu.make_async_copy(piece, weight.at[place(table, p, size)], sems.at[p])
        for p, piece in enumerate(blocks_of(arrays))
    ]


def project_body(by_rows, table, left, *refs):
    pieces, (own, mate, *sends), (weight, sems) = refs[:2], refs[2:-2], refs[-2:]
    copies = (row_copies if by_rows else column_copies)(table, pieces, weight, sems)
    for copy in copies:
        copy.start()
    size = pieces[0].shape[1 if by_rows else -1]
    chips = pieces[0].shape[0]
    for j in range(chips):
        copies[j].wait()
        copies[chips + j].wait()
        cols = slice(2 * j * size, 2 * (j + 1) * size)
        if by_rows:
            total = nt(left[...], weight[cols, :])
        else:
            total = nn(left[...], weight[:, cols])
        put_chunks(total, cols, own, mate, sends)


def fold_body(mate, *refs):
    refs[-1][...] = summed(mate, refs[:-1]).astype(BF16)


def summed(own, received):
    total = own[...]
    for ref in received:
        total = total + ref[...].astype(F32)
    return total


def second_body(count, own, x, vec, *refs):
    received, (hidden, normed_out, inverse_out, low) = refs[:count], refs[count:]
    value = x[...].astype(F32) + summed(own, received) + vec[2:3, :]
    hidden[...] = value
    normed, inverse = center_of(value)
    normed_out[...] = normed
    inverse_out[...] = jnp.broadcast_to(inverse, inverse_out.shape)
    low[...] = (normed * vec[3:4, :] + vec[4:5, :]).astype(BF16)


def upper_body(chunk_count, table, bias, *refs):
    chunks, refs = refs[:chunk_count], refs[chunk_count:]
    pieces, (low, activated, slope), (weight, sems) = refs[:2], refs[2:-2], refs[-2:]
    copies = row_copies(table, pieces, weight, sems)
    for copy in copies:
        copy.start()
    rows = chunks[0].shape[0]
    for k, chunk in enumerate(chunks):
        low[k * rows : (k + 1) * rows, :] = chunk[...]
    for copy in copies:
        copy.wait()
    columns = weight.shape[1]
    tile = min(TILE, columns)

    @pl.loop(0, columns // tile)
    def _(i):
        cols = pl.ds(pl.multiple_of(i * tile, tile), tile)
        value = nn(low[...], weight[:, cols]) + bias[:, cols].astype(F32)
        below = 0.5 * (1.0 + lax.erf(value * (0.5**0.5)))
        activated[:, cols] = (value * below).astype(BF16)
        density = jnp.exp(-0.5 * value * value) * 0.3989422804014327
        slope[:, cols] = below + value * density


def upper_grad_body(side_at, table, g, slope, *refs):
    pieces, (low, bias_grad), (weight, sems) = refs[:2], refs[2:-2], refs[-2:]
    copies = column_copies(table, pieces, weight, sems)
    for copy in copies:
        copy.start()
    bias_grad[...] = jnp.zeros(bias_grad.shape, F32)
    for copy in copies:
        copy.wait()
    hidden = weight.shape[0]
    tile = min(TILE, hidden)
    first = table[side_at] * hidden

    @pl.loop(0, hidden // tile)
    def _(i):
        cols = pl.ds(pl.multiple_of(i * tile, tile), tile)
        grad = nt(g[...], weight[cols, :]) * slope[:, cols]
        low[:, cols] = grad.astype(BF16)
        there = pl.ds(pl.multiple_of(first + i * tile, tile), tile)
        bias_grad[:, there] = jnp.sum(grad, axis=0, keepdims=True)


def second_back_body(count, own, g, vec, normed, inverse, *refs):
    received, (hidden_grad, low, sums) = refs[:count], refs[count:]
    total = summed(own, received)
    upstream = g[...].astype(F32)
    grad = upstream + norm_back(total, normed[...], inverse[:, 0:1], vec[3:4, :])
    hidden_grad[...] = grad
    low[...] = grad.astype(BF16)
    for i, values in enumerate((grad, total * normed[...], total, upstream)):
        sums[i : i + 1, :] = jnp.sum(values, axis=0, keepdims=True)


def attend_back_body(side_at, chunk_count, table, q, k, v, probs, *refs):
    chunks, refs = refs[:chunk_count], refs[chunk_count:]
    pieces, refs = refs[:2], refs[2:]
    (low, q_low, k_low, v_low, bias_grad, own, mate, *sends) = refs[:-5]
    out_weight, in_weight, mixed_grad, out_sems, in_sems = refs[-5:]
    copies = column_copies(table, pieces, out_weight, out_sems)
    for copy in copies:
        copy.start()
    size = pieces[0].shape[2]
    ins = [
        pltpu.make_async_copy(
            piece.at[pl.ds(0, 3)], in_weight.at[:, place(table, p, size)], in_sems.at[p]
        )
        for p, piece in enumerate(blocks_of(pieces))
    ]
    for copy in ins:
        copy.start()
    rows = chunks[0].shape[0]
    for j, chunk in enumerate(chunks):
        low[j * rows : (j + 1) * rows, :] = chunk[...]
    bias_grad[...] = jnp.zeros(bias_grad.shape, F32)
    for copy in copies:
        copy.wait()
    columns = q.shape[1]
    tile = min(TILE, columns)
    for start in range(0, columns, tile):
        cols = slice(start, start + tile)
        mixed_grad[:, cols] = nt(low[...], out_weight[cols, :]).astype(BF16)
    heads = columns // DH
    length = probs.shape[1]
    first = table[side_at] * columns
    for h in range(heads):
        cols = slice(h * DH, (h + 1) * DH)
        q_sum = v_sum = 0.0
        for s in range(2):
            rows = slice(s * length, (s + 1) * length)
            prob, down = probs[s * heads + h], mixed_grad[rows, cols]
            prob_grad = nt(down, v[rows, cols])
            inner = jnp.sum(prob * prob_grad, axis=-1, keepdims=True)
            score_low = (prob * (prob_grad - inner) * SCALE).astype(BF16)
            query_grad = nn(score_low, k[rows, cols])
            q_low[rows, cols] = query_grad.astype(BF16)
            q_sum = q_sum + jnp.sum(query_grad, axis=0, keepdims=True)
            k_low[rows, cols] = tn(score_low, q[rows, cols]).astype(BF16)
            value_grad = tn(prob.astype(BF16), down)
            v_low[rows, cols] = value_grad.astype(BF16)
            v_sum = v_sum + jnp.sum(value_grad, axis=0, keepdims=True)
        there = pl.multiple_of(first + h * DH, DH)
        bias_grad[:, pl.ds(there, DH)] = q_sum
        bias_grad[:, pl.ds(pl.multiple_of(there + 2 * columns, DH), DH)] = v_sum
    chips = pieces[0].shape[0]
    for j in range(chips):
        ins[j].wait()
        ins[chips + j].wait()
        cols = slice(2 * j * size, 2 * (j + 1) * size)
        total = nt(q_low[...], in_weight[0, cols, :])
        total = total + nt(k_low[...], in_weight[1, cols, :])
        total = total + nt(v_low[...], in_weight[2, cols, :])
        put_chunks(total, cols, own, mate, sends)


def first_back_body(count, own, x, vec, hidden_grad, *refs):
    received, (result, sums) = refs[:count], refs[count:]
    total = summed(own, received)
    normed, inverse = center_of(x[...].astype(F32))
    grad = hidden_grad[...] + norm_back(total, normed, inverse, vec[0:1, :])
    result[...] = grad.astype(BF16)
    for i, values in enumerate((total * normed, total)):
        sums[i : i + 1, :] = jnp.sum(values, axis=0, keepdims=True)


def output_body(count, own, hidden, vec, *refs):
    received, (result,) = refs[:count], refs[count:]
    total = summed(own, received)
    result[...] = (hidden[...] + total + vec[5:6, :]).astype(BF16)


def assemble_body(dp, tensor, table, *refs):
    chunks, (result,) = refs[:tensor], refs[tensor:]
    rows = chunks[0].shape[0]
    for k, chunk in enumerate(chunks):
        result[place(table, dp + k, rows), :] = chunk[...]


def grad_blocks(table, left, right, by_rows, first, chips, size, put):
    if by_rows:
        width = right[0].shape[1]
        tile = min(TILE, width)
        for block in range(chips):
            turned = left[:, place(table, first + block, size)].T
            for j, ref in enumerate(right):
                for c in range(0, width, tile):
                    put(block, 0, j * width + c, nn(turned, ref[:, c : c + tile]))
    else:
        hidden = left.shape[1]
        step = min(512, hidden)
        for r in range(0, hidden, step):
            turned = left[:, r : r + step].T
            for block in range(chips):
                put(block, r, 0, nn(turned, right[0][:, place(table, first + block, size)]))


def grad_body(by_rows, first, chips, size, count, table, left, *refs):
    right, theirs, out = refs[:count], refs[count:-1], refs[-1]

    def put(block, low, column, value):
        rows, cols = slice(low, low + value.shape[0]), slice(column, column + value.shape[1])
        for ref in theirs:
            value = value + ref[block, rows, cols].astype(F32)
        out[block, rows, cols] = value.astype(BF16)

    grad_blocks(table, left, right, by_rows, first, chips, size, put)


def finish_body(by_rows, planes, first, cols, blocks, out):
    chips, rows, _ = blocks.shape
    here = slice(first, first + cols)
    for half in range(2):
        total = blocks[half, :, here].astype(F32)
        for j in range(half + 2, chips, 2):
            total = total + blocks[j, :, here].astype(F32)
        if not by_rows:
            out[half * rows : (half + 1) * rows, :] = total
        elif planes == 1:
            out[:, half * cols : (half + 1) * cols] = total
        else:
            width = cols // planes
            for j in range(planes):
                out[j, :, half * width : (half + 1) * width] = total[:, j * width : (j + 1) * width]


def sems(*dims):
    return pltpu.SemaphoreType.DMA(tuple(dims))


class Layer:
    def __init__(self, at, length, features):
        self.at, self.table = at, at.table()
        self.length, self.features = length, features
        self.own = length // at.tensor
        self.side_at = at.dp + at.tensor

    def chunk_outs(self):
        sends = [shape((self.own, self.features), BF16)] * (2 * self.at.tensor - 2)
        return [shape((self.own, self.features), F32)] * 2 + sends

    def collect(self, name, own, vec, chunks, norm):
        at = self.at
        return call(
            functools.partial(collect_body, at.dp, at.tensor, norm),
            name,
            [SMEM] + [VMEM] * (2 + at.tensor),
            [shape((2 * self.length, self.features), BF16)],
            [],
            20 * self.length * self.features,
            [self.table, own, vec] + chunks,
        )[0]

    def project(self, name, left, blocks, by_rows):
        inner = left.shape[1]
        weight = (self.features, inner) if by_rows else (inner, self.features)
        return call(
            functools.partial(project_body, by_rows),
            name,
            [SMEM, VMEM] + [ANY] * 2,
            self.chunk_outs(),
            [pltpu.VMEM(weight, BF16), sems(self.at.dp)],
            4 * self.length * inner * self.features,
            [self.table, left] + blocks,
        )

    def fold(self, name, mate, received):
        return call(
            fold_body,
            name,
            [VMEM] * (1 + len(received)),
            [shape(mate.shape, BF16)],
            [],
            mate.size * 4,
            [mate] + received,
        )[0]

    def trade_mate(self, part):
        return self.at.to_peers(part[1 + self.at.tensor :])

    def trade_own(self, part):
        return self.at.to_peers(part[2 : 1 + self.at.tensor])

    def reduce(self, name, part):
        for_mate, own = self.trade_mate(part), self.trade_own(part)
        folded = self.fold(name + "_fold", part[1], for_mate)
        return own + [self.at.to_mate(folded)], folded

    def block_shape(self, left, right, by_rows):
        size = self.features // self.at.dp
        if by_rows:
            return size, (size, sum(r.shape[1] for r in right))
        return size, (left.shape[1], size)

    def grad(self, name, left, right, by_rows, *theirs):
        chips = self.at.chips
        size, block = self.block_shape(left, right, by_rows)
        return call(
            functools.partial(grad_body, by_rows, 0 if theirs else chips, chips, size, len(right)),
            name + ("_near" if theirs else "_far"),
            [SMEM] + [VMEM] * (1 + len(right) + len(theirs)),
            [shape((chips,) + block, BF16)],
            [],
            4 * self.length * chips * block[0] * block[1],
            [self.table, left] + list(right) + list(theirs),
        )[0]

    def grad_far(self, name, left, right, by_rows):
        return self.grad(name, left, right, by_rows)

    def grad_near(self, name, left, right, by_rows, theirs):
        return self.grad(name, left, right, by_rows, theirs)

    def grad_attention(self, first_low, mixed, lows, hidden_low, *theirs):
        chips, size = self.at.chips, self.features // self.at.dp
        width, heads = len(lows) * lows[0].shape[1], mixed.shape[1]
        first = 0 if theirs else chips

        def body(table, left, other, *refs):
            right, low, got, out = refs[:3], refs[3], refs[4:-1], refs[-1]

            def put_at(start):
                def put(block, row, column, value):
                    rows = slice(row, row + value.shape[0])
                    cols = slice(start + column, start + column + value.shape[1])
                    for ref in got:
                        value = value + ref[block, rows, cols].astype(F32)
                    out[block, rows, cols] = value.astype(BF16)

                return put

            grad_blocks(table, left, right, True, first, chips, size, put_at(0))
            grad_blocks(table, other, [low], False, first, chips, size, put_at(width))

        args = [self.table, first_low, mixed] + list(lows) + [hidden_low] + list(theirs)
        return call(
            body,
            "grad_attention_near" if theirs else "grad_attention_far",
            [SMEM] + [VMEM] * (len(args) - 1),
            [shape((chips, heads, width + size), BF16)],
            [],
            4 * self.length * chips * size * (width + heads),
            args,
        )[0]

    def grad_finish(self, name, blocks, by_rows):
        _, rows, cols = blocks.shape
        return call(
            functools.partial(finish_body, by_rows, 1, 0, cols),
            name + "_finish",
            [VMEM],
            [shape((rows, 2 * cols) if by_rows else (2 * rows, cols), F32)],
            [],
            blocks.size,
            [blocks],
        )[0]

    def attention_finish(self, blocks, width, planes):
        _, rows, cols = blocks.shape

        def body(ref, grad_in, grad_out):
            finish_body(True, planes, 0, width, ref, grad_in)
            finish_body(False, 1, width, cols - width, ref, grad_out)

        return call(
            body,
            "attention_finish",
            [VMEM],
            [shape((planes, rows, 2 * width // planes), F32), shape((2 * rows, cols - width), F32)],
            [],
            blocks.size,
            [blocks],
        )


def shards(
    dp,
    tensor,
    inputs,
    segment_ids,
    first_gain,
    first_shift,
    project_in,
    query_bias,
    value_bias,
    project_out,
    out_bias,
    second_gain,
    second_shift,
    up_weight,
    up_bias,
    down_weight,
    down_bias,
    cotangent,
):
    at = Places(dp, tensor)
    length, features = inputs.shape
    layer = Layer(at, length, features)
    own, table, side_at = layer.own, layer.table, layer.side_at
    heads, hidden_units = query_bias.shape[0] // 2, up_bias.shape[0] // 2
    both = 2 * length
    chunk_count = 2 * tensor
    chunk32, chunk16 = shape((own, features), F32), shape((own, features), BF16)
    tokens16 = shape((both, features), BF16)

    x_own, g_own = at.chunk_of(inputs), at.chunk_of(cotangent)
    mate = at.to_mate(jnp.concatenate([x_own, g_own]))
    ids = at.tokens_in(segment_ids)
    mate_ids = at.to_mate(ids)
    blocks = [at.halves(project_in, 2), at.halves(project_out, 0)[:, None]]
    mine_in = at.exchange(after(jnp.concatenate(blocks, 1), mate, mate_ids))
    mate_chunks = [mate] + at.to_peers(mate)
    up_blocks, down_blocks = at.halves(up_weight, 1), at.halves(down_weight, 0)
    mate_chunks = after(mate_chunks, up_blocks, down_blocks)
    vec = jnp.stack(
        [
            first_gain,
            first_shift,
            out_bias,
            second_gain,
            second_shift,
            down_bias,
            down_bias,
            down_bias,
        ]
    ).astype(F32)
    biases = [at.half_of(b)[None] for b in (query_bias, value_bias, up_bias)]
    order = at.tokens_in(jnp.arange(length, dtype=jnp.int32))
    ids = jnp.stack([ids, mate_ids])
    allowed = (
        (ids[:, :, None] == ids[:, None, :])
        & (ids[:, :, None] != 0)
        & (order[None, None, :] <= order[None, :, None])
    )
    allowed = (allowed | (order[None, None, :] == order[None, :, None])).astype(F32)
    first_low = layer.collect("first_norm", inputs, vec, mate_chunks, True)
    g = layer.collect("upstream", cotangent, vec, mate_chunks, False)
    mine_in = after(mine_in, first_low, allowed, biases, g)
    mine_up = at.exchange(after(up_blocks, mine_in))

    all_in = at.both_cores(mine_in)
    low_heads = shape((both, heads), BF16)
    query, key, value, probs, mixed = call(
        attend_body,
        "attend",
        [SMEM] + [VMEM] * 4 + [ANY] * 2,
        [low_heads] * 3 + [shape((2 * heads // DH, length, length), F32), low_heads],
        [pltpu.VMEM((3, features, heads), BF16), sems(3, dp)],
        12 * length * heads * features,
        [table, first_low, biases[0], biases[1], allowed] + all_in,
    )
    part = layer.project("project_out", mixed, all_in, False)
    received, _ = layer.reduce("project_out", part)
    hidden, normed_two, inverse_two, second_own = call(
        functools.partial(second_body, len(received)),
        "second_norm",
        [VMEM] * (3 + len(received)),
        [chunk32, chunk32, shape((own, 128), F32), chunk16],
        [],
        20 * own * features,
        [part[0], x_own, vec] + received,
    )
    second_chunks = at.spread(second_own)
    mine_up = after(mine_up, second_chunks[tensor])
    mine_down = at.exchange(after(down_blocks, mine_up))
    all_up = at.both_cores(mine_up)
    second_low, activated, slope = call(
        functools.partial(upper_body, chunk_count),
        "upper",
        [SMEM] + [VMEM] * (1 + chunk_count) + [ANY] * 2,
        [tokens16, shape((both, hidden_units), BF16), shape((both, hidden_units), F32)],
        [pltpu.VMEM((features, hidden_units), BF16), sems(dp)],
        4 * length * features * hidden_units,
        [table, biases[2]] + second_chunks + all_up,
    )
    far_down = layer.grad_far("grad_down", activated, [g], False)
    near_down = layer.grad_near("grad_down", activated, [g], False, at.to_core(far_down))
    mine_down = after(mine_down, near_down)
    ring_down = at.exchange(after(near_down, mine_down))
    all_down = at.both_cores(mine_down)
    upper_low, up_bias_grad = call(
        functools.partial(upper_grad_body, side_at),
        "upper_grad",
        [SMEM] + [VMEM] * 2 + [ANY] * 2,
        [shape((both, hidden_units), BF16), shape((1, 2 * hidden_units), F32)],
        [pltpu.VMEM((hidden_units, features), BF16), sems(dp)],
        4 * length * features * hidden_units,
        [table, g, slope] + all_down,
    )
    far_up = layer.grad_far("grad_up", second_low, [upper_low], True)
    part = layer.project("second_part", after(upper_low, far_up), all_up, True)
    for_mate = layer.trade_mate(part)
    near_up = layer.grad_near(
        "grad_up", second_low, after([upper_low], part), True, at.to_core(far_up)
    )
    folded = layer.fold("second_part_fold", part[1], for_mate)
    received = layer.trade_own(after(part, near_up)) + [at.to_mate(folded)]
    hidden_grad, hidden_low_own, sums_two = call(
        functools.partial(second_back_body, len(received)),
        "second_back",
        [VMEM] * (5 + len(received)),
        [chunk32, chunk16, shape((8, features), F32)],
        [],
        20 * own * features,
        [after(part[0], ring_down), g_own, vec, normed_two, inverse_two] + received,
    )
    hidden_chunks = at.spread(hidden_low_own)
    ring_up = at.exchange(after(near_up, hidden_chunks[tensor]))
    feed = layer.project("feed", after(activated, hidden_low_own), all_down, False)
    back = call(
        functools.partial(attend_back_body, side_at, chunk_count),
        "attend_back",
        [SMEM] + [VMEM] * (4 + chunk_count) + [ANY] * 2,
        [tokens16, low_heads, low_heads, low_heads, shape((1, 4 * heads), F32)]
        + layer.chunk_outs(),
        [
            pltpu.VMEM((heads, features), BF16),
            pltpu.VMEM((3, features, heads), BF16),
            pltpu.VMEM((both, heads), BF16),
            sems(dp),
            sems(dp),
        ],
        16 * length * heads * features,
        [table, after(query, feed), key, value, probs]
        + hidden_chunks
        + all_in,
    )
    hidden_low, q_low, k_low, v_low, heads_grad, *part = back
    lows = [q_low, k_low, v_low]
    for_mate = layer.trade_mate(part)
    far = layer.grad_attention(first_low, mixed, lows, hidden_low)
    feed_for_mate = layer.trade_mate(after(feed, far))
    folded = layer.fold("first_part_fold", part[1], for_mate)
    from_mate = at.to_mate(folded)
    near = layer.grad_attention(first_low, mixed, after(lows, folded), hidden_low, at.to_core(far))
    received = layer.trade_own(after(part, feed_for_mate[0])) + [from_mate]
    feed_folded = layer.fold("feed_fold", after(feed[1], near), feed_for_mate)
    feed_from_mate = at.to_mate(feed_folded)
    ring_in = at.exchange(after(near, ring_up, from_mate, feed_from_mate))
    grad_down = layer.grad_finish("grad_down", ring_down, False)
    grad_up = layer.grad_finish("grad_up", ring_up, True)
    input_own, sums_one = call(
        functools.partial(first_back_body, len(received)),
        "first_back",
        [VMEM] * (4 + len(received)),
        [chunk16, shape((8, features), F32)],
        [],
        20 * own * features,
        [after(part[0], grad_up, grad_down), x_own, vec, hidden_grad] + received,
    )
    def assemble(name, chunk, others):
        return call(
            functools.partial(assemble_body, dp, tensor),
            name,
            [SMEM] + [VMEM] * tensor,
            [shape((length, features), BF16)],
            [],
            length * features,
            [table, chunk] + others,
        )[0]

    input_others = at.to_peers(input_own)
    input_gradient = assemble("input_gradient", input_own, input_others)
    feed_received = layer.trade_own(after(feed, received[0])) + [feed_from_mate]
    outputs_own = call(
        functools.partial(output_body, len(feed_received)),
        "outputs_own",
        [VMEM] * (3 + len(feed_received)),
        [chunk16],
        [],
        4 * own * features,
        [after(feed[0], input_others), hidden, vec] + feed_received,
    )[0]
    output_others = at.to_peers(outputs_own)
    outputs = assemble("outputs", outputs_own, output_others)
    grad_in, grad_out = layer.attention_finish(ring_in, 3 * heads, 3)

    narrow = jnp.concatenate([heads_grad[0], up_bias_grad[0]])
    rows = -(-narrow.shape[0] // features)
    narrow = jnp.pad(narrow, (0, rows * features - narrow.shape[0])).reshape(rows, features)
    sums = at.sum_small(after(jnp.concatenate([sums_one[:2], sums_two[:4]]), input_others), narrow)
    narrow = sums[6:].reshape(-1)
    heads, hidden_units = 2 * heads, 2 * hidden_units
    return (
        outputs,
        input_gradient,
        sums[0],
        sums[1],
        grad_in,
        narrow[:heads],
        narrow[heads : 2 * heads],
        grad_out,
        sums[2],
        sums[3],
        sums[4],
        grad_up,
        narrow[2 * heads : 2 * heads + hidden_units],
        grad_down,
        sums[5],
    )


def solution(mesh):
    dp, tensor = mesh.shape["dp"], mesh.shape["tensor"]

    def program(*arguments):
        return shards(dp, tensor, *arguments)

    in_specs = (
        P("dp", None),
        P("dp"),
        P(),
        P(),
        P(None, "dp", "tensor"),
        P("tensor"),
        P("tensor"),
        P("tensor", "dp"),
        P(),
        P(),
        P(),
        P("dp", "tensor"),
        P("tensor"),
        P("tensor", "dp"),
        P(),
        P("dp", None),
    )
    out_specs = (
        P("dp", None),
        P("dp", None),
        P(),
        P(),
        P(None, "dp", "tensor"),
        P("tensor"),
        P("tensor"),
        P("tensor", "dp"),
        P(),
        P(),
        P(),
        P("dp", "tensor"),
        P("tensor"),
        P("tensor", "dp"),
        P(),
    )
    return jax.shard_map(program, mesh=mesh, in_specs=in_specs, out_specs=out_specs, check_vma=False)
```

```python
import functools

import jax
import jax.numpy as jnp
from jax import lax
from jax.experimental import pallas as pl
from jax.experimental.pallas import tpu as pltpu
from jax.sharding import PartitionSpec as P

DH = 128
EPSILON = 1e-05
NEGATIVE = -1e30
SCALE = DH ** (-0.5)
F32 = jnp.float32
BF16 = jnp.bfloat16
TILE = 512
ANY = pl.BlockSpec(memory_space=pl.ANY)
VMEM = pl.BlockSpec(memory_space=pltpu.VMEM)
SMEM = pl.BlockSpec(memory_space=pltpu.SMEM)


def nn(left, right):
    return lax.dot_general(left, right, (((1,), (0,)), ((), ())), preferred_element_type=F32)


def nt(left, right):
    return lax.dot_general(left, right, (((1,), (1,)), ((), ())), preferred_element_type=F32)


def tn(left, right):
    return lax.dot_general(left, right, (((0,), (0,)), ((), ())), preferred_element_type=F32)


def shape(dims, dtype):
    return jax.ShapeDtypeStruct(tuple(dims), dtype)


def call(body, name, in_specs, outs, scratch, flops, args):
    moved = sum(a.size * a.dtype.itemsize for a in args)
    moved += sum(o.size * o.dtype.itemsize for o in outs)
    return pl.pallas_call(
        body,
        name=name,
        out_shape=outs,
        in_specs=in_specs,
        out_specs=[VMEM] * len(outs),
        scratch_shapes=scratch,
        cost_estimate=pl.CostEstimate(flops=flops, bytes_accessed=moved, transcendentals=0),
    )(*args)


class Places:
    def __init__(self, dp, tensor):
        self.dp, self.tensor, self.chips = dp, tensor, dp // 2
        self.rank = lax.axis_index("dp")
        self.part = lax.axis_index("tensor")
        self.chip, self.core = self.rank // 2, self.rank % 2
        self.side = self.chip % 2
        self.swap = [(i, i ^ 1) for i in range(dp)]

    def table(self):
        owners = jnp.arange(self.chips, dtype=jnp.int32) * 2
        chunks = self.part ^ jnp.arange(self.tensor, dtype=jnp.int32)
        return jnp.concatenate(
            [owners + self.core, owners + (1 - self.core), chunks, self.side[None]]
        ).astype(jnp.int32)

    def tokens_in(self, values):
        size = values.shape[0] // self.tensor
        return jnp.take(
            values.reshape(self.tensor, size),
            self.part ^ jnp.arange(self.tensor, dtype=jnp.int32),
            axis=0,
        ).reshape(-1)

    def chunk_of(self, values):
        size = values.shape[0] // self.tensor
        return lax.dynamic_slice_in_dim(values, self.part * size, size, 0)

    def half_of(self, values):
        size = values.shape[0] // 2
        return lax.dynamic_slice_in_dim(values, self.side * size, size, 0)

    def to_core(self, values):
        return lax.ppermute(values, "dp", self.swap)

    def to_chip(self, values, k):
        return lax.ppermute(values, "dp", [(i, i ^ (2 * k)) for i in range(self.dp)])

    def to_mate(self, values):
        return self.to_chip(values, 1)

    def to_peer(self, values, k):
        return lax.ppermute(values, "tensor", [(i, i ^ k) for i in range(self.tensor)])

    def to_peers(self, values):
        many = isinstance(values, (list, tuple))
        return [
            self.to_peer(values[k - 1] if many else values, k)
            for k in range(self.tensor - 1, 0, -1)
        ][::-1]

    def exchange(self, blocks):
        groups = [[2 * j + core for j in range(self.chips)] for core in range(2)]
        return lax.all_to_all(blocks, "dp", 0, 0, axis_index_groups=groups, tiled=True)

    def halves(self, block, axis):
        halves = jnp.split(block, 2, axis)
        return jnp.stack([halves[j % 2] for j in range(self.chips)])

    def both_cores(self, blocks):
        return [blocks, self.to_core(blocks)]

    def spread(self, chunk):
        own = self.to_peers(chunk)
        mate = after(self.to_mate(chunk), own[:-1])
        return [chunk] + own + [mate] + self.to_peers(mate)

    def sum_small(self, wide, narrow):
        step = 1
        while step < self.tensor:
            wide = wide + self.to_peer(wide, step)
            step *= 2
        values = jnp.concatenate([wide, narrow])
        values = values + self.to_core(values)
        step = 1
        while step < self.chips:
            values = values + self.to_chip(values, step)
            step *= 2
        return values


def after(values, *events):
    values, _ = lax.optimization_barrier((values, events))
    return values


def center_of(values):
    center = values - jnp.mean(values, axis=-1, keepdims=True)
    inverse = lax.rsqrt(jnp.mean(center * center, axis=-1, keepdims=True) + EPSILON)
    return center * inverse, inverse


def norm_back(norm_grad, normed, inverse, gain):
    scaled = norm_grad * gain
    return inverse * (
        scaled
        - jnp.mean(scaled, axis=-1, keepdims=True)
        - normed * jnp.mean(scaled * normed, axis=-1, keepdims=True)
    )


def place(table, p, size):
    return pl.ds(pl.multiple_of(table[p] * size, size), size)


def collect_body(dp, tensor, norm, table, own, vec, *refs):
    chunks, (out,) = refs[:tensor], refs[tensor:]
    rows = chunks[0].shape[0] // 2
    first = 0 if norm else rows
    for s in range(2):
        for k in range(tensor):
            value = own[place(table, dp + k, rows), :] if s == 0 else chunks[k][first : first + rows, :]
            if norm:
                normed, _ = center_of(value.astype(F32))
                value = (normed * vec[0:1, :] + vec[1:2, :]).astype(BF16)
            start = (s * tensor + k) * rows
            out[start : start + rows, :] = value


def blocks_of(arrays):
    return [ref.at[j] for ref in arrays for j in range(ref.shape[0])]


def attend_body(table, x, q_bias, v_bias, allowed, *refs):
    pieces, (q, k, v, probs, mixed), (weight, sems) = blocks_of(refs[:2]), refs[2:-2], refs[-2:]
    count, size = len(pieces), refs[0].shape[2]

    def copy(j, p):
        return pltpu.make_async_copy(
            pieces[p].at[j], weight.at[j, place(table, p, size)], sems.at[j, p]
        )

    for j in range(3):
        for p in range(count):
            copy(j, p).start()
    columns = q.shape[1]
    tile = min(TILE, columns)
    for j, out in enumerate((q, k, v)):
        for p in range(count):
            copy(j, p).wait()
        for start in range(0, columns, tile):
            cols = slice(start, start + tile)
            total = nn(x[...], weight[j, :, cols])
            if j == 0:
                total = total + q_bias[:, cols].astype(F32)
            if j == 2:
                total = total + v_bias[:, cols].astype(F32)
            out[:, cols] = total.astype(BF16)
    heads = columns // DH
    length = allowed.shape[1]
    for s in range(2):
        rows = slice(s * length, (s + 1) * length)
        for h in range(heads):
            cols = slice(h * DH, (h + 1) * DH)
            scores = nt(q[rows, cols], k[rows, cols]) * SCALE
            scores = jnp.where(allowed[s] > 0, scores, NEGATIVE)
            weights = jnp.exp(scores - jnp.max(scores, axis=-1, keepdims=True))
            prob = weights / jnp.sum(weights, axis=-1, keepdims=True)
            probs[s * heads + h] = prob
            mixed[rows, cols] = nn(prob.astype(BF16), v[rows, cols]).astype(BF16)


def put_chunks(total, cols, own, mate, sends):
    rows = own.shape[0]
    length = total.shape[0] // 2
    chunks = length // rows
    own[:, cols] = total[:rows]
    mate[:, cols] = total[length : length + rows]
    for k in range(1, chunks):
        for s in range(2):
            part = total[s * length + k * rows : s * length + (k + 1) * rows].astype(BF16)
            sends[s * (chunks - 1) + k - 1][:, cols] = part


def column_copies(table, arrays, weight, sems):
    width = arrays[0].shape[-1]
    blocks = blocks_of(arrays)
    if len(arrays[0].shape) == 4:
        blocks = [block.at[3] for block in blocks]
    return [
        pltpu.make_async_copy(block, weight.at[:, place(table, p, width)], sems.at[p])
        for p, block in enumerate(blocks)
    ]


def row_copies(table, arrays, weight, sems):
    size = arrays[0].shape[1]
    return [
        pltpu.make_async_copy(piece, weight.at[place(table, p, size)], sems.at[p])
        for p, piece in enumerate(blocks_of(arrays))
    ]


def project_body(by_rows, table, left, *refs):
    pieces, (own, mate, *sends), (weight, sems) = refs[:2], refs[2:-2], refs[-2:]
    copies = (row_copies if by_rows else column_copies)(table, pieces, weight, sems)
    for copy in copies:
        copy.start()
    size = pieces[0].shape[1 if by_rows else -1]
    chips = pieces[0].shape[0]
    for j in range(chips):
        copies[j].wait()
        copies[chips + j].wait()
        cols = slice(2 * j * size, 2 * (j + 1) * size)
        if by_rows:
            total = nt(left[...], weight[cols, :])
        else:
            total = nn(left[...], weight[:, cols])
        put_chunks(total, cols, own, mate, sends)


def fold_body(mate, *refs):
    refs[-1][...] = summed(mate, refs[:-1]).astype(BF16)


def summed(own, received):
    total = own[...]
    for ref in received:
        total = total + ref[...].astype(F32)
    return total


def second_body(count, own, x, vec, *refs):
    received, (hidden, normed_out, inverse_out, low) = refs[:count], refs[count:]
    value = x[...].astype(F32) + summed(own, received) + vec[2:3, :]
    hidden[...] = value
    normed, inverse = center_of(value)
    normed_out[...] = normed
    inverse_out[...] = jnp.broadcast_to(inverse, inverse_out.shape)
    low[...] = (normed * vec[3:4, :] + vec[4:5, :]).astype(BF16)


def upper_body(chunk_count, table, bias, *refs):
    chunks, refs = refs[:chunk_count], refs[chunk_count:]
    pieces, (low, activated, slope), (weight, sems) = refs[:2], refs[2:-2], refs[-2:]
    copies = row_copies(table, pieces, weight, sems)
    for copy in copies:
        copy.start()
    rows = chunks[0].shape[0]
    for k, chunk in enumerate(chunks):
        low[k * rows : (k + 1) * rows, :] = chunk[...]
    for copy in copies:
        copy.wait()
    columns = weight.shape[1]
    tile = min(TILE, columns)

    @pl.loop(0, columns // tile)
    def _(i):
        cols = pl.ds(pl.multiple_of(i * tile, tile), tile)
        value = nn(low[...], weight[:, cols]) + bias[:, cols].astype(F32)
        below = 0.5 * (1.0 + lax.erf(value * (0.5**0.5)))
        activated[:, cols] = (value * below).astype(BF16)
        density = jnp.exp(-0.5 * value * value) * 0.3989422804014327
        slope[:, cols] = below + value * density


def upper_grad_body(side_at, table, g, slope, *refs):
    pieces, (low, bias_grad), (weight, sems) = refs[:2], refs[2:-2], refs[-2:]
    copies = column_copies(table, pieces, weight, sems)
    for copy in copies:
        copy.start()
    bias_grad[...] = jnp.zeros(bias_grad.shape, F32)
    for copy in copies:
        copy.wait()
    hidden = weight.shape[0]
    tile = min(TILE, hidden)
    first = table[side_at] * hidden

    @pl.loop(0, hidden // tile)
    def _(i):
        cols = pl.ds(pl.multiple_of(i * tile, tile), tile)
        grad = nt(g[...], weight[cols, :]) * slope[:, cols]
        low[:, cols] = grad.astype(BF16)
        there = pl.ds(pl.multiple_of(first + i * tile, tile), tile)
        bias_grad[:, there] = jnp.sum(grad, axis=0, keepdims=True)


def second_back_body(count, own, g, vec, normed, inverse, *refs):
    received, (hidden_grad, low, sums) = refs[:count], refs[count:]
    total = summed(own, received)
    upstream = g[...].astype(F32)
    grad = upstream + norm_back(total, normed[...], inverse[:, 0:1], vec[3:4, :])
    hidden_grad[...] = grad
    low[...] = grad.astype(BF16)
    for i, values in enumerate((grad, total * normed[...], total, upstream)):
        sums[i : i + 1, :] = jnp.sum(values, axis=0, keepdims=True)


def attend_back_body(side_at, chunk_count, table, q, k, v, probs, *refs):
    chunks, refs = refs[:chunk_count], refs[chunk_count:]
    pieces, refs = refs[:2], refs[2:]
    (low, q_low, k_low, v_low, bias_grad, own, mate, *sends) = refs[:-5]
    out_weight, in_weight, mixed_grad, out_sems, in_sems = refs[-5:]
    copies = column_copies(table, pieces, out_weight, out_sems)
    for copy in copies:
        copy.start()
    size = pieces[0].shape[2]
    ins = [
        pltpu.make_async_copy(
            piece.at[pl.ds(0, 3)], in_weight.at[:, place(table, p, size)], in_sems.at[p]
        )
        for p, piece in enumerate(blocks_of(pieces))
    ]
    for copy in ins:
        copy.start()
    rows = chunks[0].shape[0]
    for j, chunk in enumerate(chunks):
        low[j * rows : (j + 1) * rows, :] = chunk[...]
    bias_grad[...] = jnp.zeros(bias_grad.shape, F32)
    for copy in copies:
        copy.wait()
    columns = q.shape[1]
    tile = min(TILE, columns)
    for start in range(0, columns, tile):
        cols = slice(start, start + tile)
        mixed_grad[:, cols] = nt(low[...], out_weight[cols, :]).astype(BF16)
    heads = columns // DH
    length = probs.shape[1]
    first = table[side_at] * columns
    for h in range(heads):
        cols = slice(h * DH, (h + 1) * DH)
        q_sum = v_sum = 0.0
        for s in range(2):
            rows = slice(s * length, (s + 1) * length)
            prob, down = probs[s * heads + h], mixed_grad[rows, cols]
            prob_grad = nt(down, v[rows, cols])
            inner = jnp.sum(prob * prob_grad, axis=-1, keepdims=True)
            score_low = (prob * (prob_grad - inner) * SCALE).astype(BF16)
            query_grad = nn(score_low, k[rows, cols])
            q_low[rows, cols] = query_grad.astype(BF16)
            q_sum = q_sum + jnp.sum(query_grad, axis=0, keepdims=True)
            k_low[rows, cols] = tn(score_low, q[rows, cols]).astype(BF16)
            value_grad = tn(prob.astype(BF16), down)
            v_low[rows, cols] = value_grad.astype(BF16)
            v_sum = v_sum + jnp.sum(value_grad, axis=0, keepdims=True)
        there = pl.multiple_of(first + h * DH, DH)
        bias_grad[:, pl.ds(there, DH)] = q_sum
        bias_grad[:, pl.ds(pl.multiple_of(there + 2 * columns, DH), DH)] = v_sum
    chips = pieces[0].shape[0]
    for j in range(chips):
        ins[j].wait()
        ins[chips + j].wait()
        cols = slice(2 * j * size, 2 * (j + 1) * size)
        total = nt(q_low[...], in_weight[0, cols, :])
        total = total + nt(k_low[...], in_weight[1, cols, :])
        total = total + nt(v_low[...], in_weight[2, cols, :])
        put_chunks(total, cols, own, mate, sends)


def first_back_body(count, own, x, vec, hidden_grad, *refs):
    received, (result, sums) = refs[:count], refs[count:]
    total = summed(own, received)
    normed, inverse = center_of(x[...].astype(F32))
    grad = hidden_grad[...] + norm_back(total, normed, inverse, vec[0:1, :])
    result[...] = grad.astype(BF16)
    for i, values in enumerate((total * normed, total)):
        sums[i : i + 1, :] = jnp.sum(values, axis=0, keepdims=True)


def output_body(count, own, hidden, vec, *refs):
    received, (result,) = refs[:count], refs[count:]
    total = summed(own, received)
    result[...] = (hidden[...] + total + vec[5:6, :]).astype(BF16)


def assemble_body(dp, tensor, table, *refs):
    chunks, (result,) = refs[:tensor], refs[tensor:]
    rows = chunks[0].shape[0]
    for k, chunk in enumerate(chunks):
        result[place(table, dp + k, rows), :] = chunk[...]


def grad_blocks(table, left, right, by_rows, first, chips, size, put):
    if by_rows:
        width = right[0].shape[1]
        tile = min(TILE, width)
        for block in range(chips):
            turned = left[:, place(table, first + block, size)].T
            for j, ref in enumerate(right):
                for c in range(0, width, tile):
                    put(block, 0, j * width + c, nn(turned, ref[:, c : c + tile]))
    else:
        hidden = left.shape[1]
        step = min(512, hidden)
        for r in range(0, hidden, step):
            turned = left[:, r : r + step].T
            for block in range(chips):
                put(block, r, 0, nn(turned, right[0][:, place(table, first + block, size)]))


def grad_body(by_rows, first, chips, size, count, table, left, *refs):
    right, theirs, out = refs[:count], refs[count:-1], refs[-1]

    def put(block, low, column, value):
        rows, cols = slice(low, low + value.shape[0]), slice(column, column + value.shape[1])
        for ref in theirs:
            value = value + ref[block, rows, cols].astype(F32)
        out[block, rows, cols] = value.astype(BF16)

    grad_blocks(table, left, right, by_rows, first, chips, size, put)


def finish_body(by_rows, planes, first, cols, blocks, out):
    chips, rows, _ = blocks.shape
    here = slice(first, first + cols)
    for half in range(2):
        total = blocks[half, :, here].astype(F32)
        for j in range(half + 2, chips, 2):
            total = total + blocks[j, :, here].astype(F32)
        if not by_rows:
            out[half * rows : (half + 1) * rows, :] = total
        elif planes == 1:
            out[:, half * cols : (half + 1) * cols] = total
        else:
            width = cols // planes
            for j in range(planes):
                out[j, :, half * width : (half + 1) * width] = total[:, j * width : (j + 1) * width]


def sems(*dims):
    return pltpu.SemaphoreType.DMA(tuple(dims))


class Layer:
    def __init__(self, at, length, features):
        self.at, self.table = at, at.table()
        self.length, self.features = length, features
        self.own = length // at.tensor
        self.side_at = at.dp + at.tensor

    def chunk_outs(self):
        sends = [shape((self.own, self.features), BF16)] * (2 * self.at.tensor - 2)
        return [shape((self.own, self.features), F32)] * 2 + sends

    def collect(self, name, own, vec, chunks, norm):
        at = self.at
        return call(
            functools.partial(collect_body, at.dp, at.tensor, norm),
            name,
            [SMEM] + [VMEM] * (2 + at.tensor),
            [shape((2 * self.length, self.features), BF16)],
            [],
            20 * self.length * self.features,
            [self.table, own, vec] + chunks,
        )[0]

    def project(self, name, left, blocks, by_rows):
        inner = left.shape[1]
        weight = (self.features, inner) if by_rows else (inner, self.features)
        return call(
            functools.partial(project_body, by_rows),
            name,
            [SMEM, VMEM] + [ANY] * 2,
            self.chunk_outs(),
            [pltpu.VMEM(weight, BF16), sems(self.at.dp)],
            4 * self.length * inner * self.features,
            [self.table, left] + blocks,
        )

    def fold(self, name, mate, received):
        return call(
            fold_body,
            name,
            [VMEM] * (1 + len(received)),
            [shape(mate.shape, BF16)],
            [],
            mate.size * 4,
            [mate] + received,
        )[0]

    def trade_mate(self, part):
        return self.at.to_peers(part[1 + self.at.tensor :])

    def trade_own(self, part):
        return self.at.to_peers(part[2 : 1 + self.at.tensor])

    def reduce(self, name, part):
        for_mate, own = self.trade_mate(part), self.trade_own(part)
        folded = self.fold(name + "_fold", part[1], for_mate)
        return own + [self.at.to_mate(folded)], folded

    def block_shape(self, left, right, by_rows):
        size = self.features // self.at.dp
        if by_rows:
            return size, (size, sum(r.shape[1] for r in right))
        return size, (left.shape[1], size)

    def grad(self, name, left, right, by_rows, *theirs):
        chips = self.at.chips
        size, block = self.block_shape(left, right, by_rows)
        return call(
            functools.partial(grad_body, by_rows, 0 if theirs else chips, chips, size, len(right)),
            name + ("_near" if theirs else "_far"),
            [SMEM] + [VMEM] * (1 + len(right) + len(theirs)),
            [shape((chips,) + block, BF16)],
            [],
            4 * self.length * chips * block[0] * block[1],
            [self.table, left] + list(right) + list(theirs),
        )[0]

    def grad_far(self, name, left, right, by_rows):
        return self.grad(name, left, right, by_rows)

    def grad_near(self, name, left, right, by_rows, theirs):
        return self.grad(name, left, right, by_rows, theirs)

    def grad_attention(self, first_low, mixed, lows, hidden_low, *theirs):
        chips, size = self.at.chips, self.features // self.at.dp
        width, heads = len(lows) * lows[0].shape[1], mixed.shape[1]
        first = 0 if theirs else chips

        def body(table, left, other, *refs):
            right, low, got, out = refs[:3], refs[3], refs[4:-1], refs[-1]

            def put_at(start):
                def put(block, row, column, value):
                    rows = slice(row, row + value.shape[0])
                    cols = slice(start + column, start + column + value.shape[1])
                    for ref in got:
                        value = value + ref[block, rows, cols].astype(F32)
                    out[block, rows, cols] = value.astype(BF16)

                return put

            grad_blocks(table, left, right, True, first, chips, size, put_at(0))
            grad_blocks(table, other, [low], False, first, chips, size, put_at(width))

        args = [self.table, first_low, mixed] + list(lows) + [hidden_low] + list(theirs)
        return call(
            body,
            "grad_attention_near" if theirs else "grad_attention_far",
            [SMEM] + [VMEM] * (len(args) - 1),
            [shape((chips, heads, width + size), BF16)],
            [],
            4 * self.length * chips * size * (width + heads),
            args,
        )[0]

    def grad_finish(self, name, blocks, by_rows):
        _, rows, cols = blocks.shape
        return call(
            functools.partial(finish_body, by_rows, 1, 0, cols),
            name + "_finish",
            [VMEM],
            [shape((rows, 2 * cols) if by_rows else (2 * rows, cols), F32)],
            [],
            blocks.size,
            [blocks],
        )[0]

    def attention_finish(self, blocks, width, planes):
        _, rows, cols = blocks.shape

        def body(ref, grad_in, grad_out):
            finish_body(True, planes, 0, width, ref, grad_in)
            finish_body(False, 1, width, cols - width, ref, grad_out)

        return call(
            body,
            "attention_finish",
            [VMEM],
            [shape((planes, rows, 2 * width // planes), F32), shape((2 * rows, cols - width), F32)],
            [],
            blocks.size,
            [blocks],
        )


def shards(
    dp,
    tensor,
    inputs,
    segment_ids,
    first_gain,
    first_shift,
    project_in,
    query_bias,
    value_bias,
    project_out,
    out_bias,
    second_gain,
    second_shift,
    up_weight,
    up_bias,
    down_weight,
    down_bias,
    cotangent,
):
    at = Places(dp, tensor)
    length, features = inputs.shape
    layer = Layer(at, length, features)
    own, table, side_at = layer.own, layer.table, layer.side_at
    heads, hidden_units = query_bias.shape[0] // 2, up_bias.shape[0] // 2
    both = 2 * length
    chunk_count = 2 * tensor
    chunk32, chunk16 = shape((own, features), F32), shape((own, features), BF16)
    tokens16 = shape((both, features), BF16)

    x_own, g_own = at.chunk_of(inputs), at.chunk_of(cotangent)
    mate = at.to_mate(jnp.concatenate([x_own, g_own]))
    ids = at.tokens_in(segment_ids)
    mate_ids = at.to_mate(ids)
    blocks = [at.halves(project_in, 2), at.halves(project_out, 0)[:, None]]
    mine_in = at.exchange(after(jnp.concatenate(blocks, 1), mate, mate_ids))
    mate_chunks = [mate] + at.to_peers(mate)
    up_blocks, down_blocks = at.halves(up_weight, 1), at.halves(down_weight, 0)
    mate_chunks = after(mate_chunks, up_blocks, down_blocks)
    vec = jnp.stack(
        [
            first_gain,
            first_shift,
            out_bias,
            second_gain,
            second_shift,
            down_bias,
            down_bias,
            down_bias,
        ]
    ).astype(F32)
    biases = [at.half_of(b)[None] for b in (query_bias, value_bias, up_bias)]
    order = at.tokens_in(jnp.arange(length, dtype=jnp.int32))
    ids = jnp.stack([ids, mate_ids])
    allowed = (
        (ids[:, :, None] == ids[:, None, :])
        & (ids[:, :, None] != 0)
        & (order[None, None, :] <= order[None, :, None])
    )
    allowed = (allowed | (order[None, None, :] == order[None, :, None])).astype(F32)
    first_low = layer.collect("first_norm", inputs, vec, mate_chunks, True)
    g = layer.collect("upstream", cotangent, vec, mate_chunks, False)
    mine_in = after(mine_in, first_low, allowed, biases, g)
    mine_up = at.exchange(after(up_blocks, mine_in))

    all_in = at.both_cores(mine_in)
    low_heads = shape((both, heads), BF16)
    query, key, value, probs, mixed = call(
        attend_body,
        "attend",
        [SMEM] + [VMEM] * 4 + [ANY] * 2,
        [low_heads] * 3 + [shape((2 * heads // DH, length, length), F32), low_heads],
        [pltpu.VMEM((3, features, heads), BF16), sems(3, dp)],
        12 * length * heads * features,
        [table, first_low, biases[0], biases[1], allowed] + all_in,
    )
    part = layer.project("project_out", mixed, all_in, False)
    received, _ = layer.reduce("project_out", part)
    hidden, normed_two, inverse_two, second_own = call(
        functools.partial(second_body, len(received)),
        "second_norm",
        [VMEM] * (3 + len(received)),
        [chunk32, chunk32, shape((own, 128), F32), chunk16],
        [],
        20 * own * features,
        [part[0], x_own, vec] + received,
    )
    second_chunks = at.spread(second_own)
    mine_up = after(mine_up, second_chunks[tensor])
    mine_down = at.exchange(after(down_blocks, mine_up))
    all_up = at.both_cores(mine_up)
    second_low, activated, slope = call(
        functools.partial(upper_body, chunk_count),
        "upper",
        [SMEM] + [VMEM] * (1 + chunk_count) + [ANY] * 2,
        [tokens16, shape((both, hidden_units), BF16), shape((both, hidden_units), F32)],
        [pltpu.VMEM((features, hidden_units), BF16), sems(dp)],
        4 * length * features * hidden_units,
        [table, biases[2]] + second_chunks + all_up,
    )
    far_down = layer.grad_far("grad_down", activated, [g], False)
    near_down = layer.grad_near("grad_down", activated, [g], False, at.to_core(far_down))
    mine_down = after(mine_down, near_down)
    ring_down = at.exchange(after(near_down, mine_down))
    all_down = at.both_cores(mine_down)
    upper_low, up_bias_grad = call(
        functools.partial(upper_grad_body, side_at),
        "upper_grad",
        [SMEM] + [VMEM] * 2 + [ANY] * 2,
        [shape((both, hidden_units), BF16), shape((1, 2 * hidden_units), F32)],
        [pltpu.VMEM((hidden_units, features), BF16), sems(dp)],
        4 * length * features * hidden_units,
        [table, g, slope] + all_down,
    )
    far_up = layer.grad_far("grad_up", second_low, [upper_low], True)
    part = layer.project("second_part", after(upper_low, far_up), all_up, True)
    received, folded = layer.reduce("second_part", part)
    near_up = layer.grad_near(
        "grad_up", second_low, after([upper_low], folded, received[:-1]), True, at.to_core(far_up)
    )
    hidden_grad, hidden_low_own, sums_two = call(
        functools.partial(second_back_body, len(received)),
        "second_back",
        [VMEM] * (5 + len(received)),
        [chunk32, chunk16, shape((8, features), F32)],
        [],
        20 * own * features,
        [after(part[0], ring_down, near_up), g_own, vec, normed_two, inverse_two] + received,
    )
    hidden_chunks = at.spread(hidden_low_own)
    ring_up = at.exchange(after(near_up, hidden_chunks[tensor]))
    feed = layer.project("feed", after(activated, hidden_low_own), all_down, False)
    back = call(
        functools.partial(attend_back_body, side_at, chunk_count),
        "attend_back",
        [SMEM] + [VMEM] * (4 + chunk_count) + [ANY] * 2,
        [tokens16, low_heads, low_heads, low_heads, shape((1, 4 * heads), F32)]
        + layer.chunk_outs(),
        [
            pltpu.VMEM((heads, features), BF16),
            pltpu.VMEM((3, features, heads), BF16),
            pltpu.VMEM((both, heads), BF16),
            sems(dp),
            sems(dp),
        ],
        16 * length * heads * features,
        [table, after(query, feed), key, value, probs]
        + hidden_chunks
        + all_in,
    )
    hidden_low, q_low, k_low, v_low, heads_grad, *part = back
    lows = [q_low, k_low, v_low]
    for_mate = layer.trade_mate(part)
    far = layer.grad_attention(first_low, mixed, lows, hidden_low)
    feed_for_mate = layer.trade_mate(after(feed, far))
    folded = layer.fold("first_part_fold", part[1], for_mate)
    from_mate = at.to_mate(folded)
    near = layer.grad_attention(first_low, mixed, after(lows, folded), hidden_low, at.to_core(far))
    received = layer.trade_own(after(part, feed_for_mate[0])) + [from_mate]
    feed_folded = layer.fold("feed_fold", after(feed[1], near), feed_for_mate)
    feed_from_mate = at.to_mate(feed_folded)
    ring_in = at.exchange(after(near, ring_up, received, feed_from_mate))
    grad_down = layer.grad_finish("grad_down", ring_down, False)
    grad_up = layer.grad_finish("grad_up", ring_up, True)
    input_own, sums_one = call(
        functools.partial(first_back_body, len(received)),
        "first_back",
        [VMEM] * (4 + len(received)),
        [chunk16, shape((8, features), F32)],
        [],
        20 * own * features,
        [part[0], x_own, vec, hidden_grad] + received,
    )
    def assemble(name, chunk, others):
        return call(
            functools.partial(assemble_body, dp, tensor),
            name,
            [SMEM] + [VMEM] * tensor,
            [shape((length, features), BF16)],
            [],
            length * features,
            [table, chunk] + others,
        )[0]

    input_others = at.to_peers(input_own)
    input_gradient = assemble("input_gradient", input_own, input_others)
    feed_received = layer.trade_own(after(feed, received[0])) + [feed_from_mate]
    outputs_own = call(
        functools.partial(output_body, len(feed_received)),
        "outputs_own",
        [VMEM] * (3 + len(feed_received)),
        [chunk16],
        [],
        4 * own * features,
        [after(feed[0], input_others), hidden, vec] + feed_received,
    )[0]
    output_others = at.to_peers(outputs_own)
    outputs = assemble("outputs", outputs_own, output_others)
    grad_in, grad_out = layer.attention_finish(ring_in, 3 * heads, 3)

    narrow = jnp.concatenate([heads_grad[0], up_bias_grad[0]])
    rows = -(-narrow.shape[0] // features)
    narrow = jnp.pad(narrow, (0, rows * features - narrow.shape[0])).reshape(rows, features)
    sums = at.sum_small(after(jnp.concatenate([sums_one[:2], sums_two[:4]]), input_others, grad_down, grad_up), narrow)
    narrow = sums[6:].reshape(-1)
    heads, hidden_units = 2 * heads, 2 * hidden_units
    return (
        outputs,
        input_gradient,
        sums[0],
        sums[1],
        grad_in,
        narrow[:heads],
        narrow[heads : 2 * heads],
        grad_out,
        sums[2],
        sums[3],
        sums[4],
        grad_up,
        narrow[2 * heads : 2 * heads + hidden_units],
        grad_down,
        sums[5],
    )


def solution(mesh):
    dp, tensor = mesh.shape["dp"], mesh.shape["tensor"]

    def program(*arguments):
        return shards(dp, tensor, *arguments)

    in_specs = (
        P("dp", None),
        P("dp"),
        P(),
        P(),
        P(None, "dp", "tensor"),
        P("tensor"),
        P("tensor"),
        P("tensor", "dp"),
        P(),
        P(),
        P(),
        P("dp", "tensor"),
        P("tensor"),
        P("tensor", "dp"),
        P(),
        P("dp", None),
    )
    out_specs = (
        P("dp", None),
        P("dp", None),
        P(),
        P(),
        P(None, "dp", "tensor"),
        P("tensor"),
        P("tensor"),
        P("tensor", "dp"),
        P(),
        P(),
        P(),
        P("dp", "tensor"),
        P("tensor"),
        P("tensor", "dp"),
        P(),
    )
    return jax.shard_map(program, mesh=mesh, in_specs=in_specs, out_specs=out_specs, check_vma=False)
```

```python
import functools

import jax
import jax.numpy as jnp
from jax import lax
from jax.experimental import pallas as pl
from jax.experimental.pallas import tpu as pltpu
from jax.sharding import PartitionSpec as P

DH = 128
EPSILON = 1e-05
NEGATIVE = -1e30
SCALE = DH ** (-0.5)
F32 = jnp.float32
BF16 = jnp.bfloat16
TILE = 512
ANY = pl.BlockSpec(memory_space=pl.ANY)
VMEM = pl.BlockSpec(memory_space=pltpu.VMEM)
SMEM = pl.BlockSpec(memory_space=pltpu.SMEM)


def nn(left, right):
    return lax.dot_general(left, right, (((1,), (0,)), ((), ())), preferred_element_type=F32)


def nt(left, right):
    return lax.dot_general(left, right, (((1,), (1,)), ((), ())), preferred_element_type=F32)


def tn(left, right):
    return lax.dot_general(left, right, (((0,), (0,)), ((), ())), preferred_element_type=F32)


def shape(dims, dtype):
    return jax.ShapeDtypeStruct(tuple(dims), dtype)


def call(body, name, in_specs, outs, scratch, flops, args):
    moved = sum(a.size * a.dtype.itemsize for a in args)
    moved += sum(o.size * o.dtype.itemsize for o in outs)
    return pl.pallas_call(
        body,
        name=name,
        out_shape=outs,
        in_specs=in_specs,
        out_specs=[VMEM] * len(outs),
        scratch_shapes=scratch,
        cost_estimate=pl.CostEstimate(flops=flops, bytes_accessed=moved, transcendentals=0),
    )(*args)


class Places:
    def __init__(self, dp, tensor):
        self.dp, self.tensor, self.chips = dp, tensor, dp // 2
        self.rank = lax.axis_index("dp")
        self.part = lax.axis_index("tensor")
        self.chip, self.core = self.rank // 2, self.rank % 2
        self.side = self.chip % 2
        self.swap = [(i, i ^ 1) for i in range(dp)]

    def table(self):
        owners = jnp.arange(self.chips, dtype=jnp.int32) * 2
        chunks = self.part ^ jnp.arange(self.tensor, dtype=jnp.int32)
        return jnp.concatenate(
            [owners + self.core, owners + (1 - self.core), chunks, self.side[None]]
        ).astype(jnp.int32)

    def tokens_in(self, values):
        size = values.shape[0] // self.tensor
        return jnp.take(
            values.reshape(self.tensor, size),
            self.part ^ jnp.arange(self.tensor, dtype=jnp.int32),
            axis=0,
        ).reshape(-1)

    def chunk_of(self, values):
        size = values.shape[0] // self.tensor
        return lax.dynamic_slice_in_dim(values, self.part * size, size, 0)

    def half_of(self, values):
        size = values.shape[0] // 2
        return lax.dynamic_slice_in_dim(values, self.side * size, size, 0)

    def to_core(self, values):
        return lax.ppermute(values, "dp", self.swap)

    def to_chip(self, values, k):
        return lax.ppermute(values, "dp", [(i, i ^ (2 * k)) for i in range(self.dp)])

    def to_mate(self, values):
        return self.to_chip(values, 1)

    def to_peer(self, values, k):
        return lax.ppermute(values, "tensor", [(i, i ^ k) for i in range(self.tensor)])

    def to_peers(self, values):
        many = isinstance(values, (list, tuple))
        return [
            self.to_peer(values[k - 1] if many else values, k)
            for k in range(self.tensor - 1, 0, -1)
        ][::-1]

    def exchange(self, blocks):
        groups = [[2 * j + core for j in range(self.chips)] for core in range(2)]
        return lax.all_to_all(blocks, "dp", 0, 0, axis_index_groups=groups, tiled=True)

    def halves(self, block, axis):
        halves = jnp.split(block, 2, axis)
        return jnp.stack([halves[j % 2] for j in range(self.chips)])

    def both_cores(self, blocks):
        return [blocks, self.to_core(blocks)]

    def spread(self, chunk):
        own = self.to_peers(chunk)
        mate = after(self.to_mate(chunk), own[:-1])
        return [chunk] + own + [mate] + self.to_peers(mate)

    def sum_small(self, wide, narrow):
        step = 1
        while step < self.tensor:
            wide = wide + self.to_peer(wide, step)
            step *= 2
        values = jnp.concatenate([wide, narrow])
        values = values + self.to_core(values)
        step = 1
        while step < self.chips:
            values = values + self.to_chip(values, step)
            step *= 2
        return values


def after(values, *events):
    values, _ = lax.optimization_barrier((values, events))
    return values


def center_of(values):
    center = values - jnp.mean(values, axis=-1, keepdims=True)
    inverse = lax.rsqrt(jnp.mean(center * center, axis=-1, keepdims=True) + EPSILON)
    return center * inverse, inverse


def norm_back(norm_grad, normed, inverse, gain):
    scaled = norm_grad * gain
    return inverse * (
        scaled
        - jnp.mean(scaled, axis=-1, keepdims=True)
        - normed * jnp.mean(scaled * normed, axis=-1, keepdims=True)
    )


def place(table, p, size):
    return pl.ds(pl.multiple_of(table[p] * size, size), size)


def collect_body(dp, tensor, norm, table, own, vec, *refs):
    chunks, (out,) = refs[:tensor], refs[tensor:]
    rows = chunks[0].shape[0] // 2
    first = 0 if norm else rows
    for s in range(2):
        for k in range(tensor):
            value = own[place(table, dp + k, rows), :] if s == 0 else chunks[k][first : first + rows, :]
            if norm:
                normed, _ = center_of(value.astype(F32))
                value = (normed * vec[0:1, :] + vec[1:2, :]).astype(BF16)
            start = (s * tensor + k) * rows
            out[start : start + rows, :] = value


def blocks_of(arrays):
    return [ref.at[j] for ref in arrays for j in range(ref.shape[0])]


def attend_body(table, x, q_bias, v_bias, allowed, *refs):
    pieces, (q, k, v, probs, mixed), (weight, sems) = blocks_of(refs[:2]), refs[2:-2], refs[-2:]
    count, size = len(pieces), refs[0].shape[2]

    def copy(j, p):
        return pltpu.make_async_copy(
            pieces[p].at[j], weight.at[j, place(table, p, size)], sems.at[j, p]
        )

    for j in range(3):
        for p in range(count):
            copy(j, p).start()
    columns = q.shape[1]
    tile = min(TILE, columns)
    for j, out in enumerate((q, k, v)):
        for p in range(count):
            copy(j, p).wait()
        for start in range(0, columns, tile):
            cols = slice(start, start + tile)
            total = nn(x[...], weight[j, :, cols])
            if j == 0:
                total = total + q_bias[:, cols].astype(F32)
            if j == 2:
                total = total + v_bias[:, cols].astype(F32)
            out[:, cols] = total.astype(BF16)
    heads = columns // DH
    length = allowed.shape[1]
    for s in range(2):
        rows = slice(s * length, (s + 1) * length)
        for h in range(heads):
            cols = slice(h * DH, (h + 1) * DH)
            scores = nt(q[rows, cols], k[rows, cols]) * SCALE
            scores = jnp.where(allowed[s] > 0, scores, NEGATIVE)
            weights = jnp.exp(scores - jnp.max(scores, axis=-1, keepdims=True))
            prob = weights / jnp.sum(weights, axis=-1, keepdims=True)
            probs[s * heads + h] = prob
            mixed[rows, cols] = nn(prob.astype(BF16), v[rows, cols]).astype(BF16)


def put_chunks(total, cols, own, mate, sends):
    rows = own.shape[0]
    length = total.shape[0] // 2
    chunks = length // rows
    own[:, cols] = total[:rows]
    mate[:, cols] = total[length : length + rows]
    for k in range(1, chunks):
        for s in range(2):
            part = total[s * length + k * rows : s * length + (k + 1) * rows].astype(BF16)
            sends[s * (chunks - 1) + k - 1][:, cols] = part


def column_copies(table, arrays, weight, sems):
    width = arrays[0].shape[-1]
    blocks = blocks_of(arrays)
    if len(arrays[0].shape) == 4:
        blocks = [block.at[3] for block in blocks]
    return [
        pltpu.make_async_copy(block, weight.at[:, place(table, p, width)], sems.at[p])
        for p, block in enumerate(blocks)
    ]


def row_copies(table, arrays, weight, sems):
    size = arrays[0].shape[1]
    return [
        pltpu.make_async_copy(piece, weight.at[place(table, p, size)], sems.at[p])
        for p, piece in enumerate(blocks_of(arrays))
    ]


def project_body(by_rows, table, left, *refs):
    pieces, (own, mate, *sends), (weight, sems) = refs[:2], refs[2:-2], refs[-2:]
    copies = (row_copies if by_rows else column_copies)(table, pieces, weight, sems)
    for copy in copies:
        copy.start()
    size = pieces[0].shape[1 if by_rows else -1]
    chips = pieces[0].shape[0]
    for j in range(chips):
        copies[j].wait()
        copies[chips + j].wait()
        cols = slice(2 * j * size, 2 * (j + 1) * size)
        if by_rows:
            total = nt(left[...], weight[cols, :])
        else:
            total = nn(left[...], weight[:, cols])
        put_chunks(total, cols, own, mate, sends)


def fold_body(mate, *refs):
    refs[-1][...] = summed(mate, refs[:-1]).astype(BF16)


def summed(own, received):
    total = own[...]
    for ref in received:
        total = total + ref[...].astype(F32)
    return total


def second_body(count, own, x, vec, *refs):
    received, (hidden, normed_out, inverse_out, low) = refs[:count], refs[count:]
    value = x[...].astype(F32) + summed(own, received) + vec[2:3, :]
    hidden[...] = value
    normed, inverse = center_of(value)
    normed_out[...] = normed
    inverse_out[...] = jnp.broadcast_to(inverse, inverse_out.shape)
    low[...] = (normed * vec[3:4, :] + vec[4:5, :]).astype(BF16)


def upper_body(chunk_count, table, bias, *refs):
    chunks, refs = refs[:chunk_count], refs[chunk_count:]
    pieces, (low, activated, slope), (weight, sems) = refs[:2], refs[2:-2], refs[-2:]
    copies = row_copies(table, pieces, weight, sems)
    for copy in copies:
        copy.start()
    rows = chunks[0].shape[0]
    for k, chunk in enumerate(chunks):
        low[k * rows : (k + 1) * rows, :] = chunk[...]
    for copy in copies:
        copy.wait()
    columns = weight.shape[1]
    tile = min(TILE, columns)

    @pl.loop(0, columns // tile)
    def _(i):
        cols = pl.ds(pl.multiple_of(i * tile, tile), tile)
        value = nn(low[...], weight[:, cols]) + bias[:, cols].astype(F32)
        below = 0.5 * (1.0 + lax.erf(value * (0.5**0.5)))
        activated[:, cols] = (value * below).astype(BF16)
        density = jnp.exp(-0.5 * value * value) * 0.3989422804014327
        slope[:, cols] = below + value * density


def upper_grad_body(side_at, table, g, slope, *refs):
    pieces, (low, bias_grad), (weight, sems) = refs[:2], refs[2:-2], refs[-2:]
    copies = column_copies(table, pieces, weight, sems)
    for copy in copies:
        copy.start()
    bias_grad[...] = jnp.zeros(bias_grad.shape, F32)
    for copy in copies:
        copy.wait()
    hidden = weight.shape[0]
    tile = min(TILE, hidden)
    first = table[side_at] * hidden

    @pl.loop(0, hidden // tile)
    def _(i):
        cols = pl.ds(pl.multiple_of(i * tile, tile), tile)
        grad = nt(g[...], weight[cols, :]) * slope[:, cols]
        low[:, cols] = grad.astype(BF16)
        there = pl.ds(pl.multiple_of(first + i * tile, tile), tile)
        bias_grad[:, there] = jnp.sum(grad, axis=0, keepdims=True)


def second_back_body(count, own, g, vec, normed, inverse, *refs):
    received, (hidden_grad, low, sums) = refs[:count], refs[count:]
    total = summed(own, received)
    upstream = g[...].astype(F32)
    grad = upstream + norm_back(total, normed[...], inverse[:, 0:1], vec[3:4, :])
    hidden_grad[...] = grad
    low[...] = grad.astype(BF16)
    for i, values in enumerate((grad, total * normed[...], total, upstream)):
        sums[i : i + 1, :] = jnp.sum(values, axis=0, keepdims=True)


def attend_back_body(side_at, chunk_count, table, q, k, v, probs, *refs):
    chunks, refs = refs[:chunk_count], refs[chunk_count:]
    pieces, refs = refs[:2], refs[2:]
    (low, q_low, k_low, v_low, bias_grad, own, mate, *sends) = refs[:-5]
    out_weight, in_weight, mixed_grad, out_sems, in_sems = refs[-5:]
    copies = column_copies(table, pieces, out_weight, out_sems)
    for copy in copies:
        copy.start()
    size = pieces[0].shape[2]
    ins = [
        pltpu.make_async_copy(
            piece.at[pl.ds(0, 3)], in_weight.at[:, place(table, p, size)], in_sems.at[p]
        )
        for p, piece in enumerate(blocks_of(pieces))
    ]
    for copy in ins:
        copy.start()
    rows = chunks[0].shape[0]
    for j, chunk in enumerate(chunks):
        low[j * rows : (j + 1) * rows, :] = chunk[...]
    bias_grad[...] = jnp.zeros(bias_grad.shape, F32)
    for copy in copies:
        copy.wait()
    columns = q.shape[1]
    tile = min(TILE, columns)
    for start in range(0, columns, tile):
        cols = slice(start, start + tile)
        mixed_grad[:, cols] = nt(low[...], out_weight[cols, :]).astype(BF16)
    heads = columns // DH
    length = probs.shape[1]
    first = table[side_at] * columns
    for h in range(heads):
        cols = slice(h * DH, (h + 1) * DH)
        q_sum = v_sum = 0.0
        for s in range(2):
            rows = slice(s * length, (s + 1) * length)
            prob, down = probs[s * heads + h], mixed_grad[rows, cols]
            prob_grad = nt(down, v[rows, cols])
            inner = jnp.sum(prob * prob_grad, axis=-1, keepdims=True)
            score_low = (prob * (prob_grad - inner) * SCALE).astype(BF16)
            query_grad = nn(score_low, k[rows, cols])
            q_low[rows, cols] = query_grad.astype(BF16)
            q_sum = q_sum + jnp.sum(query_grad, axis=0, keepdims=True)
            k_low[rows, cols] = tn(score_low, q[rows, cols]).astype(BF16)
            value_grad = tn(prob.astype(BF16), down)
            v_low[rows, cols] = value_grad.astype(BF16)
            v_sum = v_sum + jnp.sum(value_grad, axis=0, keepdims=True)
        there = pl.multiple_of(first + h * DH, DH)
        bias_grad[:, pl.ds(there, DH)] = q_sum
        bias_grad[:, pl.ds(pl.multiple_of(there + 2 * columns, DH), DH)] = v_sum
    chips = pieces[0].shape[0]
    for j in range(chips):
        ins[j].wait()
        ins[chips + j].wait()
        cols = slice(2 * j * size, 2 * (j + 1) * size)
        total = nt(q_low[...], in_weight[0, cols, :])
        total = total + nt(k_low[...], in_weight[1, cols, :])
        total = total + nt(v_low[...], in_weight[2, cols, :])
        put_chunks(total, cols, own, mate, sends)


def first_back_body(count, own, x, vec, hidden_grad, *refs):
    received, (result, sums) = refs[:count], refs[count:]
    total = summed(own, received)
    normed, inverse = center_of(x[...].astype(F32))
    grad = hidden_grad[...] + norm_back(total, normed, inverse, vec[0:1, :])
    result[...] = grad.astype(BF16)
    for i, values in enumerate((total * normed, total)):
        sums[i : i + 1, :] = jnp.sum(values, axis=0, keepdims=True)


def output_body(count, own, hidden, vec, *refs):
    received, (result,) = refs[:count], refs[count:]
    total = summed(own, received)
    result[...] = (hidden[...] + total + vec[5:6, :]).astype(BF16)


def assemble_body(dp, tensor, table, *refs):
    chunks, (result,) = refs[:tensor], refs[tensor:]
    rows = chunks[0].shape[0]
    for k, chunk in enumerate(chunks):
        result[place(table, dp + k, rows), :] = chunk[...]


def grad_blocks(table, left, right, by_rows, first, chips, size, put):
    if by_rows:
        width = right[0].shape[1]
        tile = min(TILE, width)
        for block in range(chips):
            turned = left[:, place(table, first + block, size)].T
            for j, ref in enumerate(right):
                for c in range(0, width, tile):
                    put(block, 0, j * width + c, nn(turned, ref[:, c : c + tile]))
    else:
        hidden = left.shape[1]
        step = min(512, hidden)
        for r in range(0, hidden, step):
            turned = left[:, r : r + step].T
            for block in range(chips):
                put(block, r, 0, nn(turned, right[0][:, place(table, first + block, size)]))


def grad_body(by_rows, first, chips, size, count, table, left, *refs):
    right, theirs, out = refs[:count], refs[count:-1], refs[-1]

    def put(block, low, column, value):
        rows, cols = slice(low, low + value.shape[0]), slice(column, column + value.shape[1])
        for ref in theirs:
            value = value + ref[block, rows, cols].astype(F32)
        out[block, rows, cols] = value.astype(BF16)

    grad_blocks(table, left, right, by_rows, first, chips, size, put)


def finish_body(by_rows, planes, first, cols, blocks, out):
    chips, rows, _ = blocks.shape
    here = slice(first, first + cols)
    for half in range(2):
        total = blocks[half, :, here].astype(F32)
        for j in range(half + 2, chips, 2):
            total = total + blocks[j, :, here].astype(F32)
        if not by_rows:
            out[half * rows : (half + 1) * rows, :] = total
        elif planes == 1:
            out[:, half * cols : (half + 1) * cols] = total
        else:
            width = cols // planes
            for j in range(planes):
                out[j, :, half * width : (half + 1) * width] = total[:, j * width : (j + 1) * width]


def sems(*dims):
    return pltpu.SemaphoreType.DMA(tuple(dims))


class Layer:
    def __init__(self, at, length, features):
        self.at, self.table = at, at.table()
        self.length, self.features = length, features
        self.own = length // at.tensor
        self.side_at = at.dp + at.tensor

    def chunk_outs(self):
        sends = [shape((self.own, self.features), BF16)] * (2 * self.at.tensor - 2)
        return [shape((self.own, self.features), F32)] * 2 + sends

    def collect(self, name, own, vec, chunks, norm):
        at = self.at
        return call(
            functools.partial(collect_body, at.dp, at.tensor, norm),
            name,
            [SMEM] + [VMEM] * (2 + at.tensor),
            [shape((2 * self.length, self.features), BF16)],
            [],
            20 * self.length * self.features,
            [self.table, own, vec] + chunks,
        )[0]

    def project(self, name, left, blocks, by_rows):
        inner = left.shape[1]
        weight = (self.features, inner) if by_rows else (inner, self.features)
        return call(
            functools.partial(project_body, by_rows),
            name,
            [SMEM, VMEM] + [ANY] * 2,
            self.chunk_outs(),
            [pltpu.VMEM(weight, BF16), sems(self.at.dp)],
            4 * self.length * inner * self.features,
            [self.table, left] + blocks,
        )

    def fold(self, name, mate, received):
        return call(
            fold_body,
            name,
            [VMEM] * (1 + len(received)),
            [shape(mate.shape, BF16)],
            [],
            mate.size * 4,
            [mate] + received,
        )[0]

    def trade_mate(self, part):
        return self.at.to_peers(part[1 + self.at.tensor :])

    def trade_own(self, part):
        return self.at.to_peers(part[2 : 1 + self.at.tensor])

    def reduce(self, name, part):
        for_mate, own = self.trade_mate(part), self.trade_own(part)
        folded = self.fold(name + "_fold", part[1], for_mate)
        return own + [self.at.to_mate(folded)], folded

    def block_shape(self, left, right, by_rows):
        size = self.features // self.at.dp
        if by_rows:
            return size, (size, sum(r.shape[1] for r in right))
        return size, (left.shape[1], size)

    def grad(self, name, left, right, by_rows, *theirs):
        chips = self.at.chips
        size, block = self.block_shape(left, right, by_rows)
        return call(
            functools.partial(grad_body, by_rows, 0 if theirs else chips, chips, size, len(right)),
            name + ("_near" if theirs else "_far"),
            [SMEM] + [VMEM] * (1 + len(right) + len(theirs)),
            [shape((chips,) + block, BF16)],
            [],
            4 * self.length * chips * block[0] * block[1],
            [self.table, left] + list(right) + list(theirs),
        )[0]

    def grad_far(self, name, left, right, by_rows):
        return self.grad(name, left, right, by_rows)

    def grad_near(self, name, left, right, by_rows, theirs):
        return self.grad(name, left, right, by_rows, theirs)

    def grad_attention(self, first_low, mixed, lows, hidden_low, *theirs):
        chips, size = self.at.chips, self.features // self.at.dp
        width, heads = len(lows) * lows[0].shape[1], mixed.shape[1]
        first = 0 if theirs else chips

        def body(table, left, other, *refs):
            right, low, got, out = refs[:3], refs[3], refs[4:-1], refs[-1]

            def put_at(start):
                def put(block, row, column, value):
                    rows = slice(row, row + value.shape[0])
                    cols = slice(start + column, start + column + value.shape[1])
                    for ref in got:
                        value = value + ref[block, rows, cols].astype(F32)
                    out[block, rows, cols] = value.astype(BF16)

                return put

            grad_blocks(table, left, right, True, first, chips, size, put_at(0))
            grad_blocks(table, other, [low], False, first, chips, size, put_at(width))

        args = [self.table, first_low, mixed] + list(lows) + [hidden_low] + list(theirs)
        return call(
            body,
            "grad_attention_near" if theirs else "grad_attention_far",
            [SMEM] + [VMEM] * (len(args) - 1),
            [shape((chips, heads, width + size), BF16)],
            [],
            4 * self.length * chips * size * (width + heads),
            args,
        )[0]

    def grad_finish(self, name, blocks, by_rows):
        _, rows, cols = blocks.shape
        return call(
            functools.partial(finish_body, by_rows, 1, 0, cols),
            name + "_finish",
            [VMEM],
            [shape((rows, 2 * cols) if by_rows else (2 * rows, cols), F32)],
            [],
            blocks.size,
            [blocks],
        )[0]

    def attention_finish(self, blocks, width, planes):
        _, rows, cols = blocks.shape

        def body(ref, grad_in, grad_out):
            finish_body(True, planes, 0, width, ref, grad_in)
            finish_body(False, 1, width, cols - width, ref, grad_out)

        return call(
            body,
            "attention_finish",
            [VMEM],
            [shape((planes, rows, 2 * width // planes), F32), shape((2 * rows, cols - width), F32)],
            [],
            blocks.size,
            [blocks],
        )


def shards(
    dp,
    tensor,
    inputs,
    segment_ids,
    first_gain,
    first_shift,
    project_in,
    query_bias,
    value_bias,
    project_out,
    out_bias,
    second_gain,
    second_shift,
    up_weight,
    up_bias,
    down_weight,
    down_bias,
    cotangent,
):
    at = Places(dp, tensor)
    length, features = inputs.shape
    layer = Layer(at, length, features)
    own, table, side_at = layer.own, layer.table, layer.side_at
    heads, hidden_units = query_bias.shape[0] // 2, up_bias.shape[0] // 2
    both = 2 * length
    chunk_count = 2 * tensor
    chunk32, chunk16 = shape((own, features), F32), shape((own, features), BF16)
    tokens16 = shape((both, features), BF16)

    x_own, g_own = at.chunk_of(inputs), at.chunk_of(cotangent)
    mate = at.to_mate(jnp.concatenate([x_own, g_own]))
    ids = at.tokens_in(segment_ids)
    mate_ids = at.to_mate(ids)
    blocks = [at.halves(project_in, 2), at.halves(project_out, 0)[:, None]]
    mine_in = at.exchange(after(jnp.concatenate(blocks, 1), mate, mate_ids))
    mate_chunks = [mate] + at.to_peers(mate)
    up_blocks, down_blocks = at.halves(up_weight, 1), at.halves(down_weight, 0)
    mate_chunks = after(mate_chunks, up_blocks, down_blocks)
    vec = jnp.stack(
        [
            first_gain,
            first_shift,
            out_bias,
            second_gain,
            second_shift,
            down_bias,
            down_bias,
            down_bias,
        ]
    ).astype(F32)
    biases = [at.half_of(b)[None] for b in (query_bias, value_bias, up_bias)]
    order = at.tokens_in(jnp.arange(length, dtype=jnp.int32))
    ids = jnp.stack([ids, mate_ids])
    allowed = (
        (ids[:, :, None] == ids[:, None, :])
        & (ids[:, :, None] != 0)
        & (order[None, None, :] <= order[None, :, None])
    )
    allowed = (allowed | (order[None, None, :] == order[None, :, None])).astype(F32)
    first_low = layer.collect("first_norm", inputs, vec, mate_chunks, True)
    g = layer.collect("upstream", cotangent, vec, mate_chunks, False)
    mine_in = after(mine_in, first_low, allowed, biases, g)
    mine_up = at.exchange(after(up_blocks, mine_in))

    all_in = at.both_cores(mine_in)
    low_heads = shape((both, heads), BF16)
    query, key, value, probs, mixed = call(
        attend_body,
        "attend",
        [SMEM] + [VMEM] * 4 + [ANY] * 2,
        [low_heads] * 3 + [shape((2 * heads // DH, length, length), F32), low_heads],
        [pltpu.VMEM((3, features, heads), BF16), sems(3, dp)],
        12 * length * heads * features,
        [table, first_low, biases[0], biases[1], allowed] + all_in,
    )
    part = layer.project("project_out", mixed, all_in, False)
    received, _ = layer.reduce("project_out", part)
    hidden, normed_two, inverse_two, second_own = call(
        functools.partial(second_body, len(received)),
        "second_norm",
        [VMEM] * (3 + len(received)),
        [chunk32, chunk32, shape((own, 128), F32), chunk16],
        [],
        20 * own * features,
        [part[0], x_own, vec] + received,
    )
    second_chunks = at.spread(second_own)
    mine_up = after(mine_up, second_chunks[tensor])
    mine_down = at.exchange(after(down_blocks, mine_up))
    all_up = at.both_cores(mine_up)
    second_low, activated, slope = call(
        functools.partial(upper_body, chunk_count),
        "upper",
        [SMEM] + [VMEM] * (1 + chunk_count) + [ANY] * 2,
        [tokens16, shape((both, hidden_units), BF16), shape((both, hidden_units), F32)],
        [pltpu.VMEM((features, hidden_units), BF16), sems(dp)],
        4 * length * features * hidden_units,
        [table, biases[2]] + second_chunks + all_up,
    )
    far_down = layer.grad_far("grad_down", activated, [g], False)
    near_down = layer.grad_near("grad_down", activated, [g], False, at.to_core(far_down))
    mine_down = after(mine_down, near_down)
    ring_down = at.exchange(after(near_down, mine_down))
    all_down = at.both_cores(mine_down)
    upper_low, up_bias_grad = call(
        functools.partial(upper_grad_body, side_at),
        "upper_grad",
        [SMEM] + [VMEM] * 2 + [ANY] * 2,
        [shape((both, hidden_units), BF16), shape((1, 2 * hidden_units), F32)],
        [pltpu.VMEM((hidden_units, features), BF16), sems(dp)],
        4 * length * features * hidden_units,
        [table, g, slope] + all_down,
    )
    far_up = layer.grad_far("grad_up", second_low, [upper_low], True)
    part = layer.project("second_part", after(upper_low, far_up), all_up, True)
    received, folded = layer.reduce("second_part", part)
    near_up = layer.grad_near(
        "grad_up", second_low, after([upper_low], folded, received[:-1]), True, at.to_core(far_up)
    )
    hidden_grad, hidden_low_own, sums_two = call(
        functools.partial(second_back_body, len(received)),
        "second_back",
        [VMEM] * (5 + len(received)),
        [chunk32, chunk16, shape((8, features), F32)],
        [],
        20 * own * features,
        [after(part[0], ring_down, near_up), g_own, vec, normed_two, inverse_two] + received,
    )
    hidden_chunks = at.spread(hidden_low_own)
    feed = layer.project("feed", after(activated, hidden_low_own), all_down, False)
    ring_up = at.exchange(after(near_up, hidden_chunks[tensor], feed[0]))
    back = call(
        functools.partial(attend_back_body, side_at, chunk_count),
        "attend_back",
        [SMEM] + [VMEM] * (4 + chunk_count) + [ANY] * 2,
        [tokens16, low_heads, low_heads, low_heads, shape((1, 4 * heads), F32)]
        + layer.chunk_outs(),
        [
            pltpu.VMEM((heads, features), BF16),
            pltpu.VMEM((3, features, heads), BF16),
            pltpu.VMEM((both, heads), BF16),
            sems(dp),
            sems(dp),
        ],
        16 * length * heads * features,
        [table, after(query, feed), key, value, probs]
        + hidden_chunks
        + all_in,
    )
    hidden_low, q_low, k_low, v_low, heads_grad, *part = back
    lows = [q_low, k_low, v_low]
    for_mate = layer.trade_mate(part)
    far = layer.grad_attention(first_low, mixed, lows, hidden_low)
    feed_for_mate = layer.trade_mate(after(feed, far))
    folded = layer.fold("first_part_fold", part[1], for_mate)
    from_mate = at.to_mate(folded)
    near = layer.grad_attention(first_low, mixed, after(lows, folded), hidden_low, at.to_core(far))
    received = layer.trade_own(after(part, feed_for_mate[0])) + [from_mate]
    feed_folded = layer.fold("feed_fold", after(feed[1], near), feed_for_mate)
    feed_from_mate = at.to_mate(feed_folded)
    ring_in = at.exchange(after(near, ring_up, received, feed_from_mate))
    grad_down = layer.grad_finish("grad_down", ring_down, False)
    grad_up = layer.grad_finish("grad_up", ring_up, True)
    input_own, sums_one = call(
        functools.partial(first_back_body, len(received)),
        "first_back",
        [VMEM] * (4 + len(received)),
        [chunk16, shape((8, features), F32)],
        [],
        20 * own * features,
        [part[0], x_own, vec, hidden_grad] + received,
    )
    def assemble(name, chunk, others):
        return call(
            functools.partial(assemble_body, dp, tensor),
            name,
            [SMEM] + [VMEM] * tensor,
            [shape((length, features), BF16)],
            [],
            length * features,
            [table, chunk] + others,
        )[0]

    input_others = at.to_peers(input_own)
    input_gradient = assemble("input_gradient", input_own, input_others)
    feed_received = layer.trade_own(after(feed, received[0])) + [feed_from_mate]
    outputs_own = call(
        functools.partial(output_body, len(feed_received)),
        "outputs_own",
        [VMEM] * (3 + len(feed_received)),
        [chunk16],
        [],
        4 * own * features,
        [after(feed[0], input_others), hidden, vec] + feed_received,
    )[0]
    output_others = at.to_peers(outputs_own)
    outputs = assemble("outputs", outputs_own, output_others)
    grad_in, grad_out = layer.attention_finish(ring_in, 3 * heads, 3)

    narrow = jnp.concatenate([heads_grad[0], up_bias_grad[0]])
    rows = -(-narrow.shape[0] // features)
    narrow = jnp.pad(narrow, (0, rows * features - narrow.shape[0])).reshape(rows, features)
    sums = at.sum_small(after(jnp.concatenate([sums_one[:2], sums_two[:4]]), input_others, grad_down, grad_up), narrow)
    narrow = sums[6:].reshape(-1)
    heads, hidden_units = 2 * heads, 2 * hidden_units
    return (
        outputs,
        input_gradient,
        sums[0],
        sums[1],
        grad_in,
        narrow[:heads],
        narrow[heads : 2 * heads],
        grad_out,
        sums[2],
        sums[3],
        sums[4],
        grad_up,
        narrow[2 * heads : 2 * heads + hidden_units],
        grad_down,
        sums[5],
    )


def solution(mesh):
    dp, tensor = mesh.shape["dp"], mesh.shape["tensor"]

    def program(*arguments):
        return shards(dp, tensor, *arguments)

    in_specs = (
        P("dp", None),
        P("dp"),
        P(),
        P(),
        P(None, "dp", "tensor"),
        P("tensor"),
        P("tensor"),
        P("tensor", "dp"),
        P(),
        P(),
        P(),
        P("dp", "tensor"),
        P("tensor"),
        P("tensor", "dp"),
        P(),
        P("dp", None),
    )
    out_specs = (
        P("dp", None),
        P("dp", None),
        P(),
        P(),
        P(None, "dp", "tensor"),
        P("tensor"),
        P("tensor"),
        P("tensor", "dp"),
        P(),
        P(),
        P(),
        P("dp", "tensor"),
        P("tensor"),
        P("tensor", "dp"),
        P(),
    )
    return jax.shard_map(program, mesh=mesh, in_specs=in_specs, out_specs=out_specs, check_vma=False)
```

```python
import functools

import jax
import jax.numpy as jnp
from jax import lax
from jax.experimental import pallas as pl
from jax.experimental.pallas import tpu as pltpu
from jax.sharding import PartitionSpec as P

DH = 128
EPSILON = 1e-05
NEGATIVE = -1e30
SCALE = DH ** (-0.5)
F32 = jnp.float32
BF16 = jnp.bfloat16
TILE = 512
ANY = pl.BlockSpec(memory_space=pl.ANY)
VMEM = pl.BlockSpec(memory_space=pltpu.VMEM)
SMEM = pl.BlockSpec(memory_space=pltpu.SMEM)


def nn(left, right):
    return lax.dot_general(left, right, (((1,), (0,)), ((), ())), preferred_element_type=F32)


def nt(left, right):
    return lax.dot_general(left, right, (((1,), (1,)), ((), ())), preferred_element_type=F32)


def tn(left, right):
    return lax.dot_general(left, right, (((0,), (0,)), ((), ())), preferred_element_type=F32)


def shape(dims, dtype):
    return jax.ShapeDtypeStruct(tuple(dims), dtype)


def call(body, name, in_specs, outs, scratch, flops, args):
    moved = sum(a.size * a.dtype.itemsize for a in args)
    moved += sum(o.size * o.dtype.itemsize for o in outs)
    return pl.pallas_call(
        body,
        name=name,
        out_shape=outs,
        in_specs=in_specs,
        out_specs=[VMEM] * len(outs),
        scratch_shapes=scratch,
        cost_estimate=pl.CostEstimate(flops=flops, bytes_accessed=moved, transcendentals=0),
    )(*args)


class Places:
    def __init__(self, dp, tensor):
        self.dp, self.tensor, self.chips = dp, tensor, dp // 2
        self.rank = lax.axis_index("dp")
        self.part = lax.axis_index("tensor")
        self.chip, self.core = self.rank // 2, self.rank % 2
        self.side = self.chip % 2
        self.swap = [(i, i ^ 1) for i in range(dp)]

    def table(self):
        owners = jnp.arange(self.chips, dtype=jnp.int32) * 2
        chunks = self.part ^ jnp.arange(self.tensor, dtype=jnp.int32)
        return jnp.concatenate(
            [owners + self.core, owners + (1 - self.core), chunks, self.side[None]]
        ).astype(jnp.int32)

    def tokens_in(self, values):
        size = values.shape[0] // self.tensor
        return jnp.take(
            values.reshape(self.tensor, size),
            self.part ^ jnp.arange(self.tensor, dtype=jnp.int32),
            axis=0,
        ).reshape(-1)

    def chunk_of(self, values):
        size = values.shape[0] // self.tensor
        return lax.dynamic_slice_in_dim(values, self.part * size, size, 0)

    def half_of(self, values):
        size = values.shape[0] // 2
        return lax.dynamic_slice_in_dim(values, self.side * size, size, 0)

    def to_core(self, values):
        return lax.ppermute(values, "dp", self.swap)

    def to_chip(self, values, k):
        return lax.ppermute(values, "dp", [(i, i ^ (2 * k)) for i in range(self.dp)])

    def to_mate(self, values):
        return self.to_chip(values, 1)

    def to_peer(self, values, k):
        return lax.ppermute(values, "tensor", [(i, i ^ k) for i in range(self.tensor)])

    def to_peers(self, values):
        many = isinstance(values, (list, tuple))
        return [
            self.to_peer(values[k - 1] if many else values, k)
            for k in range(self.tensor - 1, 0, -1)
        ][::-1]

    def exchange(self, blocks):
        groups = [[2 * j + core for j in range(self.chips)] for core in range(2)]
        return lax.all_to_all(blocks, "dp", 0, 0, axis_index_groups=groups, tiled=True)

    def halves(self, block, axis):
        halves = jnp.split(block, 2, axis)
        return jnp.stack([halves[j % 2] for j in range(self.chips)])

    def both_cores(self, blocks):
        return [blocks, self.to_core(blocks)]

    def spread(self, chunk):
        own = self.to_peers(chunk)
        mate = after(self.to_mate(chunk), own[:-1])
        return [chunk] + own + [mate] + self.to_peers(mate)

    def sum_small(self, wide, narrow):
        step = 1
        while step < self.tensor:
            wide = wide + self.to_peer(wide, step)
            step *= 2
        values = jnp.concatenate([wide, narrow])
        values = values + self.to_core(values)
        step = 1
        while step < self.chips:
            values = values + self.to_chip(values, step)
            step *= 2
        return values


def after(values, *events):
    values, _ = lax.optimization_barrier((values, events))
    return values


def center_of(values):
    center = values - jnp.mean(values, axis=-1, keepdims=True)
    inverse = lax.rsqrt(jnp.mean(center * center, axis=-1, keepdims=True) + EPSILON)
    return center * inverse, inverse


def norm_back(norm_grad, normed, inverse, gain):
    scaled = norm_grad * gain
    return inverse * (
        scaled
        - jnp.mean(scaled, axis=-1, keepdims=True)
        - normed * jnp.mean(scaled * normed, axis=-1, keepdims=True)
    )


def place(table, p, size):
    return pl.ds(pl.multiple_of(table[p] * size, size), size)


def collect_body(dp, tensor, norm, table, own, vec, *refs):
    chunks, (out,) = refs[:tensor], refs[tensor:]
    rows = chunks[0].shape[0] // 2
    first = 0 if norm else rows
    for s in range(2):
        for k in range(tensor):
            value = own[place(table, dp + k, rows), :] if s == 0 else chunks[k][first : first + rows, :]
            if norm:
                normed, _ = center_of(value.astype(F32))
                value = (normed * vec[0:1, :] + vec[1:2, :]).astype(BF16)
            start = (s * tensor + k) * rows
            out[start : start + rows, :] = value


def blocks_of(arrays):
    return [ref.at[j] for ref in arrays for j in range(ref.shape[0])]


def attend_body(table, x, q_bias, v_bias, allowed, *refs):
    pieces, (q, k, v, probs, mixed), (weight, sems) = blocks_of(refs[:2]), refs[2:-2], refs[-2:]
    count, size = len(pieces), refs[0].shape[2]

    def copy(j, p):
        return pltpu.make_async_copy(
            pieces[p].at[j], weight.at[j, place(table, p, size)], sems.at[j, p]
        )

    for j in range(3):
        for p in range(count):
            copy(j, p).start()
    columns = q.shape[1]
    tile = min(TILE, columns)
    for j, out in enumerate((q, k, v)):
        for p in range(count):
            copy(j, p).wait()
        for start in range(0, columns, tile):
            cols = slice(start, start + tile)
            total = nn(x[...], weight[j, :, cols])
            if j == 0:
                total = total + q_bias[:, cols].astype(F32)
            if j == 2:
                total = total + v_bias[:, cols].astype(F32)
            out[:, cols] = total.astype(BF16)
    heads = columns // DH
    length = allowed.shape[1]
    for s in range(2):
        rows = slice(s * length, (s + 1) * length)
        for h in range(heads):
            cols = slice(h * DH, (h + 1) * DH)
            scores = nt(q[rows, cols], k[rows, cols]) * SCALE
            scores = jnp.where(allowed[s] > 0, scores, NEGATIVE)
            weights = jnp.exp(scores - jnp.max(scores, axis=-1, keepdims=True))
            prob = weights / jnp.sum(weights, axis=-1, keepdims=True)
            probs[s * heads + h] = prob
            mixed[rows, cols] = nn(prob.astype(BF16), v[rows, cols]).astype(BF16)


def put_chunks(total, cols, own, mate, sends):
    rows = own.shape[0]
    length = total.shape[0] // 2
    chunks = length // rows
    own[:, cols] = total[:rows]
    mate[:, cols] = total[length : length + rows]
    for k in range(1, chunks):
        for s in range(2):
            part = total[s * length + k * rows : s * length + (k + 1) * rows].astype(BF16)
            sends[s * (chunks - 1) + k - 1][:, cols] = part


def column_copies(table, arrays, weight, sems):
    width = arrays[0].shape[-1]
    blocks = blocks_of(arrays)
    if len(arrays[0].shape) == 4:
        blocks = [block.at[3] for block in blocks]
    return [
        pltpu.make_async_copy(block, weight.at[:, place(table, p, width)], sems.at[p])
        for p, block in enumerate(blocks)
    ]


def row_copies(table, arrays, weight, sems):
    size = arrays[0].shape[1]
    return [
        pltpu.make_async_copy(piece, weight.at[place(table, p, size)], sems.at[p])
        for p, piece in enumerate(blocks_of(arrays))
    ]


def project_body(by_rows, table, left, *refs):
    pieces, (own, mate, *sends), (weight, sems) = refs[:2], refs[2:-2], refs[-2:]
    copies = (row_copies if by_rows else column_copies)(table, pieces, weight, sems)
    for copy in copies:
        copy.start()
    size = pieces[0].shape[1 if by_rows else -1]
    chips = pieces[0].shape[0]
    for j in range(chips):
        copies[j].wait()
        copies[chips + j].wait()
        cols = slice(2 * j * size, 2 * (j + 1) * size)
        if by_rows:
            total = nt(left[...], weight[cols, :])
        else:
            total = nn(left[...], weight[:, cols])
        put_chunks(total, cols, own, mate, sends)


def fold_body(mate, *refs):
    refs[-1][...] = summed(mate, refs[:-1]).astype(BF16)


def summed(own, received):
    total = own[...]
    for ref in received:
        total = total + ref[...].astype(F32)
    return total


def second_body(count, own, x, vec, *refs):
    received, (hidden, normed_out, inverse_out, low) = refs[:count], refs[count:]
    value = x[...].astype(F32) + summed(own, received) + vec[2:3, :]
    hidden[...] = value
    normed, inverse = center_of(value)
    normed_out[...] = normed
    inverse_out[...] = jnp.broadcast_to(inverse, inverse_out.shape)
    low[...] = (normed * vec[3:4, :] + vec[4:5, :]).astype(BF16)


def upper_body(chunk_count, table, bias, *refs):
    chunks, refs = refs[:chunk_count], refs[chunk_count:]
    pieces, (low, activated, slope), (weight, sems) = refs[:2], refs[2:-2], refs[-2:]
    copies = row_copies(table, pieces, weight, sems)
    for copy in copies:
        copy.start()
    rows = chunks[0].shape[0]
    for k, chunk in enumerate(chunks):
        low[k * rows : (k + 1) * rows, :] = chunk[...]
    for copy in copies:
        copy.wait()
    columns = weight.shape[1]
    tile = min(TILE, columns)

    @pl.loop(0, columns // tile)
    def _(i):
        cols = pl.ds(pl.multiple_of(i * tile, tile), tile)
        value = nn(low[...], weight[:, cols]) + bias[:, cols].astype(F32)
        below = 0.5 * (1.0 + lax.erf(value * (0.5**0.5)))
        activated[:, cols] = (value * below).astype(BF16)
        density = jnp.exp(-0.5 * value * value) * 0.3989422804014327
        slope[:, cols] = below + value * density


def upper_grad_body(side_at, table, g, slope, *refs):
    pieces, (low, bias_grad), (weight, sems) = refs[:2], refs[2:-2], refs[-2:]
    copies = column_copies(table, pieces, weight, sems)
    for copy in copies:
        copy.start()
    bias_grad[...] = jnp.zeros(bias_grad.shape, F32)
    for copy in copies:
        copy.wait()
    hidden = weight.shape[0]
    tile = min(TILE, hidden)
    first = table[side_at] * hidden

    @pl.loop(0, hidden // tile)
    def _(i):
        cols = pl.ds(pl.multiple_of(i * tile, tile), tile)
        grad = nt(g[...], weight[cols, :]) * slope[:, cols]
        low[:, cols] = grad.astype(BF16)
        there = pl.ds(pl.multiple_of(first + i * tile, tile), tile)
        bias_grad[:, there] = jnp.sum(grad, axis=0, keepdims=True)


def second_back_body(count, own, g, vec, normed, inverse, *refs):
    received, (hidden_grad, low, sums) = refs[:count], refs[count:]
    total = summed(own, received)
    upstream = g[...].astype(F32)
    grad = upstream + norm_back(total, normed[...], inverse[:, 0:1], vec[3:4, :])
    hidden_grad[...] = grad
    low[...] = grad.astype(BF16)
    for i, values in enumerate((grad, total * normed[...], total, upstream)):
        sums[i : i + 1, :] = jnp.sum(values, axis=0, keepdims=True)


def attend_back_body(side_at, chunk_count, table, q, k, v, probs, *refs):
    chunks, refs = refs[:chunk_count], refs[chunk_count:]
    pieces, refs = refs[:2], refs[2:]
    (low, q_low, k_low, v_low, bias_grad, own, mate, *sends) = refs[:-5]
    out_weight, in_weight, mixed_grad, out_sems, in_sems = refs[-5:]
    copies = column_copies(table, pieces, out_weight, out_sems)
    for copy in copies:
        copy.start()
    size = pieces[0].shape[2]
    ins = [
        pltpu.make_async_copy(
            piece.at[pl.ds(0, 3)], in_weight.at[:, place(table, p, size)], in_sems.at[p]
        )
        for p, piece in enumerate(blocks_of(pieces))
    ]
    for copy in ins:
        copy.start()
    rows = chunks[0].shape[0]
    for j, chunk in enumerate(chunks):
        low[j * rows : (j + 1) * rows, :] = chunk[...]
    bias_grad[...] = jnp.zeros(bias_grad.shape, F32)
    for copy in copies:
        copy.wait()
    columns = q.shape[1]
    tile = min(TILE, columns)
    for start in range(0, columns, tile):
        cols = slice(start, start + tile)
        mixed_grad[:, cols] = nt(low[...], out_weight[cols, :]).astype(BF16)
    heads = columns // DH
    length = probs.shape[1]
    first = table[side_at] * columns
    for h in range(heads):
        cols = slice(h * DH, (h + 1) * DH)
        q_sum = v_sum = 0.0
        for s in range(2):
            rows = slice(s * length, (s + 1) * length)
            prob, down = probs[s * heads + h], mixed_grad[rows, cols]
            prob_grad = nt(down, v[rows, cols])
            inner = jnp.sum(prob * prob_grad, axis=-1, keepdims=True)
            score_low = (prob * (prob_grad - inner) * SCALE).astype(BF16)
            query_grad = nn(score_low, k[rows, cols])
            q_low[rows, cols] = query_grad.astype(BF16)
            q_sum = q_sum + jnp.sum(query_grad, axis=0, keepdims=True)
            k_low[rows, cols] = tn(score_low, q[rows, cols]).astype(BF16)
            value_grad = tn(prob.astype(BF16), down)
            v_low[rows, cols] = value_grad.astype(BF16)
            v_sum = v_sum + jnp.sum(value_grad, axis=0, keepdims=True)
        there = pl.multiple_of(first + h * DH, DH)
        bias_grad[:, pl.ds(there, DH)] = q_sum
        bias_grad[:, pl.ds(pl.multiple_of(there + 2 * columns, DH), DH)] = v_sum
    chips = pieces[0].shape[0]
    for j in range(chips):
        ins[j].wait()
        ins[chips + j].wait()
        cols = slice(2 * j * size, 2 * (j + 1) * size)
        total = nt(q_low[...], in_weight[0, cols, :])
        total = total + nt(k_low[...], in_weight[1, cols, :])
        total = total + nt(v_low[...], in_weight[2, cols, :])
        put_chunks(total, cols, own, mate, sends)


def first_back_body(count, own, x, vec, hidden_grad, *refs):
    received, (result, sums) = refs[:count], refs[count:]
    total = summed(own, received)
    normed, inverse = center_of(x[...].astype(F32))
    grad = hidden_grad[...] + norm_back(total, normed, inverse, vec[0:1, :])
    result[...] = grad.astype(BF16)
    for i, values in enumerate((total * normed, total)):
        sums[i : i + 1, :] = jnp.sum(values, axis=0, keepdims=True)


def output_body(count, own, hidden, vec, *refs):
    received, (result,) = refs[:count], refs[count:]
    total = summed(own, received)
    result[...] = (hidden[...] + total + vec[5:6, :]).astype(BF16)


def assemble_body(dp, tensor, table, *refs):
    chunks, (result,) = refs[:tensor], refs[tensor:]
    rows = chunks[0].shape[0]
    for k, chunk in enumerate(chunks):
        result[place(table, dp + k, rows), :] = chunk[...]


def grad_blocks(table, left, right, by_rows, first, chips, size, put):
    if by_rows:
        width = right[0].shape[1]
        tile = min(TILE, width)
        for block in range(chips):
            turned = left[:, place(table, first + block, size)].T
            for j, ref in enumerate(right):
                for c in range(0, width, tile):
                    put(block, 0, j * width + c, nn(turned, ref[:, c : c + tile]))
    else:
        hidden = left.shape[1]
        step = min(512, hidden)
        for r in range(0, hidden, step):
            turned = left[:, r : r + step].T
            for block in range(chips):
                put(block, r, 0, nn(turned, right[0][:, place(table, first + block, size)]))


def grad_body(by_rows, first, chips, size, count, table, left, *refs):
    right, theirs, out = refs[:count], refs[count:-1], refs[-1]

    def put(block, low, column, value):
        rows, cols = slice(low, low + value.shape[0]), slice(column, column + value.shape[1])
        for ref in theirs:
            value = value + ref[block, rows, cols].astype(F32)
        out[block, rows, cols] = value.astype(BF16)

    grad_blocks(table, left, right, by_rows, first, chips, size, put)


def finish_body(by_rows, planes, first, cols, blocks, out):
    chips, rows, _ = blocks.shape
    here = slice(first, first + cols)
    for half in range(2):
        total = blocks[half, :, here].astype(F32)
        for j in range(half + 2, chips, 2):
            total = total + blocks[j, :, here].astype(F32)
        if not by_rows:
            out[half * rows : (half + 1) * rows, :] = total
        elif planes == 1:
            out[:, half * cols : (half + 1) * cols] = total
        else:
            width = cols // planes
            for j in range(planes):
                out[j, :, half * width : (half + 1) * width] = total[:, j * width : (j + 1) * width]


def sems(*dims):
    return pltpu.SemaphoreType.DMA(tuple(dims))


class Layer:
    def __init__(self, at, length, features):
        self.at, self.table = at, at.table()
        self.length, self.features = length, features
        self.own = length // at.tensor
        self.side_at = at.dp + at.tensor

    def chunk_outs(self):
        sends = [shape((self.own, self.features), BF16)] * (2 * self.at.tensor - 2)
        return [shape((self.own, self.features), F32)] * 2 + sends

    def collect(self, name, own, vec, chunks, norm):
        at = self.at
        return call(
            functools.partial(collect_body, at.dp, at.tensor, norm),
            name,
            [SMEM] + [VMEM] * (2 + at.tensor),
            [shape((2 * self.length, self.features), BF16)],
            [],
            20 * self.length * self.features,
            [self.table, own, vec] + chunks,
        )[0]

    def project(self, name, left, blocks, by_rows):
        inner = left.shape[1]
        weight = (self.features, inner) if by_rows else (inner, self.features)
        return call(
            functools.partial(project_body, by_rows),
            name,
            [SMEM, VMEM] + [ANY] * 2,
            self.chunk_outs(),
            [pltpu.VMEM(weight, BF16), sems(self.at.dp)],
            4 * self.length * inner * self.features,
            [self.table, left] + blocks,
        )

    def fold(self, name, mate, received):
        return call(
            fold_body,
            name,
            [VMEM] * (1 + len(received)),
            [shape(mate.shape, BF16)],
            [],
            mate.size * 4,
            [mate] + received,
        )[0]

    def trade_mate(self, part):
        return self.at.to_peers(part[1 + self.at.tensor :])

    def trade_own(self, part):
        return self.at.to_peers(part[2 : 1 + self.at.tensor])

    def reduce(self, name, part):
        for_mate, own = self.trade_mate(part), self.trade_own(part)
        folded = self.fold(name + "_fold", part[1], for_mate)
        return own + [self.at.to_mate(folded)], folded

    def block_shape(self, left, right, by_rows):
        size = self.features // self.at.dp
        if by_rows:
            return size, (size, sum(r.shape[1] for r in right))
        return size, (left.shape[1], size)

    def grad(self, name, left, right, by_rows, *theirs):
        chips = self.at.chips
        size, block = self.block_shape(left, right, by_rows)
        return call(
            functools.partial(grad_body, by_rows, 0 if theirs else chips, chips, size, len(right)),
            name + ("_near" if theirs else "_far"),
            [SMEM] + [VMEM] * (1 + len(right) + len(theirs)),
            [shape((chips,) + block, BF16)],
            [],
            4 * self.length * chips * block[0] * block[1],
            [self.table, left] + list(right) + list(theirs),
        )[0]

    def grad_far(self, name, left, right, by_rows):
        return self.grad(name, left, right, by_rows)

    def grad_near(self, name, left, right, by_rows, theirs):
        return self.grad(name, left, right, by_rows, theirs)

    def grad_attention(self, first_low, mixed, lows, hidden_low, *theirs):
        chips, size = self.at.chips, self.features // self.at.dp
        width, heads = len(lows) * lows[0].shape[1], mixed.shape[1]
        first = 0 if theirs else chips

        def body(table, left, other, *refs):
            right, low, got, out = refs[:3], refs[3], refs[4:-1], refs[-1]

            def put_at(start):
                def put(block, row, column, value):
                    rows = slice(row, row + value.shape[0])
                    cols = slice(start + column, start + column + value.shape[1])
                    for ref in got:
                        value = value + ref[block, rows, cols].astype(F32)
                    out[block, rows, cols] = value.astype(BF16)

                return put

            grad_blocks(table, left, right, True, first, chips, size, put_at(0))
            grad_blocks(table, other, [low], False, first, chips, size, put_at(width))

        args = [self.table, first_low, mixed] + list(lows) + [hidden_low] + list(theirs)
        return call(
            body,
            "grad_attention_near" if theirs else "grad_attention_far",
            [SMEM] + [VMEM] * (len(args) - 1),
            [shape((chips, heads, width + size), BF16)],
            [],
            4 * self.length * chips * size * (width + heads),
            args,
        )[0]

    def grad_finish(self, name, blocks, by_rows):
        _, rows, cols = blocks.shape
        return call(
            functools.partial(finish_body, by_rows, 1, 0, cols),
            name + "_finish",
            [VMEM],
            [shape((rows, 2 * cols) if by_rows else (2 * rows, cols), F32)],
            [],
            blocks.size,
            [blocks],
        )[0]

    def attention_finish(self, blocks, width, planes):
        _, rows, cols = blocks.shape

        def body(ref, grad_in, grad_out):
            finish_body(True, planes, 0, width, ref, grad_in)
            finish_body(False, 1, width, cols - width, ref, grad_out)

        return call(
            body,
            "attention_finish",
            [VMEM],
            [shape((planes, rows, 2 * width // planes), F32), shape((2 * rows, cols - width), F32)],
            [],
            blocks.size,
            [blocks],
        )


def shards(
    dp,
    tensor,
    inputs,
    segment_ids,
    first_gain,
    first_shift,
    project_in,
    query_bias,
    value_bias,
    project_out,
    out_bias,
    second_gain,
    second_shift,
    up_weight,
    up_bias,
    down_weight,
    down_bias,
    cotangent,
):
    at = Places(dp, tensor)
    length, features = inputs.shape
    layer = Layer(at, length, features)
    own, table, side_at = layer.own, layer.table, layer.side_at
    heads, hidden_units = query_bias.shape[0] // 2, up_bias.shape[0] // 2
    both = 2 * length
    chunk_count = 2 * tensor
    chunk32, chunk16 = shape((own, features), F32), shape((own, features), BF16)
    tokens16 = shape((both, features), BF16)

    x_own, g_own = at.chunk_of(inputs), at.chunk_of(cotangent)
    mate = at.to_mate(jnp.concatenate([x_own, g_own]))
    ids = at.tokens_in(segment_ids)
    mate_ids = at.to_mate(ids)
    blocks = [at.halves(project_in, 2), at.halves(project_out, 0)[:, None]]
    mine_in = at.exchange(after(jnp.concatenate(blocks, 1), mate, mate_ids))
    mate_chunks = [mate] + at.to_peers(mate)
    up_blocks, down_blocks = at.halves(up_weight, 1), at.halves(down_weight, 0)
    mate_chunks = after(mate_chunks, up_blocks, down_blocks)
    vec = jnp.stack(
        [
            first_gain,
            first_shift,
            out_bias,
            second_gain,
            second_shift,
            down_bias,
            down_bias,
            down_bias,
        ]
    ).astype(F32)
    biases = [at.half_of(b)[None] for b in (query_bias, value_bias, up_bias)]
    order = at.tokens_in(jnp.arange(length, dtype=jnp.int32))
    ids = jnp.stack([ids, mate_ids])
    allowed = (
        (ids[:, :, None] == ids[:, None, :])
        & (ids[:, :, None] != 0)
        & (order[None, None, :] <= order[None, :, None])
    )
    allowed = (allowed | (order[None, None, :] == order[None, :, None])).astype(F32)
    first_low = layer.collect("first_norm", inputs, vec, mate_chunks, True)
    g = layer.collect("upstream", cotangent, vec, mate_chunks, False)
    mine_in = after(mine_in, first_low, allowed, biases, g)
    mine_up = at.exchange(after(up_blocks, mine_in))

    all_in = at.both_cores(mine_in)
    low_heads = shape((both, heads), BF16)
    query, key, value, probs, mixed = call(
        attend_body,
        "attend",
        [SMEM] + [VMEM] * 4 + [ANY] * 2,
        [low_heads] * 3 + [shape((2 * heads // DH, length, length), F32), low_heads],
        [pltpu.VMEM((3, features, heads), BF16), sems(3, dp)],
        12 * length * heads * features,
        [table, first_low, biases[0], biases[1], allowed] + all_in,
    )
    part = layer.project("project_out", mixed, all_in, False)
    received, _ = layer.reduce("project_out", part)
    hidden, normed_two, inverse_two, second_own = call(
        functools.partial(second_body, len(received)),
        "second_norm",
        [VMEM] * (3 + len(received)),
        [chunk32, chunk32, shape((own, 128), F32), chunk16],
        [],
        20 * own * features,
        [part[0], x_own, vec] + received,
    )
    second_chunks = at.spread(second_own)
    mine_up = after(mine_up, second_chunks[tensor])
    mine_down = at.exchange(after(down_blocks, mine_up))
    all_up = at.both_cores(mine_up)
    second_low, activated, slope = call(
        functools.partial(upper_body, chunk_count),
        "upper",
        [SMEM] + [VMEM] * (1 + chunk_count) + [ANY] * 2,
        [tokens16, shape((both, hidden_units), BF16), shape((both, hidden_units), F32)],
        [pltpu.VMEM((features, hidden_units), BF16), sems(dp)],
        4 * length * features * hidden_units,
        [table, biases[2]] + second_chunks + all_up,
    )
    far_down = layer.grad_far("grad_down", activated, [g], False)
    near_down = layer.grad_near("grad_down", activated, [g], False, at.to_core(far_down))
    mine_down = after(mine_down, near_down)
    ring_down = at.exchange(after(near_down, mine_down))
    all_down = at.both_cores(mine_down)
    upper_low, up_bias_grad = call(
        functools.partial(upper_grad_body, side_at),
        "upper_grad",
        [SMEM] + [VMEM] * 2 + [ANY] * 2,
        [shape((both, hidden_units), BF16), shape((1, 2 * hidden_units), F32)],
        [pltpu.VMEM((hidden_units, features), BF16), sems(dp)],
        4 * length * features * hidden_units,
        [table, g, slope] + all_down,
    )
    far_up = layer.grad_far("grad_up", second_low, [upper_low], True)
    part = layer.project("second_part", after(upper_low, far_up), all_up, True)
    received, folded = layer.reduce("second_part", part)
    near_up = layer.grad_near(
        "grad_up", second_low, after([upper_low], folded, received[:-1]), True, at.to_core(far_up)
    )
    hidden_grad, hidden_low_own, sums_two = call(
        functools.partial(second_back_body, len(received)),
        "second_back",
        [VMEM] * (5 + len(received)),
        [chunk32, chunk16, shape((8, features), F32)],
        [],
        20 * own * features,
        [after(part[0], ring_down, near_up), g_own, vec, normed_two, inverse_two] + received,
    )
    hidden_chunks = at.spread(hidden_low_own)
    feed = layer.project("feed", after(activated, hidden_low_own), all_down, False)
    ring_up = at.exchange(after(near_up, hidden_chunks[tensor], feed[0]))
    back = call(
        functools.partial(attend_back_body, side_at, chunk_count),
        "attend_back",
        [SMEM] + [VMEM] * (4 + chunk_count) + [ANY] * 2,
        [tokens16, low_heads, low_heads, low_heads, shape((1, 4 * heads), F32)]
        + layer.chunk_outs(),
        [
            pltpu.VMEM((heads, features), BF16),
            pltpu.VMEM((3, features, heads), BF16),
            pltpu.VMEM((both, heads), BF16),
            sems(dp),
            sems(dp),
        ],
        16 * length * heads * features,
        [table, after(query, feed), key, value, probs]
        + hidden_chunks
        + all_in,
    )
    hidden_low, q_low, k_low, v_low, heads_grad, *part = back
    lows = [q_low, k_low, v_low]
    for_mate = layer.trade_mate(part)
    far = layer.grad_attention(first_low, mixed, lows, hidden_low)
    feed_for_mate = layer.trade_mate(after(feed, far))
    folded = layer.fold("first_part_fold", part[1], for_mate)
    from_mate = at.to_mate(folded)
    near = layer.grad_attention(first_low, mixed, after(lows, folded), hidden_low, at.to_core(far))
    received = layer.trade_own(after(part, feed_for_mate[0])) + [from_mate]
    feed_folded = layer.fold("feed_fold", after(feed[1], near), feed_for_mate)
    feed_from_mate = at.to_mate(feed_folded)
    ring_in = at.exchange(after(near, ring_up, received, feed_from_mate))
    grad_down = layer.grad_finish("grad_down", ring_down, False)
    grad_up = layer.grad_finish("grad_up", ring_up, True)
    input_own, sums_one = call(
        functools.partial(first_back_body, len(received)),
        "first_back",
        [VMEM] * (4 + len(received)),
        [chunk16, shape((8, features), F32)],
        [],
        20 * own * features,
        [part[0], x_own, vec, hidden_grad] + received,
    )
    def assemble(name, chunk, others):
        return call(
            functools.partial(assemble_body, dp, tensor),
            name,
            [SMEM] + [VMEM] * tensor,
            [shape((length, features), BF16)],
            [],
            length * features,
            [table, chunk] + others,
        )[0]

    input_others = at.to_peers(input_own)
    input_gradient = assemble("input_gradient", input_own, input_others)
    feed_received = layer.trade_own(after(feed, received[0])) + [feed_from_mate]
    outputs_own = call(
        functools.partial(output_body, len(feed_received)),
        "outputs_own",
        [VMEM] * (3 + len(feed_received)),
        [chunk16],
        [],
        4 * own * features,
        [after(feed[0], input_others), hidden, vec] + feed_received,
    )[0]
    output_others = at.to_peers(outputs_own)
    outputs = assemble("outputs", outputs_own, output_others)
    grad_in, grad_out = layer.attention_finish(ring_in, 3 * heads, 3)

    narrow = jnp.concatenate([heads_grad[0], up_bias_grad[0]])
    rows = -(-narrow.shape[0] // features)
    narrow = jnp.pad(narrow, (0, rows * features - narrow.shape[0])).reshape(rows, features)
    sums = at.sum_small(after(jnp.concatenate([sums_one[:2], sums_two[:4]]), outputs_own, grad_down, grad_up), narrow)
    narrow = sums[6:].reshape(-1)
    heads, hidden_units = 2 * heads, 2 * hidden_units
    return (
        outputs,
        input_gradient,
        sums[0],
        sums[1],
        grad_in,
        narrow[:heads],
        narrow[heads : 2 * heads],
        grad_out,
        sums[2],
        sums[3],
        sums[4],
        grad_up,
        narrow[2 * heads : 2 * heads + hidden_units],
        grad_down,
        sums[5],
    )


def solution(mesh):
    dp, tensor = mesh.shape["dp"], mesh.shape["tensor"]

    def program(*arguments):
        return shards(dp, tensor, *arguments)

    in_specs = (
        P("dp", None),
        P("dp"),
        P(),
        P(),
        P(None, "dp", "tensor"),
        P("tensor"),
        P("tensor"),
        P("tensor", "dp"),
        P(),
        P(),
        P(),
        P("dp", "tensor"),
        P("tensor"),
        P("tensor", "dp"),
        P(),
        P("dp", None),
    )
    out_specs = (
        P("dp", None),
        P("dp", None),
        P(),
        P(),
        P(None, "dp", "tensor"),
        P("tensor"),
        P("tensor"),
        P("tensor", "dp"),
        P(),
        P(),
        P(),
        P("dp", "tensor"),
        P("tensor"),
        P("tensor", "dp"),
        P(),
    )
    return jax.shard_map(program, mesh=mesh, in_specs=in_specs, out_specs=out_specs, check_vma=False)
```
